128 devices in a mesh: region: 128 (over x, y, z, core).
Axes of the slice: x: 4, y: 4, z: 4, core: 2. Of those that a mesh axis runs over, the one named last changes fastest.
Arguments:
- sample_points: float32 [32768, 3, 128], P('region'), may hold values from -6 to 6
- sample_spacing: float32 [32768, 128], P('region'), may hold values from 0.004 to 0.04
- crossed: int32 [32768, 4], P('region'), may hold values from 0 to 127, all different within a row; in each aligned block of 256 rows (0 to 255, 256 to 511, ...) at most 20 rows name the same one
- colour_grad: float32 [3, 32768], P(None, 'region'), may hold values from -24 to 24
- freq: bfloat16 [128, 3, 64], P('region'), may hold values from -18 to 18
- w_hidden: bfloat16 [128, 128, 256], P('region'), may hold values from -0.5 to 0.5
- w_head: bfloat16 [128, 4, 256], P('region'), may hold values from -0.375 to 0.375
Outputs:
- rendered: float32 [3, 32768], P(None, 'region')
- head_grad: float32 [128, 4, 256], P('region')
The draws below stay inside these ranges and needn't reach their ends.
Inputs may be any that keep to these rules, and one draw needn't show every extreme that they name: `crossed`: row r lists 4 distinct regions, in the order ray r meets them. In each aligned block of 256 rays (the rays of one device) no region is listed by more than 20 rays; in some block some region is listed by exactly 20 rays. Every region is listed by some ray.
All inputs are finite; a program needn't handle non-finite values.
Results may differ from the reference program's by a relative error of at most 0.0019.
Values may be sent and summed in bfloat16 or wider, within the bound.
A program may use at most 192 MiB of HBM per device.

```python
import math
import jax
import jax.numpy as jnp
import numpy as np
from jax import lax

RAYS_DEV = 256
K = 4
S = 32
FREQ = 64
HID = 256
FEAT = 128
REGIONS = 128
RAYS = 32768
CAP = 20


def level_of(own_key, extent, pieces, low, high):
    loudness = 1.0
    for axis_at, shards_of in pieces:
        steps = jax.random.uniform(jax.random.fold_in(jax.random.fold_in(own_key, 6), axis_at), (shards_of,), jnp.float32, low / len(pieces), high / len(pieces))
        loudness = loudness * jnp.repeat(jnp.exp(steps), extent[axis_at] // shards_of).reshape((-1,) + (1,) * (len(extent) - 1 - axis_at))
    return loudness


def shared_out(key, own, number, rows, count, top, reach, lean):
    order = jax.random.permutation(key, count)
    crowded, common = portions_of(count, rows * top, reach, lean, True), portions_of(count, rows * top, reach, lean, False)
    places = jnp.arange(count)

    def named(sizes, rotation):
        used = int((sizes > 0).sum())
        fixed = max(1, used // 4)
        passed = fixed + (places - fixed + rotation * (used - fixed)) % max(1, count - fixed)
        return jnp.zeros((count,), jnp.int32).at[order[jnp.where(places < fixed, places, passed)]].set(jnp.asarray(sizes, jnp.int32))

    sizes = jnp.where(number % 4 == 0, named(crowded, number // 4), named(common, number - number // 4 - 1))
    mixed = jax.random.permutation(jax.random.fold_in(own, 3), count)
    source_of, receiver = mixed[0:count // 2 * 2:2], mixed[1:count // 2 * 2:2]
    room = jnp.minimum(sizes[source_of] - 1, reach - sizes[receiver]) // 2
    room = jnp.where((source_of == order[0]) | (receiver == order[0]) | (sizes[receiver] == 0), 0, jnp.maximum(room, 0))
    passed = jax.random.randint(jax.random.fold_in(own, 4), (count // 2,), 0, 1 << 20) % (room + 1)
    sizes = sizes.at[source_of].add(-passed).at[receiver].add(passed)
    items = jnp.searchsorted(jnp.cumsum(sizes), jnp.arange(rows * top), side="right").astype(jnp.int32)
    grid = items.reshape(top, rows).T
    grid = grid[jax.random.permutation(jax.random.fold_in(own, 1), rows)]
    rotation = jax.random.randint(jax.random.fold_in(own, 2), (rows, 1), 0, top)
    return jnp.take_along_axis(grid, (jnp.arange(top)[None, :] + rotation) % top, axis=1)


def portions_of(count, total, reach, slope, full):
    loads = [(1 << 20) // math.isqrt(standing ** slope) + 1 for standing in range(1, count + 1)]
    largest = reach if full else min(reach, max(-(-total // count), total * loads[0] // sum(loads)))
    least = 1 if total - largest >= count - 1 else 0
    counts, spare = [largest] + [least] * (count - 1), total - largest - least * (count - 1)
    while spare > 0:
        free = [i for i in range(1, count) if counts[i] < largest] or [i for i in range(1, count) if counts[i] < reach]
        whole, left = sum([loads[i] for i in free]), spare
        for i in free:
            more = min(reach - counts[i], max(1, left * loads[i] // whole), spare)
            counts[i] = counts[i] + more
            spare = spare - more
    return np.array(counts)


def scatter_about(stream_key, dims, width, bound, cuts=(), held_as=jnp.bfloat16):
    array = jax.random.normal(stream_key, dims, jnp.float32) * width
    if len(cuts) > 0:
        array = level_of(stream_key, dims, cuts, -0.22, 0.18) * array
    return jnp.clip(array, min=-bound, max=bound).astype(held_as)


def setup_inputs(seed: int = 0) -> dict:
    streams_of = jax.random.split(jax.random.key(seed), 8)
    sample_points = scatter_about(streams_of[0], (RAYS, 3, K * S), 1.0, 6.0, ((0, 128),), jnp.float32)
    sample_spacing = jnp.clip(jnp.exp(math.log(0.04) - 2.30258502 * jax.random.uniform(streams_of[1], (RAYS, K * S), jnp.float32) ** level_of(streams_of[1], (RAYS, K * S), ((0, 128),), -0.2, 0.2)), 0.004, 0.04)
    crossed_keys = jax.random.split(jax.random.fold_in(streams_of[2], 1), RAYS // RAYS_DEV)
    crossed_turns = jax.random.permutation(jax.random.fold_in(streams_of[2], 3), RAYS // RAYS_DEV)
    crossed = jax.vmap(lambda own, number: shared_out(jax.random.fold_in(streams_of[2], 2), own, number, RAYS_DEV, REGIONS, K, CAP, 1))(crossed_keys, crossed_turns).reshape((RAYS, K))
    colour_grad = scatter_about(streams_of[3], (3, RAYS), 4.0, 24.0, ((1, 128),), jnp.float32)
    freq = scatter_about(streams_of[4], (REGIONS, 3, FREQ), 3.0, 18.0, ((0, 128),))
    w_hidden = scatter_about(streams_of[5], (REGIONS, FEAT, HID), FEAT ** -0.5, 0.5, ((0, 128),))
    w_head = scatter_about(streams_of[6], (REGIONS, 4, HID), HID ** -0.5, 0.375, ((0, 128),))
    return {"sample_points": sample_points, "sample_spacing": sample_spacing, "crossed": crossed, "colour_grad": colour_grad, "freq": freq, "w_hidden": w_hidden, "w_head": w_head}


def features(points, freq, w_hidden):
    coords = points.reshape(points.shape[0], 3, -1).astype(jnp.float32)
    freq32 = freq.astype(jnp.float32)
    phases = coords[:, 0, :, None] * freq32[:, 0][:, None, :]
    phases = phases + coords[:, 1, :, None] * freq32[:, 1][:, None, :]
    phases = phases + coords[:, 2, :, None] * freq32[:, 2][:, None, :]
    feature = jnp.concatenate([jnp.sin(phases), jnp.cos(phases)], axis=-1).astype(jnp.bfloat16)
    feature = lax.optimization_barrier(feature)
    hidden = jnp.einsum('bsf,bfh->bsh', feature.astype(jnp.float32), w_hidden.astype(jnp.float32), precision=lax.Precision.HIGHEST)
    hidden = jnp.maximum(hidden, 0.0).astype(jnp.bfloat16)
    return lax.optimization_barrier(hidden)

def outputs(hidden, w_head):
    return jnp.einsum('bsh,boh->obs', hidden.astype(jnp.float32), w_head.astype(jnp.float32), precision=lax.Precision.HIGHEST)

def render(raw_out, spacing):
    density = jax.nn.softplus(raw_out[0])
    colour = jax.nn.sigmoid(raw_out[1:])
    optical = density * spacing
    running = jnp.cumsum(optical, axis=-1)
    transmit = jnp.exp(optical - running)
    weight = transmit * (1.0 - jnp.exp(-optical))
    seg_colour = lax.optimization_barrier(jnp.sum(weight[None] * colour, axis=-1))
    seg_trans = jnp.exp(-running[:, -1])
    return jnp.concatenate([seg_colour, seg_trans[None]], axis=0).T

def composite(partials, colour_grad):
    upstream = colour_grad.T
    crossings = partials.shape[1]
    before = jnp.ones(partials.shape[:1], partials.dtype)
    befores = []
    rendered = jnp.zeros_like(upstream)
    for k in range(crossings):
        befores.append(before)
        rendered = rendered + before[:, None] * partials[:, k, :3]
        before = before * partials[:, k, 3]
    behind = jnp.zeros_like(upstream)
    seg_grads = [None] * crossings
    for k in range(crossings - 1, -1, -1):
        grad_colour = befores[k][:, None] * upstream
        grad_trans = befores[k] * lax.optimization_barrier(jnp.sum(upstream * behind, axis=-1))
        seg_grads[k] = jnp.concatenate([grad_colour, grad_trans[:, None]], axis=-1)
        behind = partials[:, k, :3] + partials[:, k, 3][:, None] * behind
    return (rendered.T, jnp.stack(seg_grads, axis=1))

def reference(sample_points, sample_spacing, crossed, colour_grad, freq, w_hidden, w_head):
    seg_total = RAYS * K
    row_block = min(256, seg_total)
    blocks = seg_total // row_block
    points_seg = sample_points.reshape(RAYS, 3, K, S).transpose(0, 2, 1, 3)
    points_in = points_seg.reshape(blocks, row_block, 3 * S)
    spacing_in = sample_spacing.reshape(blocks, row_block, S)
    region_in = crossed.reshape(blocks, row_block).astype(jnp.int32)

    def forward(item_data):
        points, spacing, owner = item_data
        hidden = features(points, freq[owner], w_hidden[owner])
        return render(outputs(hidden, w_head[owner]), spacing)
    partials = lax.map(forward, (points_in, spacing_in, region_in)).reshape(RAYS, K, 4)
    rendered, seg_grads = composite(partials, colour_grad)
    grads_in = seg_grads.reshape(blocks, row_block, 4)

    def backward(accum, item_data):
        points, spacing, owner, upstream = item_data
        hidden = features(points, freq[owner], w_hidden[owner])
        raw_out = outputs(hidden, w_head[owner])
        unused, pullback = jax.vjp(lambda value: render(value, spacing), raw_out)
        raw_grad = pullback(upstream)[0].astype(jnp.bfloat16)
        raw_grad = lax.optimization_barrier(raw_grad)
        contrib = jnp.einsum('obs,bsh->boh', raw_grad.astype(jnp.float32), hidden.astype(jnp.float32), precision=lax.Precision.HIGHEST)
        return (accum.at[owner].add(contrib), None)
    start = jnp.zeros((REGIONS, 4, HID), jnp.float32)
    head_grad, unused = lax.scan(backward, start, (points_in, spacing_in, region_in, grads_in))
    return (rendered, head_grad)
```

```python
import functools

import jax
import jax.numpy as jnp
import numpy as np
from jax import lax
from jax.experimental import pallas as pl
from jax.experimental.pallas import tpu as pltpu
from jax.sharding import PartitionSpec as P

RAYS = 256
K = 4
S = 32
REG = 128
SEG = RAYS * K
NB = 352
FREQ = 64
HID = 256
LANES = 128

F32 = jnp.float32
BF16 = jnp.bfloat16

SIN_C = (4.44288292, -7.3082457, 3.60635441, -0.84611289, 0.10982699)
COS_C = (1.4142135, -6.97885099, 5.73946117, -1.88356298, 0.31069819)

VM = pl.BlockSpec(memory_space=pltpu.VMEM)
SM = pl.BlockSpec(memory_space=pltpu.SMEM)
ANY = pl.BlockSpec(memory_space=pl.ANY)


def iota(shape, dim):
    return lax.broadcasted_iota(jnp.int32, shape, dim)


def dot(a, b, dims=((1,), (0,))):
    return lax.dot_general(a, b, (dims, ((), ())), preferred_element_type=F32)


def pieces(x):
    hi = x.astype(BF16)
    rest = x - hi.astype(F32)
    mid = rest.astype(BF16)
    low = (rest - mid.astype(F32)).astype(BF16)
    return hi, mid, low


def exact_dot(x, pattern):
    hi, mid, low = pieces(x)
    return dot(hi, pattern) + dot(mid, pattern) + dot(low, pattern)


def poly(z, coef):
    out = coef[-1] * z + coef[-2]
    for value in coef[-3::-1]:
        out = out * z + value
    return out


def sort_kernel(crossed_ref, points_ref, spacing_ref, picks_ref, coords_ref, table_ref):
    owner = crossed_ref[...]
    onehot = (iota((REG, SEG), 0) == owner).astype(F32)
    onehot16 = onehot.astype(BF16)
    earlier = (iota((SEG, SEG), 0) < iota((SEG, SEG), 1)).astype(F32).astype(BF16)
    rank = dot(onehot16, earlier)
    counts = jnp.sum(onehot, axis=1, keepdims=True)
    blocks = jnp.floor((counts + 3.0) * 0.25)
    lower = (iota((REG, REG), 1) <= iota((REG, REG), 0)).astype(F32).astype(BF16)
    ends = dot(lower, jnp.broadcast_to(blocks, (REG, LANES)).astype(BF16))[:, :1]
    starts = ends - blocks
    rank_row = jnp.sum(onehot * rank, axis=0, keepdims=True)
    start_row = jnp.sum(onehot * starts, axis=0, keepdims=True)
    step = jnp.floor(rank_row * 0.25)
    place = (rank_row - 4.0 * step) * NB + start_row + step
    place = place.astype(jnp.int32)
    block_at = iota((REG, 384), 1).astype(F32)
    owner_of = jnp.sum((block_at >= ends).astype(F32), axis=0, keepdims=True)
    owner_of = jnp.minimum(owner_of, REG - 1.0)
    total = jnp.sum(blocks, axis=0, keepdims=True)
    table = jnp.where(iota((1, 384), 1) == 383, total, owner_of)
    table_ref[...] = table.astype(jnp.int32)

    lane_group = iota((RAYS, LANES), 1) // S
    sources = [points_ref[:, 0, :], points_ref[:, 1, :], points_ref[:, 2, :], spacing_ref[...]]
    rows = []
    for k in range(K):
        row = jnp.zeros((RAYS, LANES), F32)
        for c in range(4):
            moved = sources[c]
            if c != k:
                moved = pltpu.roll(moved, ((c - k) % 4) * S, 1)
            row = jnp.where(lane_group == c, moved, row)
        rows.append(row)
    packed = jnp.concatenate(rows, axis=0)
    hi, mid, low = pieces(packed)
    source = jnp.concatenate([hi, mid, low], axis=1)
    block_group = iota((NB, LANES), 1) // S
    coords = [jnp.zeros((NB, LANES), F32) for _ in range(4)]
    for q in range(4):
        picks = (iota((NB, SEG), 0) + q * NB == place).astype(F32).astype(BF16)
        picks_ref[q] = picks
        three = dot(picks, source)
        got = three[:, :128] + three[:, 128:256] + three[:, 256:]
        for c in range(4):
            moved = got
            if c != q:
                moved = pltpu.roll(got, ((q - c) % 4) * S, 1)
            coords[c] = jnp.where(block_group == q, moved, coords[c])
    for c in range(4):
        value = coords[c] * np.float32(0.5 / np.pi) if c < 3 else coords[c]
        coords_ref[pl.ds(c, NB, stride=8), :] = value
    for c in range(4, 8):
        coords_ref[pl.ds(c, NB, stride=8), :] = jnp.zeros((NB, LANES), F32)


def feature_kernel(table_ref, coords_ref, freq_ref, feature_ref):
    def body(b, carry):
        region = table_ref[b]
        f8 = freq_ref[region]
        f24 = jnp.concatenate([f8, f8, f8], axis=0).astype(BF16)
        x = coords_ref[pl.ds(b * 8, 8), :]
        hi = x.astype(BF16).astype(F32)
        mid = (x - hi).astype(BF16).astype(F32)
        low = x - hi - mid
        x24 = jnp.concatenate([hi, mid, low], axis=0).astype(BF16)
        turns = dot(f24, x24, ((0,), (0,)))[:FREQ]
        r = turns - jnp.round(turns)
        z = r * r
        s = r * poly(z, SIN_C)
        c = poly(z, COS_C)
        feature = jnp.concatenate([s * c, 1.0 - s * s], axis=0)
        feature_ref[b] = feature.astype(BF16)
        return carry

    lax.fori_loop(0, NB, body, 0, unroll=2)


def tri(kind):
    row, col = iota((LANES, LANES), 0), iota((LANES, LANES), 1)
    same = row // S == col // S
    if kind == "upto":
        keep = row <= col
    elif kind == "after":
        keep = row > col
    else:
        keep = row >= 0
    return (same & keep).astype(F32).astype(BF16)


def render_kernel(
    table_ref, coords_ref, picks_ref, colour_grad_ref, feature_ref, hidden_w_ref, head_ref,
    rendered_ref, grad_ref, hidden_ref, raw_ref,
):
    total = table_ref[383]

    def forward(b, carry):
        region = table_ref[b]
        hid = jnp.maximum(dot(hidden_w_ref[region], feature_ref[b]), 0.0).astype(BF16)
        hidden_ref[b] = hid
        raw_ref[pl.ds(b * 8, 8), :] = dot(head_ref[region], hid)
        return carry

    def blank(b, carry):
        raw_ref[pl.ds(b * 8, 8), :] = jnp.zeros((8, LANES), F32)
        return carry

    lax.fori_loop(0, total, forward, 0)
    lax.fori_loop(total, NB, blank, 0)

    raw = [raw_ref[pl.ds(o, NB, stride=8), :] for o in range(4)]
    spacing = coords_ref[pl.ds(3, NB, stride=8), :]
    soft = jnp.maximum(raw[0], 0.0) + jnp.log1p(jnp.exp(-jnp.abs(raw[0])))
    colour = [1.0 / (1.0 + jnp.exp(-raw[c])) for c in (1, 2, 3)]
    gate = 1.0 / (1.0 + jnp.exp(-raw[0]))
    optical = soft * spacing
    running = exact_dot(optical, tri("upto"))
    after = jnp.exp(-running)
    weight = jnp.exp(optical - running) * (1.0 - jnp.exp(-optical))
    chooser = (iota((8, LANES), 1) // S == iota((8, LANES), 0)).astype(F32).astype(BF16)
    last = (iota((8, LANES), 1) == iota((8, LANES), 0) * S + (S - 1)).astype(F32).astype(BF16)

    def seg_rows(value, pattern):
        return [dot(pattern, part, ((1,), (1,))) for part in pieces(value)]

    sums = []
    for c in range(3):
        three = seg_rows(weight * colour[c], chooser)
        sums.append(three[0] + three[1] + three[2])
    three = seg_rows(after, last)
    sums.append(three[0] + three[1] + three[2])
    by_seg = jnp.zeros((16, SEG), F32)
    for q in range(4):
        four = jnp.concatenate([value[q:q + 1] for value in sums], axis=0)
        hi, mid, low = pieces(four)
        rows = jnp.concatenate(
            [hi.astype(F32), mid.astype(F32), low.astype(F32), jnp.zeros((4, NB), F32)], axis=0
        )
        by_seg = by_seg + dot(rows.astype(BF16), picks_ref[q])
    partial = by_seg[0:4] + by_seg[4:8] + by_seg[8:12]
    seg_colour = [partial[0:3, k * RAYS:(k + 1) * RAYS] for k in range(K)]
    seg_trans = [partial[3:4, k * RAYS:(k + 1) * RAYS] for k in range(K)]
    upstream = colour_grad_ref[...]
    before = jnp.ones((1, RAYS), F32)
    befores = []
    rendered = jnp.zeros((3, RAYS), F32)
    for k in range(K):
        befores.append(before)
        rendered = rendered + before * seg_colour[k]
        before = before * seg_trans[k]
    rendered_ref[...] = rendered
    behind = jnp.zeros((3, RAYS), F32)
    grads = [None] * K
    for k in range(K - 1, -1, -1):
        trans = befores[k] * jnp.sum(upstream * behind, axis=0, keepdims=True)
        grads[k] = jnp.concatenate([befores[k] * upstream, trans], axis=0)
        behind = seg_colour[k] + seg_trans[k] * behind
    grad_rows = jnp.concatenate(grads, axis=1)
    hi, mid, low = pieces(grad_rows)
    grad_rows = jnp.concatenate(
        [hi.astype(F32), mid.astype(F32), low.astype(F32), jnp.zeros((4, SEG), F32)], axis=0
    ).astype(BF16)
    spread = [jnp.zeros((NB, LANES), F32) for _ in range(4)]
    for q in range(4):
        got = dot(picks_ref[q], grad_rows, ((1,), (1,))).astype(BF16)
        lane = iota((16, LANES), 1) // S == q
        for o in range(4):
            row = iota((16, LANES), 0)
            expand = (lane & (row % 4 == o) & (row < 12)).astype(F32).astype(BF16)
            spread[o] = spread[o] + dot(got, expand)
    shade = spread[0] * colour[0] + spread[1] * colour[1] + spread[2] * colour[2]
    later = exact_dot(shade * weight, tri("after")) + spread[3] * exact_dot_last(after)
    d_optical = shade * after - later
    raw_grads = [d_optical * spacing * gate]
    for c in range(3):
        raw_grads.append(spread[c] * weight * colour[c] * (1.0 - colour[c]))
    for o in range(4):
        raw_ref[pl.ds(o, NB, stride=8), :] = raw_grads[o]
    for o in range(4, 8):
        raw_ref[pl.ds(o, NB, stride=8), :] = jnp.zeros((NB, LANES), F32)
    grad_ref[...] = jnp.zeros_like(grad_ref)

    def backward(b, carry):
        region = table_ref[b]
        rg = raw_ref[pl.ds(b * 8, 8), :].astype(BF16)
        grad_ref[region] += dot(rg, hidden_ref[b], ((1,), (1,)))
        return carry

    lax.fori_loop(0, total, backward, 0)


def exact_dot_last(after):
    row, col = iota((LANES, LANES), 0), iota((LANES, LANES), 1)
    pattern = ((row // S == col // S) & (row % S == S - 1)).astype(F32).astype(BF16)
    return exact_dot(after, pattern)


def params(mib, **kw):
    return pltpu.CompilerParams(vmem_limit_bytes=mib * 1024 * 1024, **kw)


def sort_segments(sample_points, sample_spacing, crossed):
    crossed_row = crossed.T.reshape(1, SEG)
    return pl.pallas_call(
        sort_kernel,
        out_shape=(
            jax.ShapeDtypeStruct((4, NB, SEG), BF16),
            jax.ShapeDtypeStruct((NB * 8, LANES), F32),
            jax.ShapeDtypeStruct((1, 384), jnp.int32),
        ),
        in_specs=[VM, VM, VM],
        out_specs=(VM, VM, VM),
        compiler_params=params(32),
    )(crossed_row, sample_points, sample_spacing)


def make_features(table, coords, freq_all):
    return pl.pallas_call(
        feature_kernel,
        out_shape=jax.ShapeDtypeStruct((NB, LANES, LANES), BF16),
        in_specs=[SM, VM, VM],
        out_specs=VM,
        compiler_params=params(40),
    )(table, coords, freq_all)


def render_all(table, coords, picks, colour_grad, feature, hidden_all, head_all):
    return pl.pallas_call(
        render_kernel,
        out_shape=(
            jax.ShapeDtypeStruct((3, RAYS), F32),
            jax.ShapeDtypeStruct((REG, 8, HID), F32),
        ),
        in_specs=[SM, VM, VM, VM, VM, VM, VM],
        out_specs=(VM, VM),
        scratch_shapes=[
            pltpu.VMEM((NB, HID, LANES), BF16),
            pltpu.VMEM((NB * 8, LANES), F32),
        ],
        compiler_params=params(60),
    )(table, coords, picks, colour_grad, feature, hidden_all, head_all)


def local_part(sample_points, sample_spacing, crossed, colour_grad, freq_all, hidden_all, head_all):
    picks, coords, table = sort_segments(sample_points, sample_spacing, crossed)
    table = table.reshape(384)
    feature = make_features(table, coords, freq_all)
    return render_all(table, coords, picks, colour_grad, feature, hidden_all, head_all)


def on_device(sample_points, sample_spacing, crossed, colour_grad, freq, w_hidden, w_head):
    freq8 = jnp.pad(freq[0].astype(F32), ((0, 5), (0, LANES - FREQ)))
    head8 = jnp.pad(w_head[0], ((0, 4), (0, 0)))
    freq_all = lax.all_gather(freq8, "region")
    hidden_all = lax.all_gather(w_hidden[0].T, "region")
    head_all = lax.all_gather(head8, "region")
    rendered, grad = local_part(
        sample_points, sample_spacing, crossed, colour_grad, freq_all, hidden_all, head_all
    )
    parts = lax.all_to_all(grad[:, :4], "region", split_axis=0, concat_axis=0, tiled=True)
    return rendered, jnp.sum(parts, axis=0, keepdims=True)


def solution(mesh):
    return jax.shard_map(
        on_device,
        mesh=mesh,
        in_specs=(
            P("region", None, None),
            P("region", None),
            P("region", None),
            P(None, "region"),
            P("region", None, None),
            P("region", None, None),
            P("region", None, None),
        ),
        out_specs=(P(None, "region"), P("region", None, None)),
        check_vma=False,
    )
```

```python
import functools

import jax
import jax.numpy as jnp
import numpy as np
from jax import lax
from jax.experimental import pallas as pl
from jax.experimental.pallas import tpu as pltpu
from jax.sharding import PartitionSpec as P

RAYS = 256
K = 4
S = 32
REG = 128
SEG = RAYS * K
NB = 352
FREQ = 64
HID = 256
LANES = 128
COPIES = 152
GF = 32
CHUNKS = (1, 1, 2, 2, 2, 2, 1)
GR = 16

F32 = jnp.float32
BF16 = jnp.bfloat16

SIN_C = (4.44288292, -7.3082457, 3.60635441, -0.84611289, 0.10982699)
COS_C = (1.4142135, -6.97885099, 5.73946117, -1.88356298, 0.31069819)

VM = pl.BlockSpec(memory_space=pltpu.VMEM)
SM = pl.BlockSpec(memory_space=pltpu.SMEM)
ANY = pl.BlockSpec(memory_space=pl.ANY)


def iota(shape, dim):
    return lax.broadcasted_iota(jnp.int32, shape, dim)


def dot(a, b, dims=((1,), (0,))):
    return lax.dot_general(a, b, (dims, ((), ())), preferred_element_type=F32)


def pieces(x):
    hi = x.astype(BF16)
    rest = x - hi.astype(F32)
    mid = rest.astype(BF16)
    low = (rest - mid.astype(F32)).astype(BF16)
    return hi, mid, low


def exact_dot(x, pattern):
    hi, mid, low = pieces(x)
    return dot(hi, pattern) + dot(mid, pattern) + dot(low, pattern)


def poly(z, coef):
    out = coef[-1] * z + coef[-2]
    for value in coef[-3::-1]:
        out = out * z + value
    return out


def sort_kernel(crossed_ref, points_ref, spacing_ref, picks_ref, coords_ref, table_ref):
    owner = crossed_ref[...]
    onehot = (iota((REG, SEG), 0) == owner).astype(F32)
    onehot16 = onehot.astype(BF16)
    earlier = (iota((SEG, SEG), 0) < iota((SEG, SEG), 1)).astype(F32).astype(BF16)
    rank = dot(onehot16, earlier)
    counts = jnp.sum(onehot, axis=1, keepdims=True)
    blocks = jnp.floor((counts + 3.0) * 0.25)
    lower = (iota((REG, REG), 1) <= iota((REG, REG), 0)).astype(F32).astype(BF16)
    ends = dot(lower, jnp.broadcast_to(blocks, (REG, LANES)).astype(BF16))[:, :1]
    starts = ends - blocks
    rank_row = jnp.sum(onehot * rank, axis=0, keepdims=True)
    start_row = jnp.sum(onehot * starts, axis=0, keepdims=True)
    step = jnp.floor(rank_row * 0.25)
    place = (rank_row - 4.0 * step) * NB + start_row + step
    place = place.astype(jnp.int32)
    block_at = iota((REG, 384), 1).astype(F32)
    owner_of = jnp.sum((block_at >= ends).astype(F32), axis=0, keepdims=True)
    owner_of = jnp.minimum(owner_of, REG - 1.0)
    total = jnp.sum(blocks, axis=0, keepdims=True)
    table = jnp.where(iota((1, 384), 1) == 383, total, owner_of)
    for part in range(3):
        bound = ends[(part + 1) * 32 - 1:(part + 1) * 32]
        table = jnp.where(iota((1, 384), 1) == 380 + part, bound, table)
    table_ref[...] = table.astype(jnp.int32)

    lane_group = iota((RAYS, LANES), 1) // S
    sources = [points_ref[:, 0, :], points_ref[:, 1, :], points_ref[:, 2, :], spacing_ref[...]]
    rows = []
    for k in range(K):
        row = jnp.zeros((RAYS, LANES), F32)
        for c in range(4):
            moved = sources[c]
            if c != k:
                moved = pltpu.roll(moved, ((c - k) % 4) * S, 1)
            row = jnp.where(lane_group == c, moved, row)
        rows.append(row)
    packed = jnp.concatenate(rows, axis=0)
    hi, mid, low = pieces(packed)
    source = jnp.concatenate([hi, mid, low], axis=1)
    block_group = iota((NB, LANES), 1) // S
    coords = [jnp.zeros((NB, LANES), F32) for _ in range(4)]
    for q in range(4):
        picks = (iota((NB, SEG), 0) + q * NB == place).astype(F32).astype(BF16)
        picks_ref[q] = picks
        three = dot(picks, source)
        got = three[:, :128] + three[:, 128:256] + three[:, 256:]
        for c in range(4):
            moved = got
            if c != q:
                moved = pltpu.roll(got, ((q - c) % 4) * S, 1)
            coords[c] = jnp.where(block_group == q, moved, coords[c])
    for c in range(4):
        value = coords[c] * np.float32(0.5 / np.pi) if c < 3 else coords[c]
        coords_ref[pl.ds(c, NB, stride=4), :] = value


def features_of(freq, coords):
    f12 = jnp.concatenate([freq, freq, freq], axis=0).astype(BF16)
    hi = coords.astype(BF16).astype(F32)
    mid = (coords - hi).astype(BF16).astype(F32)
    low = coords - hi - mid
    x12 = jnp.concatenate([hi, mid, low], axis=0).astype(BF16)
    return dot(f12, x12, ((0,), (0,)))[:FREQ]


def encode(turns):
    r = turns - jnp.round(turns)
    z = r * r
    s = r * poly(z, SIN_C)
    c = poly(z, COS_C)
    return jnp.concatenate([s * c, 1.0 - s * s], axis=0).astype(BF16)


ORDERS = ((0, 1, 2), (1, 2, 0), (2, 0, 1))
STRIDES = (32, 8, 2)
MESH_ID = pl.DeviceIdType.MESH


def gather_kernel(
    table_ref, coords_ref, freq_in_ref, hidden_in_ref, head_in_ref, nets_ref, feature_out_ref,
    payload_ref, freq_ref, feature_ref,
    send_sem, recv_sem, freq_send, freq_recv, local_sem, feature_sem,
):
    me = lax.axis_index("region")
    core = lax.rem(me, 2)
    sibling = me + 1 - 2 * core
    pos = [lax.rem(lax.div(me, stride), 4) for stride in STRIDES]
    barrier = pltpu.get_barrier_semaphore()

    def greet(step, carry):
        peer = lax.rem(me + step, REG)
        pl.semaphore_signal(barrier, inc=1, device_id=(peer,), device_id_type=MESH_ID)
        return carry

    lax.fori_loop(1, REG, greet, 0)
    payload_ref[0:HID, :] = hidden_in_ref[...].astype(F32).T.astype(BF16)
    payload_ref[HID:HID + 32, :] = head_in_ref[...]
    freq_ref[me] = freq_in_ref[...]
    pl.semaphore_wait(barrier, REG - 1)

    def send_freq(step, carry):
        peer = lax.rem(me + step, REG)
        pltpu.make_async_remote_copy(
            freq_in_ref, freq_ref.at[me], freq_send, freq_recv,
            device_id=(peer,), device_id_type=MESH_ID,
        ).start()
        return carry

    lax.fori_loop(1, REG, send_freq, 0)

    counter = [0]
    sends = []

    def new_id():
        counter[0] += 1
        return counter[0] - 1

    def device(axis, delta):
        return me + (lax.rem(pos[axis] + delta, 4) - pos[axis]) * STRIDES[axis]

    def view(where, parity, rows):
        return nets_ref.at[where[0], where[1], where[2], parity, rows, :]

    def start(src, dst, peer, number):
        copy = pltpu.make_async_remote_copy(
            src, dst, send_sem.at[number], recv_sem.at[number],
            device_id=(peer,), device_id_type=MESH_ID,
        )
        copy.start()
        sends.append(copy)

    def arrive(dst, number):
        pltpu.make_async_remote_copy(
            dst, dst, send_sem.at[number], recv_sem.at[number],
            device_id=(sibling,), device_id_type=MESH_ID,
        ).wait_recv()

    home = {0: pos[0], 1: pos[1], 2: pos[2]}
    sibling_waits = []

    def to_sibling(where, rows):
        number = new_id()
        start(view(where, core, rows), view(where, core, rows), sibling, number)
        sibling_waits.append((view(where, 1 - core, rows), number))

    whole = pl.ds(0, 4)

    def make_stream(t):
        a, b, c = ORDERS[t]
        rows = pl.ds(96 * t, 96)
        near = pl.ds(96 * t, 48)
        far = pl.ds(96 * t + 48, 48)
        base = dict(home)
        left = {axis: lax.rem(pos[axis] + 3, 4) for axis in range(3)}
        right = {axis: lax.rem(pos[axis] + 1, 4) for axis in range(3)}
        opposite = {axis: lax.rem(pos[axis] + 2, 4) for axis in range(3)}

        def spec(**kw):
            out = dict(base)
            for key, value in kw.items():
                out[{"a": a, "b": b, "c": c}[key]] = value
            return out

        ids = {}

        def send(name, axis, delta, where, part=rows, src=None):
            number = new_id()
            source = view(where, core, part) if src is None else src
            start(source, view(where, core, part), device(axis, delta), number)
            ids[name] = number

        def wait(name, where, part=rows):
            arrive(view(where, core, part), ids[name])

        def stage0():
            mine = payload_ref.at[rows, :]
            send("A+", a, 1, spec(), src=mine)
            send("A-", a, 3, spec(), src=mine)
            send("B+o", b, 1, spec(), src=mine)
            send("B-o", b, 3, spec(), src=mine)
            send("C+o", c, 1, spec(), src=mine)
            send("C-o", c, 3, spec(), src=mine)

        def spread(where, tag):
            send("B+" + tag, b, 1, where)
            send("B-" + tag, b, 3, where)
            send("C+" + tag, c, 1, where)
            send("C-" + tag, c, 3, where)

        def stage1():
            low, high = spec(a=left[a]), spec(a=right[a])
            wait("A+", low)
            send("H+", a, 1, low, near)
            spread(low, "l")
            wait("A-", high)
            send("H-", a, 3, high, far)
            spread(high, "r")
            to_sibling(low, rows)
            to_sibling(high, rows)

        def stage2():
            across = spec(a=opposite[a])
            wait("H+", across, near)
            wait("H-", across, far)
            spread(across, "d")
            to_sibling(across, rows)

        def line_arrivals(prefix, **kw):
            wait(prefix + "o", spec(**kw))
            wait(prefix + "l", spec(a=left[a], **kw))
            wait(prefix + "r", spec(a=right[a], **kw))
            wait(prefix + "d", spec(a=opposite[a], **kw))

        def stage3():
            line_arrivals("B+", b=left[b])
            low = spec(a=whole, b=left[b])
            send("BH+", b, 1, spec(a=pl.ds(0, 2), b=left[b]))
            send("C+L", c, 1, low)
            send("C-L", c, 3, low)
            line_arrivals("B-", b=right[b])
            high = spec(a=whole, b=right[b])
            send("BH-", b, 3, spec(a=pl.ds(2, 2), b=right[b]))
            send("C+R", c, 1, high)
            send("C-R", c, 3, high)
            to_sibling(low, rows)
            to_sibling(high, rows)

        def stage4():
            wait("BH+", spec(a=pl.ds(0, 2), b=opposite[b]))
            wait("BH-", spec(a=pl.ds(2, 2), b=opposite[b]))
            across = spec(a=whole, b=opposite[b])
            send("C+D", c, 1, across)
            send("C-D", c, 3, across)
            to_sibling(across, rows)

        def stage5():
            line_arrivals("C+", c=left[c])
            send("CH+o", c, 1, spec(a=whole, c=left[c]))
            line_arrivals("C-", c=right[c])
            wait("C-R", spec(a=whole, b=right[b], c=right[c]))
            send("CH-R", c, 3, spec(a=whole, b=right[b], c=right[c]))
            wait("C+L", spec(a=whole, b=left[b], c=left[c]))
            send("CH+L", c, 1, spec(a=whole, b=left[b], c=left[c]))
            to_sibling(spec(a=whole, c=left[c]), rows)
            to_sibling(spec(a=whole, c=right[c]), rows)
            to_sibling(spec(a=whole, b=left[b], c=left[c]), rows)
            to_sibling(spec(a=whole, b=right[b], c=right[c]), rows)

        def stage6():
            wait("C-D", spec(a=whole, b=opposite[b], c=right[c]))
            send("CH-D", c, 3, spec(a=whole, b=opposite[b], c=right[c]))
            wait("C+R", spec(a=whole, b=right[b], c=left[c]))
            wait("C+D", spec(a=whole, b=opposite[b], c=left[c]))
            wait("C-L", spec(a=whole, b=left[b], c=right[c]))
            to_sibling(spec(a=whole, b=right[b], c=left[c]), rows)
            to_sibling(spec(a=whole, b=opposite[b], c=left[c]), rows)
            to_sibling(spec(a=whole, b=left[b], c=right[c]), rows)
            to_sibling(spec(a=whole, b=opposite[b], c=right[c]), rows)

        def stage7():
            for name, line in (("CH+o", pos[b]), ("CH+L", left[b]), ("CH-R", right[b]), ("CH-D", opposite[b])):
                where = spec(a=whole, b=line, c=opposite[c])
                wait(name, where)
                to_sibling(where, rows)

        return (stage0, stage1, stage2, stage3, stage4, stage5, stage6, stage7)

    streams = [make_stream(t) for t in range(3)]

    def stage(number):
        for stream in streams:
            stream[number]()

    stage(0)
    own = new_id()
    start(payload_ref, view(home, core, pl.ds(0, 288)), sibling, own)
    sibling_waits.append((view(home, 1 - core, pl.ds(0, 288)), own))
    keep = pltpu.make_async_copy(payload_ref, view(home, core, pl.ds(0, 288)), local_sem)
    keep.start()

    def features(first, count):
        def body(step, carry):
            turns = []
            for j in range(GF):
                b = step * GF + j
                turns.append(features_of(freq_ref[table_ref[b]], coords_ref[pl.ds(b * 4, 4), :]))
            for j in range(GF):
                feature_ref[step * GF + j] = encode(turns[j])
            return carry

        lax.fori_loop(first, first + count, body, 0)
        part = pl.ds(first * GF, count * GF)
        copy = pltpu.make_async_copy(
            feature_ref.at[part], feature_out_ref.at[part], feature_sem.at[first]
        )
        copy.start()
        feature_copies.append(copy)

    feature_copies = []
    arrived = freq_ref.at[pl.ds(0, REG - 1)]
    pltpu.make_async_copy(arrived, arrived, freq_recv).wait()
    done = 0
    for number in range(1, 8):
        count = CHUNKS[number - 1]
        if count:
            features(done, count)
        done += count
        stage(number)
    for ref, number in sibling_waits:
        arrive(ref, number)
    for copy in sends:
        copy.wait_send()
    pltpu.make_async_copy(arrived, arrived, freq_send).wait()
    keep.wait()
    for copy in feature_copies:
        copy.wait()


def tri(kind):
    row, col = iota((LANES, LANES), 0), iota((LANES, LANES), 1)
    same = row // S == col // S
    if kind == "upto":
        keep = row <= col
    elif kind == "after":
        keep = row > col
    else:
        keep = row >= 0
    return (same & keep).astype(F32).astype(BF16)


def render_kernel(
    table_ref, coords_ref, picks_ref, colour_grad_ref, feature_hbm_ref, nets_hbm_ref,
    rendered_ref, grad_ref, hidden_ref, raw_ref, feature_ref, nets_ref, feature_sem, nets_sem,
):
    total = table_ref[383]

    def net_copy(part):
        rows = pl.ds(part * 32, 32)
        return pltpu.make_async_copy(nets_hbm_ref.at[rows], nets_ref.at[rows], nets_sem.at[part])

    def feature_copy(step):
        rows = pl.ds(step * GR, GR)
        return pltpu.make_async_copy(feature_hbm_ref.at[rows], feature_ref.at[rows], feature_sem.at[step])

    for part in range(4):
        net_copy(part).start()
        for step in range(NB // GR):
            if step * 4 // (NB // GR) == part:
                feature_copy(step).start()

    groups = lax.div(total + (GR - 1), GR)

    def forward(step, carry):
        feature_copy(step).wait()
        hids = []
        for j in range(GR):
            b = step * GR + j
            hid = dot(nets_ref[table_ref[b], 0:HID, :], feature_ref[b])
            hid = jnp.maximum(hid, 0.0).astype(BF16)
            hidden_ref[b] = hid
            hids.append(hid)
        for j in range(GR):
            b = step * GR + j
            region = table_ref[b]
            head = jnp.concatenate(
                [nets_ref[region, HID:HID + 16, :], nets_ref[region, HID + 16:HID + 32, :]], axis=1
            )
            raw_ref[pl.ds(b * 8, 8), :] = dot(head, hids[j])[0:8]
        return carry

    def blank(step, carry):
        feature_copy(step).wait()
        for j in range(GR):
            raw_ref[pl.ds((step * GR + j) * 8, 8), :] = jnp.zeros((8, LANES), F32)
        return carry

    first = 0
    for part in range(4):
        net_copy(part).wait()
        last = groups if part == 3 else lax.div(table_ref[380 + part], GR)
        lax.fori_loop(first, last, forward, 0)
        first = last
    lax.fori_loop(groups, NB // GR, blank, 0)

    raw = [raw_ref[pl.ds(o, NB, stride=8), :] for o in range(4)]
    spacing = coords_ref[pl.ds(3, NB, stride=4), :]
    soft = jnp.maximum(raw[0], 0.0) + jnp.log1p(jnp.exp(-jnp.abs(raw[0])))
    colour = [1.0 / (1.0 + jnp.exp(-raw[c])) for c in (1, 2, 3)]
    gate = 1.0 / (1.0 + jnp.exp(-raw[0]))
    optical = soft * spacing
    running = exact_dot(optical, tri("upto"))
    after = jnp.exp(-running)
    weight = jnp.exp(optical - running) * (1.0 - jnp.exp(-optical))
    chooser = (iota((8, LANES), 1) // S == iota((8, LANES), 0)).astype(F32).astype(BF16)
    last = (iota((8, LANES), 1) == iota((8, LANES), 0) * S + (S - 1)).astype(F32).astype(BF16)

    def seg_rows(value, pattern):
        return [dot(pattern, part, ((1,), (1,))) for part in pieces(value)]

    sums = []
    for c in range(3):
        three = seg_rows(weight * colour[c], chooser)
        sums.append(three[0] + three[1] + three[2])
    three = seg_rows(after, last)
    sums.append(three[0] + three[1] + three[2])
    by_seg = jnp.zeros((16, SEG), F32)
    for q in range(4):
        four = jnp.concatenate([value[q:q + 1] for value in sums], axis=0)
        hi, mid, low = pieces(four)
        rows = jnp.concatenate(
            [hi.astype(F32), mid.astype(F32), low.astype(F32), jnp.zeros((4, NB), F32)], axis=0
        )
        by_seg = by_seg + dot(rows.astype(BF16), picks_ref[q])
    partial = by_seg[0:4] + by_seg[4:8] + by_seg[8:12]
    seg_colour = [partial[0:3, k * RAYS:(k + 1) * RAYS] for k in range(K)]
    seg_trans = [partial[3:4, k * RAYS:(k + 1) * RAYS] for k in range(K)]
    upstream = colour_grad_ref[...]
    before = jnp.ones((1, RAYS), F32)
    befores = []
    rendered = jnp.zeros((3, RAYS), F32)
    for k in range(K):
        befores.append(before)
        rendered = rendered + before * seg_colour[k]
        before = before * seg_trans[k]
    rendered_ref[...] = rendered
    behind = jnp.zeros((3, RAYS), F32)
    grads = [None] * K
    for k in range(K - 1, -1, -1):
        trans = befores[k] * jnp.sum(upstream * behind, axis=0, keepdims=True)
        grads[k] = jnp.concatenate([befores[k] * upstream, trans], axis=0)
        behind = seg_colour[k] + seg_trans[k] * behind
    grad_rows = jnp.concatenate(grads, axis=1)
    hi, mid, low = pieces(grad_rows)
    grad_rows = jnp.concatenate(
        [hi.astype(F32), mid.astype(F32), low.astype(F32), jnp.zeros((4, SEG), F32)], axis=0
    ).astype(BF16)
    spread = [jnp.zeros((NB, LANES), F32) for _ in range(4)]
    for q in range(4):
        got = dot(picks_ref[q], grad_rows, ((1,), (1,))).astype(BF16)
        lane = iota((16, LANES), 1) // S == q
        for o in range(4):
            row = iota((16, LANES), 0)
            expand = (lane & (row % 4 == o) & (row < 12)).astype(F32).astype(BF16)
            spread[o] = spread[o] + dot(got, expand)
    shade = spread[0] * colour[0] + spread[1] * colour[1] + spread[2] * colour[2]
    later = exact_dot(shade * weight, tri("after")) + spread[3] * exact_dot_last(after)
    d_optical = shade * after - later
    raw_grads = [d_optical * spacing * gate]
    for c in range(3):
        raw_grads.append(spread[c] * weight * colour[c] * (1.0 - colour[c]))
    for o in range(4):
        raw_ref[pl.ds(o, NB, stride=8), :] = raw_grads[o]
    for o in range(4, 8):
        raw_ref[pl.ds(o, NB, stride=8), :] = jnp.zeros((NB, LANES), F32)
    grad_ref[...] = jnp.zeros_like(grad_ref)

    def backward(step, carry):
        parts = []
        for j in range(GR):
            b = step * GR + j
            rg = raw_ref[pl.ds(b * 8, 8), :].astype(BF16)
            parts.append(dot(rg, hidden_ref[b], ((1,), (1,))))
        for j in range(GR):
            grad_ref[table_ref[step * GR + j]] += parts[j]
        return carry

    lax.fori_loop(0, groups, backward, 0)


def exact_dot_last(after):
    row, col = iota((LANES, LANES), 0), iota((LANES, LANES), 1)
    pattern = ((row // S == col // S) & (row % S == S - 1)).astype(F32).astype(BF16)
    return exact_dot(after, pattern)


def params(mib, **kw):
    return pltpu.CompilerParams(vmem_limit_bytes=mib * 1024 * 1024, **kw)


def sort_segments(sample_points, sample_spacing, crossed):
    crossed_row = crossed.T.reshape(1, SEG)
    return pl.pallas_call(
        sort_kernel,
        out_shape=(
            jax.ShapeDtypeStruct((4, NB, SEG), BF16),
            jax.ShapeDtypeStruct((NB * 4, LANES), F32),
            jax.ShapeDtypeStruct((1, 384), jnp.int32),
        ),
        in_specs=[VM, VM, VM],
        out_specs=(VM, VM, VM),
        compiler_params=params(32),
    )(crossed_row, sample_points, sample_spacing)


def gather_nets(table, coords, freq4, hidden, head32):
    return pl.pallas_call(
        gather_kernel,
        out_shape=(
            jax.ShapeDtypeStruct((4, 4, 4, 2, HID + 32, LANES), BF16),
            jax.ShapeDtypeStruct((NB, LANES, LANES), BF16),
        ),
        in_specs=[SM, VM, VM, VM, VM],
        out_specs=(ANY, ANY),
        scratch_shapes=[
            pltpu.VMEM((HID + 32, LANES), BF16),
            pltpu.VMEM((REG, 4, LANES), F32),
            pltpu.VMEM((NB, LANES, LANES), BF16),
            pltpu.SemaphoreType.DMA((COPIES,)),
            pltpu.SemaphoreType.DMA((COPIES,)),
            pltpu.SemaphoreType.DMA,
            pltpu.SemaphoreType.DMA,
            pltpu.SemaphoreType.DMA,
            pltpu.SemaphoreType.DMA((NB // GF,)),
        ],
        compiler_params=params(40, collective_id=0, has_side_effects=True),
    )(table, coords, freq4, hidden, head32)


def render_all(table, coords, picks, colour_grad, feature, nets):
    return pl.pallas_call(
        render_kernel,
        out_shape=(
            jax.ShapeDtypeStruct((3, RAYS), F32),
            jax.ShapeDtypeStruct((REG, 8, HID), F32),
        ),
        in_specs=[SM, VM, VM, VM, ANY, ANY],
        out_specs=(VM, VM),
        scratch_shapes=[
            pltpu.VMEM((NB, HID, LANES), BF16),
            pltpu.VMEM((NB * 8, LANES), F32),
            pltpu.VMEM((NB, LANES, LANES), BF16),
            pltpu.VMEM((REG, HID + 32, LANES), BF16),
            pltpu.SemaphoreType.DMA((NB // GR,)),
            pltpu.SemaphoreType.DMA((4,)),
        ],
        compiler_params=params(60),
    )(table, coords, picks, colour_grad, feature, nets)


def on_device(sample_points, sample_spacing, crossed, colour_grad, freq, w_hidden, w_head):
    freq4 = jnp.pad(freq[0].astype(F32), ((0, 1), (0, LANES - FREQ)))
    halves = w_head[0].reshape(4, 2, LANES).transpose(1, 0, 2)
    head32 = jnp.pad(halves, ((0, 0), (0, 12), (0, 0))).reshape(32, LANES)
    picks, coords, table = sort_segments(sample_points, sample_spacing, crossed)
    table = table.reshape(384)
    nets, feature = gather_nets(table, coords, freq4, w_hidden[0], head32)
    nets = nets.reshape(REG, HID + 32, LANES)
    rendered, grad = render_all(table, coords, picks, colour_grad, feature, nets)
    parts = lax.all_to_all(grad[:, :4], "region", split_axis=0, concat_axis=0, tiled=True)
    return rendered, jnp.sum(parts, axis=0, keepdims=True)


def solution(mesh):
    return jax.shard_map(
        on_device,
        mesh=mesh,
        in_specs=(
            P("region", None, None),
            P("region", None),
            P("region", None),
            P(None, "region"),
            P("region", None, None),
            P("region", None, None),
            P("region", None, None),
        ),
        out_specs=(P(None, "region"), P("region", None, None)),
        check_vma=False,
    )
```

```python
import functools

import jax
import jax.numpy as jnp
import numpy as np
from jax import lax
from jax.experimental import pallas as pl
from jax.experimental.pallas import tpu as pltpu
from jax.sharding import PartitionSpec as P

RAYS = 256
K = 4
S = 32
REG = 128
SEG = RAYS * K
NB = 352
FREQ = 64
HID = 256
LANES = 128
COPIES = 152
GF = 32
CHUNKS = (4, 3, 2, 1, 1)
GR = 16

F32 = jnp.float32
BF16 = jnp.bfloat16
FREQ_TYPE = BF16

SIN_C = (4.44288292, -7.3082457, 3.60635441, -0.84611289, 0.10982699)
COS_C = (1.4142135, -6.97885099, 5.73946117, -1.88356298, 0.31069819)

HBM = pl.BlockSpec(memory_space=pltpu.HBM)
VM = pl.BlockSpec(memory_space=pltpu.VMEM)
SM = pl.BlockSpec(memory_space=pltpu.SMEM)
ANY = pl.BlockSpec(memory_space=pl.ANY)


def iota(shape, dim):
    return lax.broadcasted_iota(jnp.int32, shape, dim)


def dot(a, b, dims=((1,), (0,))):
    return lax.dot_general(a, b, (dims, ((), ())), preferred_element_type=F32)


def pieces(x):
    hi = x.astype(BF16)
    rest = x - hi.astype(F32)
    mid = rest.astype(BF16)
    low = (rest - mid.astype(F32)).astype(BF16)
    return hi, mid, low


def exact_dot(x, pattern):
    hi, mid, low = pieces(x)
    return dot(hi, pattern) + dot(mid, pattern) + dot(low, pattern)


def poly(z, coef):
    out = coef[-1] * z + coef[-2]
    for value in coef[-3::-1]:
        out = out * z + value
    return out


def sort_places(crossed):
    owner = jnp.concatenate([crossed[k:k + 1] for k in range(K)], axis=1)
    onehot = (iota((REG, SEG), 0) == owner).astype(F32)
    onehot16 = onehot.astype(BF16)
    earlier = (iota((SEG, SEG), 0) < iota((SEG, SEG), 1)).astype(F32).astype(BF16)
    rank = dot(onehot16, earlier)
    counts = jnp.sum(onehot, axis=1, keepdims=True)
    blocks = jnp.floor((counts + 3.0) * 0.25)
    lower = (iota((REG, REG), 1) <= iota((REG, REG), 0)).astype(F32).astype(BF16)
    ends = dot(lower, jnp.broadcast_to(blocks, (REG, LANES)).astype(BF16))[:, :1]
    starts = ends - blocks
    rank_row = jnp.sum(onehot * rank, axis=0, keepdims=True)
    start_row = jnp.sum(onehot * starts, axis=0, keepdims=True)
    step = jnp.floor(rank_row * 0.25)
    place = (rank_row - 4.0 * step) * NB + start_row + step
    block_at = iota((REG, 384), 1).astype(F32)
    owner_of = jnp.sum((block_at >= ends).astype(F32), axis=0, keepdims=True)
    owner_of = jnp.minimum(owner_of, REG - 1.0)
    total = jnp.sum(blocks, axis=0, keepdims=True)
    table = jnp.where(iota((1, 384), 1) == 383, total, owner_of)
    for part in range(3):
        bound = ends[(part + 1) * 32 - 1:(part + 1) * 32]
        table = jnp.where(iota((1, 384), 1) == 380 + part, bound, table)
    return place.astype(jnp.int32), table.astype(jnp.int32)


def sort_sources(sources):
    lane_group = iota((RAYS, LANES), 1) // S
    rows = []
    for k in range(K):
        row = jnp.zeros((RAYS, LANES), F32)
        for c in range(4):
            moved = sources[c]
            if c != k:
                moved = pltpu.roll(moved, ((c - k) % 4) * S, 1)
            row = jnp.where(lane_group == c, moved, row)
        rows.append(row)
    packed = jnp.concatenate(rows, axis=0)
    return jnp.concatenate(pieces(packed), axis=1)


def sort_coords(picks_ref, source, coords_ref):
    block_group = iota((NB, LANES), 1) // S
    coords = [jnp.zeros((NB, LANES), F32) for _ in range(4)]
    for q in range(4):
        three = dot(picks_ref[q], source)
        got = three[:, :128] + three[:, 128:256] + three[:, 256:]
        for c in range(4):
            moved = got
            if c != q:
                moved = pltpu.roll(got, ((q - c) % 4) * S, 1)
            coords[c] = jnp.where(block_group == q, moved, coords[c])
    for c in range(4):
        value = coords[c] * np.float32(0.5 / np.pi) if c < 3 else coords[c]
        coords_ref[pl.ds(c, NB, stride=4), :] = value
    return coords[3]


def bounded(region):
    return jnp.maximum(jnp.minimum(region, REG - 1), 0)


def features_of(freq, coords):
    freq = freq.astype(F32)
    f12 = jnp.concatenate([freq, freq, freq], axis=0).astype(BF16)
    hi = coords.astype(BF16).astype(F32)
    mid = (coords - hi).astype(BF16).astype(F32)
    low = coords - hi - mid
    x12 = jnp.concatenate([hi, mid, low], axis=0).astype(BF16)
    return dot(f12, x12, ((0,), (0,)))[:FREQ]


def encode(turns):
    r = turns - jnp.round(turns)
    z = r * r
    s = r * poly(z, SIN_C)
    c = poly(z, COS_C)
    return jnp.concatenate([s * c, 1.0 - s * s], axis=0).astype(BF16)


ORDERS = ((0, 1, 2), (1, 2, 0), (2, 0, 1))
STRIDES = (32, 8, 2)
MESH_ID = pl.DeviceIdType.MESH


def greet(barrier, me):
    base, inner, outer = me - lax.rem(me, 8), lax.rem(me, 8), lax.div(me, 8)

    def within(step, carry):
        peer = base + lax.rem(inner + step, 8)
        pl.semaphore_signal(barrier, inc=1, device_id=(peer,), device_id_type=MESH_ID)
        return carry

    def across(step, carry):
        peer = lax.rem(outer + step, 16) * 8 + inner
        pl.semaphore_signal(barrier, inc=1, device_id=(peer,), device_id_type=MESH_ID)
        return carry

    lax.fori_loop(1, 8, within, 0)
    lax.fori_loop(1, 16, across, 0)


def gather_kernel(
    crossed_hbm, points_hbm, spacing_hbm, freq_hbm, hidden_hbm, head_hbm,
    nets_ref, feature_out_ref, picks_out_ref, spacing_out_ref, table_out_ref,
    payload_ref, freq_ref, feature_ref, picks_ref, coords_ref, table_ref,
    crossed_ref, points_ref, spacing_ref, freq_in_ref, hidden_in_ref, head_in_ref,
    send_sem, recv_sem, freq_send, freq_recv, local_sem, feature_sem, input_sem,
):
    me = lax.axis_index("region")
    core = lax.rem(me, 2)
    sibling = me + 1 - 2 * core
    pos = [lax.rem(lax.div(me, stride), 4) for stride in STRIDES]
    base, inner, outer = me - lax.rem(me, 8), lax.rem(me, 8), lax.div(me, 8)
    barrier = pltpu.get_barrier_semaphore()
    inputs = [
        pltpu.make_async_copy(src, dst, input_sem.at[number])
        for number, (src, dst) in enumerate((
            (hidden_hbm, hidden_in_ref), (freq_hbm, freq_in_ref), (head_hbm, head_in_ref),
            (crossed_hbm, crossed_ref), (points_hbm, points_ref), (spacing_hbm, spacing_ref),
        ))
    ]
    for copy in inputs:
        copy.start()
    greet(barrier, me)
    for copy in inputs[:3]:
        copy.wait()
    payload_ref[0:HID, :] = hidden_in_ref[...].astype(F32).T.astype(BF16)
    head = head_in_ref[...].astype(F32)
    blank = jnp.zeros((12, LANES), F32)
    head = jnp.concatenate([head[:, :LANES], blank, head[:, LANES:], blank], axis=0)
    payload_ref[HID:HID + 32, :] = head.astype(BF16)
    freq_in = jnp.concatenate([freq_in_ref[...].astype(F32), jnp.zeros((3, FREQ), F32)], axis=1)
    freq_in = jnp.concatenate([freq_in, jnp.zeros((1, LANES), F32)], axis=0)
    freq_ref[me] = freq_in.astype(FREQ_TYPE)
    pl.semaphore_wait(barrier, 22)

    def freq_within(step, carry):
        peer = base + lax.rem(inner + step, 8)
        pltpu.make_async_remote_copy(
            freq_ref.at[me], freq_ref.at[me], freq_send.at[0], freq_recv.at[0],
            device_id=(peer,), device_id_type=MESH_ID,
        ).start()
        return carry

    def freq_across(step, carry):
        peer = lax.rem(outer + step, 16) * 8 + inner
        rows = pl.ds(base, 8)
        pltpu.make_async_remote_copy(
            freq_ref.at[rows], freq_ref.at[rows], freq_send.at[1], freq_recv.at[1],
            device_id=(peer,), device_id_type=MESH_ID,
        ).start()
        return carry

    lax.fori_loop(1, 8, freq_within, 0)

    counter = [0]
    sends = []

    def new_id():
        counter[0] += 1
        return counter[0] - 1

    def device(axis, delta):
        return me + (lax.rem(pos[axis] + delta, 4) - pos[axis]) * STRIDES[axis]

    def view(where, parity, rows):
        return nets_ref.at[where[0], where[1], where[2], parity, rows, :]

    def start(src, dst, peer, number):
        copy = pltpu.make_async_remote_copy(
            src, dst, send_sem.at[number], recv_sem.at[number],
            device_id=(peer,), device_id_type=MESH_ID,
        )
        copy.start()
        sends.append(copy)

    def arrive(dst, number):
        pltpu.make_async_remote_copy(
            dst, dst, send_sem.at[number], recv_sem.at[number],
            device_id=(sibling,), device_id_type=MESH_ID,
        ).wait_recv()

    home = {0: pos[0], 1: pos[1], 2: pos[2]}
    sibling_waits = []

    def to_sibling(where, rows):
        number = new_id()
        start(view(where, core, rows), view(where, core, rows), sibling, number)
        sibling_waits.append((view(where, 1 - core, rows), number))

    whole = pl.ds(0, 4)

    def make_stream(t):
        a, b, c = ORDERS[t]
        rows = pl.ds(96 * t, 96)
        near = pl.ds(96 * t, 48)
        far = pl.ds(96 * t + 48, 48)
        base = dict(home)
        left = {axis: lax.rem(pos[axis] + 3, 4) for axis in range(3)}
        right = {axis: lax.rem(pos[axis] + 1, 4) for axis in range(3)}
        opposite = {axis: lax.rem(pos[axis] + 2, 4) for axis in range(3)}

        def spec(**kw):
            out = dict(base)
            for key, value in kw.items():
                out[{"a": a, "b": b, "c": c}[key]] = value
            return out

        ids = {}

        def send(name, axis, delta, where, part=rows, src=None):
            number = new_id()
            source = view(where, core, part) if src is None else src
            start(source, view(where, core, part), device(axis, delta), number)
            ids[name] = number

        def wait(name, where, part=rows):
            arrive(view(where, core, part), ids[name])

        def stage0():
            mine = payload_ref.at[rows, :]
            send("A+", a, 1, spec(), src=mine)
            send("A-", a, 3, spec(), src=mine)
            send("B+o", b, 1, spec(), src=mine)
            send("B-o", b, 3, spec(), src=mine)
            send("C+o", c, 1, spec(), src=mine)
            send("C-o", c, 3, spec(), src=mine)

        def spread(where, tag):
            send("B+" + tag, b, 1, where)
            send("B-" + tag, b, 3, where)
            send("C+" + tag, c, 1, where)
            send("C-" + tag, c, 3, where)

        def stage1():
            low, high = spec(a=left[a]), spec(a=right[a])
            wait("A+", low)
            send("H+", a, 1, low, near)
            spread(low, "l")
            wait("A-", high)
            send("H-", a, 3, high, far)
            spread(high, "r")
            to_sibling(low, rows)
            to_sibling(high, rows)

        def stage2():
            across = spec(a=opposite[a])
            wait("H+", across, near)
            wait("H-", across, far)
            spread(across, "d")
            to_sibling(across, rows)

        def line_arrivals(prefix, **kw):
            wait(prefix + "o", spec(**kw))
            wait(prefix + "l", spec(a=left[a], **kw))
            wait(prefix + "r", spec(a=right[a], **kw))
            wait(prefix + "d", spec(a=opposite[a], **kw))

        def stage3():
            line_arrivals("B+", b=left[b])
            low = spec(a=whole, b=left[b])
            send("BH+", b, 1, spec(a=pl.ds(0, 2), b=left[b]))
            send("C+L", c, 1, low)
            send("C-L", c, 3, low)
            line_arrivals("B-", b=right[b])
            high = spec(a=whole, b=right[b])
            send("BH-", b, 3, spec(a=pl.ds(2, 2), b=right[b]))
            send("C+R", c, 1, high)
            send("C-R", c, 3, high)
            to_sibling(low, rows)
            to_sibling(high, rows)

        def stage4():
            wait("BH+", spec(a=pl.ds(0, 2), b=opposite[b]))
            wait("BH-", spec(a=pl.ds(2, 2), b=opposite[b]))
            across = spec(a=whole, b=opposite[b])
            send("C+D", c, 1, across)
            send("C-D", c, 3, across)
            to_sibling(across, rows)

        def stage5():
            line_arrivals("C+", c=left[c])
            send("CH+o", c, 1, spec(a=whole, c=left[c]))
            line_arrivals("C-", c=right[c])
            wait("C-R", spec(a=whole, b=right[b], c=right[c]))
            send("CH-R", c, 3, spec(a=whole, b=right[b], c=right[c]))
            wait("C+L", spec(a=whole, b=left[b], c=left[c]))
            send("CH+L", c, 1, spec(a=whole, b=left[b], c=left[c]))
            to_sibling(spec(a=whole, c=left[c]), rows)
            to_sibling(spec(a=whole, c=right[c]), rows)
            to_sibling(spec(a=whole, b=left[b], c=left[c]), rows)
            to_sibling(spec(a=whole, b=right[b], c=right[c]), rows)

        def stage6():
            wait("C-D", spec(a=whole, b=opposite[b], c=right[c]))
            send("CH-D", c, 3, spec(a=whole, b=opposite[b], c=right[c]))
            wait("C+R", spec(a=whole, b=right[b], c=left[c]))
            wait("C+D", spec(a=whole, b=opposite[b], c=left[c]))
            wait("C-L", spec(a=whole, b=left[b], c=right[c]))
            to_sibling(spec(a=whole, b=right[b], c=left[c]), rows)
            to_sibling(spec(a=whole, b=opposite[b], c=left[c]), rows)
            to_sibling(spec(a=whole, b=left[b], c=right[c]), rows)
            to_sibling(spec(a=whole, b=opposite[b], c=right[c]), rows)

        def stage7():
            for name, line in (("CH+o", pos[b]), ("CH+L", left[b]), ("CH-R", right[b]), ("CH-D", opposite[b])):
                where = spec(a=whole, b=line, c=opposite[c])
                wait(name, where)
                to_sibling(where, rows)

        return (stage0, stage1, stage2, stage3, stage4, stage5, stage6, stage7)

    streams = [make_stream(t) for t in range(3)]

    def stage(number):
        for stream in streams:
            stream[number]()

    stage(0)
    own = new_id()
    start(payload_ref, view(home, core, pl.ds(0, 288)), sibling, own)
    sibling_waits.append((view(home, 1 - core, pl.ds(0, 288)), own))
    keep = pltpu.make_async_copy(payload_ref, view(home, core, pl.ds(0, 288)), local_sem)
    keep.start()

    def features(first, count):
        def body(step, carry):
            turns = []
            for j in range(GF):
                b = step * GF + j
                turns.append(features_of(freq_ref[bounded(table_ref[0, b])], coords_ref[pl.ds(b * 4, 4), :]))
            for j in range(GF):
                feature_ref[step * GF + j] = encode(turns[j])
            return carry

        lax.fori_loop(first, first + count, body, 0)
        part = pl.ds(first * GF, count * GF)
        copy = pltpu.make_async_copy(
            feature_ref.at[part], feature_out_ref.at[part], feature_sem.at[first]
        )
        copy.start()
        feature_copies.append(copy)

    feature_copies = []
    inputs[3].wait()
    place, table = sort_places(crossed_ref[...])
    table_out_ref[...] = table
    table_copy = pltpu.make_async_copy(table_out_ref, table_ref, input_sem.at[6])
    table_copy.start()
    seven, many = freq_ref.at[pl.ds(0, 7)], freq_ref.at[pl.ds(0, 120)]
    pltpu.make_async_copy(seven, seven, freq_recv.at[0]).wait()
    lax.fori_loop(1, 16, freq_across, 0)
    stage(1)
    for q in range(4):
        picks_ref[q] = (iota((NB, SEG), 0) + q * NB == place).astype(F32).astype(BF16)
    picks_copy = pltpu.make_async_copy(picks_ref, picks_out_ref, input_sem.at[7])
    picks_copy.start()
    inputs[4].wait()
    inputs[5].wait()
    source = sort_sources([points_ref[0], points_ref[1], points_ref[2], spacing_ref[...]])
    stage(2)
    spacing_out_ref[...] = sort_coords(picks_ref, source, coords_ref)
    table_copy.wait()
    pltpu.make_async_copy(many, many, freq_recv.at[1]).wait()
    done = 0
    for number in range(3, 8):
        count = CHUNKS[number - 3]
        features(done, count)
        done += count
        stage(number)
    for ref, number in sibling_waits:
        arrive(ref, number)
    for copy in sends:
        copy.wait_send()
    pltpu.make_async_copy(seven, seven, freq_send.at[0]).wait()
    pltpu.make_async_copy(many, many, freq_send.at[1]).wait()
    keep.wait()
    picks_copy.wait()
    for copy in feature_copies:
        copy.wait()


def tri(kind):
    row, col = iota((LANES, LANES), 0), iota((LANES, LANES), 1)
    same = row // S == col // S
    if kind == "upto":
        keep = row <= col
    elif kind == "after":
        keep = row > col
    else:
        keep = row >= 0
    return (same & keep).astype(F32).astype(BF16)


def render_kernel(
    table_ref, spacing_ref, colour_grad_ref, picks_hbm_ref, feature_hbm_ref, nets_hbm_ref,
    rendered_ref, grad_ref, hidden_ref, raw_ref, feature_ref, nets_ref, picks_ref,
    feature_sem, nets_sem, picks_sem,
):
    total = table_ref[0, 383]

    def net_copy(part):
        rows = pl.ds(part * 32, 32)
        return pltpu.make_async_copy(nets_hbm_ref.at[rows], nets_ref.at[rows], nets_sem.at[part])

    def feature_copy(step):
        rows = pl.ds(step * GR, GR)
        return pltpu.make_async_copy(feature_hbm_ref.at[rows], feature_ref.at[rows], feature_sem.at[step])

    for part in range(4):
        net_copy(part).start()
        for step in range(NB // GR):
            if step * 4 // (NB // GR) == part:
                feature_copy(step).start()

    picks_copy = pltpu.make_async_copy(picks_hbm_ref, picks_ref, picks_sem)
    picks_copy.start()
    groups = lax.div(total + (GR - 1), GR)

    def forward(step, carry):
        feature_copy(step).wait()
        hids = []
        for j in range(GR):
            b = step * GR + j
            hid = dot(nets_ref[table_ref[0, b], 0:HID, :], feature_ref[b])
            hid = jnp.maximum(hid, 0.0).astype(BF16)
            hidden_ref[b] = hid
            hids.append(hid)
        for j in range(GR):
            b = step * GR + j
            region = table_ref[0, b]
            head = jnp.concatenate(
                [nets_ref[region, HID:HID + 16, :], nets_ref[region, HID + 16:HID + 32, :]], axis=1
            )
            raw_ref[pl.ds(b * 8, 8), :] = dot(head, hids[j])[0:8]
        return carry

    def blank(step, carry):
        feature_copy(step).wait()
        for j in range(GR):
            raw_ref[pl.ds((step * GR + j) * 8, 8), :] = jnp.zeros((8, LANES), F32)
        return carry

    first = 0
    for part in range(4):
        net_copy(part).wait()
        last = groups if part == 3 else lax.div(table_ref[0, 380 + part], GR)
        lax.fori_loop(first, last, forward, 0)
        first = last
    lax.fori_loop(groups, NB // GR, blank, 0)

    raw = [raw_ref[pl.ds(o, NB, stride=8), :] for o in range(4)]
    spacing = spacing_ref[...]
    picks_copy.wait()
    soft = jnp.maximum(raw[0], 0.0) + jnp.log1p(jnp.exp(-jnp.abs(raw[0])))
    colour = [1.0 / (1.0 + jnp.exp(-raw[c])) for c in (1, 2, 3)]
    gate = 1.0 / (1.0 + jnp.exp(-raw[0]))
    optical = soft * spacing
    running = exact_dot(optical, tri("upto"))
    after = jnp.exp(-running)
    weight = jnp.exp(optical - running) * (1.0 - jnp.exp(-optical))
    chooser = (iota((8, LANES), 1) // S == iota((8, LANES), 0)).astype(F32).astype(BF16)
    last = (iota((8, LANES), 1) == iota((8, LANES), 0) * S + (S - 1)).astype(F32).astype(BF16)

    def seg_rows(value, pattern):
        return [dot(pattern, part, ((1,), (1,))) for part in pieces(value)]

    sums = []
    for c in range(3):
        three = seg_rows(weight * colour[c], chooser)
        sums.append(three[0] + three[1] + three[2])
    three = seg_rows(after, last)
    sums.append(three[0] + three[1] + three[2])
    by_seg = jnp.zeros((16, SEG), F32)
    for q in range(4):
        four = jnp.concatenate([value[q:q + 1] for value in sums], axis=0)
        hi, mid, low = pieces(four)
        rows = jnp.concatenate(
            [hi.astype(F32), mid.astype(F32), low.astype(F32), jnp.zeros((4, NB), F32)], axis=0
        )
        by_seg = by_seg + dot(rows.astype(BF16), picks_ref[q])
    partial = by_seg[0:4] + by_seg[4:8] + by_seg[8:12]
    seg_colour = [partial[0:3, k * RAYS:(k + 1) * RAYS] for k in range(K)]
    seg_trans = [partial[3:4, k * RAYS:(k + 1) * RAYS] for k in range(K)]
    upstream = colour_grad_ref[...]
    before = jnp.ones((1, RAYS), F32)
    befores = []
    rendered = jnp.zeros((3, RAYS), F32)
    for k in range(K):
        befores.append(before)
        rendered = rendered + before * seg_colour[k]
        before = before * seg_trans[k]
    rendered_ref[...] = rendered
    behind = jnp.zeros((3, RAYS), F32)
    grads = [None] * K
    for k in range(K - 1, -1, -1):
        trans = befores[k] * jnp.sum(upstream * behind, axis=0, keepdims=True)
        grads[k] = jnp.concatenate([befores[k] * upstream, trans], axis=0)
        behind = seg_colour[k] + seg_trans[k] * behind
    grad_rows = jnp.concatenate(grads, axis=1)
    hi, mid, low = pieces(grad_rows)
    grad_rows = jnp.concatenate(
        [hi.astype(F32), mid.astype(F32), low.astype(F32), jnp.zeros((4, SEG), F32)], axis=0
    ).astype(BF16)
    spread = [jnp.zeros((NB, LANES), F32) for _ in range(4)]
    for q in range(4):
        got = dot(picks_ref[q], grad_rows, ((1,), (1,))).astype(BF16)
        lane = iota((16, LANES), 1) // S == q
        for o in range(4):
            row = iota((16, LANES), 0)
            expand = (lane & (row % 4 == o) & (row < 12)).astype(F32).astype(BF16)
            spread[o] = spread[o] + dot(got, expand)
    shade = spread[0] * colour[0] + spread[1] * colour[1] + spread[2] * colour[2]
    later = exact_dot(shade * weight, tri("after")) + spread[3] * exact_dot_last(after)
    d_optical = shade * after - later
    raw_grads = [d_optical * spacing * gate]
    for c in range(3):
        raw_grads.append(spread[c] * weight * colour[c] * (1.0 - colour[c]))
    for o in range(4):
        raw_ref[pl.ds(o, NB, stride=8), :] = raw_grads[o]
    for o in range(4, 8):
        raw_ref[pl.ds(o, NB, stride=8), :] = jnp.zeros((NB, LANES), F32)
    grad_ref[...] = jnp.zeros_like(grad_ref)

    def backward(step, carry):
        parts = []
        for j in range(GR):
            b = step * GR + j
            rg = raw_ref[pl.ds(b * 8, 8), :].astype(BF16)
            parts.append(dot(rg, hidden_ref[b], ((1,), (1,))))
        for j in range(GR):
            region = table_ref[0, step * GR + j]
            grad_ref[0, region] += parts[j][0:4, :LANES]
            grad_ref[1, region] += parts[j][0:4, LANES:]
        return carry

    lax.fori_loop(0, groups, backward, 0)


def exact_dot_last(after):
    row, col = iota((LANES, LANES), 0), iota((LANES, LANES), 1)
    pattern = ((row // S == col // S) & (row % S == S - 1)).astype(F32).astype(BF16)
    return exact_dot(after, pattern)


def params(mib, **kw):
    return pltpu.CompilerParams(vmem_limit_bytes=mib * 1024 * 1024, **kw)


def gather_nets(crossed, points, spacing, freq, hidden, head):
    return pl.pallas_call(
        gather_kernel,
        out_shape=(
            jax.ShapeDtypeStruct((4, 4, 4, 2, HID + 32, LANES), BF16),
            jax.ShapeDtypeStruct((NB, LANES, LANES), BF16),
            jax.ShapeDtypeStruct((4, NB, SEG), BF16),
            jax.ShapeDtypeStruct((NB, LANES), F32),
            jax.ShapeDtypeStruct((1, 384), jnp.int32),
        ),
        in_specs=[ANY] * 6,
        out_specs=(HBM, HBM, HBM, VM, VM),
        scratch_shapes=[
            pltpu.VMEM((HID + 32, LANES), BF16),
            pltpu.VMEM((REG, 4, LANES), FREQ_TYPE),
            pltpu.VMEM((NB, LANES, LANES), BF16),
            pltpu.VMEM((4, NB, SEG), BF16),
            pltpu.VMEM((NB * 4, LANES), F32),
            pltpu.SMEM((1, 384), jnp.int32),
            pltpu.VMEM((K, RAYS), jnp.int32),
            pltpu.VMEM((3, RAYS, LANES), F32),
            pltpu.VMEM((RAYS, LANES), F32),
            pltpu.VMEM((3, FREQ), BF16),
            pltpu.VMEM((LANES, HID), BF16),
            pltpu.VMEM((4, HID), BF16),
            pltpu.SemaphoreType.DMA((COPIES,)),
            pltpu.SemaphoreType.DMA((COPIES,)),
            pltpu.SemaphoreType.DMA((2,)),
            pltpu.SemaphoreType.DMA((2,)),
            pltpu.SemaphoreType.DMA,
            pltpu.SemaphoreType.DMA((NB // GF,)),
            pltpu.SemaphoreType.DMA((8,)),
        ],
        compiler_params=params(50, collective_id=0, has_side_effects=True),
    )(crossed, points, spacing, freq, hidden, head)


def render_all(table, spacing, colour_grad, picks, feature, nets):
    return pl.pallas_call(
        render_kernel,
        out_shape=(
            jax.ShapeDtypeStruct((3, RAYS), F32),
            jax.ShapeDtypeStruct((2, REG, 4, LANES), F32),
        ),
        in_specs=[SM, VM, VM, HBM, HBM, HBM],
        out_specs=(VM, VM),
        scratch_shapes=[
            pltpu.VMEM((NB, HID, LANES), BF16),
            pltpu.VMEM((NB * 8, LANES), F32),
            pltpu.VMEM((NB, LANES, LANES), BF16),
            pltpu.VMEM((REG, HID + 32, LANES), BF16),
            pltpu.VMEM((4, NB, SEG), BF16),
            pltpu.SemaphoreType.DMA((NB // GR,)),
            pltpu.SemaphoreType.DMA((4,)),
            pltpu.SemaphoreType.DMA,
        ],
        compiler_params=params(60),
    )(table, spacing, colour_grad, picks, feature, nets)


def reduce_kernel(
    grad_ref, out_ref, got_a, sum_a, last_a, got_b, sum_b, last_b, send_sem, recv_sem
):
    me = lax.axis_index("region")
    base, inner, outer = me - lax.rem(me, 8), lax.rem(me, 8), lax.div(me, 8)
    barrier = pltpu.get_barrier_semaphore()
    greet(barrier, me)
    pl.semaphore_wait(barrier, 22)
    within = lambda step: base + lax.rem(inner + step, 8)
    across = lambda step: lax.rem(outer + step, 16) * 8 + inner

    def copy(src, dst, number, peer):
        return pltpu.make_async_remote_copy(
            src, dst, send_sem.at[number], recv_sem.at[number],
            device_id=(peer,), device_id_type=MESH_ID,
        )

    def each(count, first, make):
        def body(step, carry):
            make(step, first + step)
            return carry

        lax.fori_loop(1, count, body, 0)

    sent_a = lambda step: grad_ref.at[0, :, lax.rem(inner + step, 8)]
    sent_b = lambda step: grad_ref.at[1, lax.rem(outer + step, 16)]
    each(8, 0, lambda step, n: copy(sent_a(step), got_a.at[step], n, within(step)).start())
    each(16, 8, lambda step, n: copy(sent_b(step), got_b.at[step], n, across(step)).start())

    def add_a(step, total):
        copy(sent_a(step), got_a.at[step], step, within(step)).wait_recv()
        return total + got_a[step]

    sum_a[...] = lax.fori_loop(1, 8, add_a, grad_ref[0, :, inner])
    part_a = lambda step: sum_a.at[lax.rem(outer + step, 16)]
    each(16, 24, lambda step, n: copy(part_a(step), last_a.at[step], n, across(step)).start())

    def add_b(step, total):
        copy(sent_b(step), got_b.at[step], 8 + step, across(step)).wait_recv()
        return total + got_b[step]

    sum_b[...] = lax.fori_loop(1, 16, add_b, grad_ref[1, outer])
    part_b = lambda step: sum_b.at[lax.rem(inner + step, 8)]
    each(8, 40, lambda step, n: copy(part_b(step), last_b.at[step], n, within(step)).start())

    def end_a(step, total):
        copy(part_a(step), last_a.at[step], 24 + step, across(step)).wait_recv()
        return total + last_a[step]

    def end_b(step, total):
        copy(part_b(step), last_b.at[step], 40 + step, within(step)).wait_recv()
        return total + last_b[step]

    out_ref[:, :LANES] = lax.fori_loop(1, 16, end_a, sum_a[outer])
    out_ref[:, LANES:] = lax.fori_loop(1, 8, end_b, sum_b[inner])
    each(8, 0, lambda step, n: copy(sent_a(step), got_a.at[step], n, within(step)).wait_send())
    each(16, 8, lambda step, n: copy(sent_b(step), got_b.at[step], n, across(step)).wait_send())
    each(16, 24, lambda step, n: copy(part_a(step), last_a.at[step], n, across(step)).wait_send())
    each(8, 40, lambda step, n: copy(part_b(step), last_b.at[step], n, within(step)).wait_send())


def reduce_heads(grad):
    return pl.pallas_call(
        reduce_kernel,
        out_shape=jax.ShapeDtypeStruct((4, HID), F32),
        in_specs=[VM],
        out_specs=VM,
        scratch_shapes=[
            pltpu.VMEM((8, 16, 4, LANES), F32),
            pltpu.VMEM((16, 4, LANES), F32),
            pltpu.VMEM((16, 4, LANES), F32),
            pltpu.VMEM((16, 8, 4, LANES), F32),
            pltpu.VMEM((8, 4, LANES), F32),
            pltpu.VMEM((8, 4, LANES), F32),
            pltpu.SemaphoreType.DMA((48,)),
            pltpu.SemaphoreType.DMA((48,)),
        ],
        compiler_params=params(16, collective_id=1, has_side_effects=True),
    )(grad.reshape(2, 16, 8, 4, LANES))


def on_device(sample_points, sample_spacing, crossed, colour_grad, freq, w_hidden, w_head):
    nets, feature, picks, spacing, table = gather_nets(
        crossed.T, sample_points.transpose(1, 0, 2), sample_spacing, freq[0], w_hidden[0], w_head[0]
    )
    nets = nets.reshape(REG, HID + 32, LANES)
    rendered, grad = render_all(table, spacing, colour_grad, picks, feature, nets)
    return rendered, reduce_heads(grad)[None]


def solution(mesh):
    return jax.shard_map(
        on_device,
        mesh=mesh,
        in_specs=(
            P("region", None, None),
            P("region", None),
            P("region", None),
            P(None, "region"),
            P("region", None, None),
            P("region", None, None),
            P("region", None, None),
        ),
        out_specs=(P(None, "region"), P("region", None, None)),
        check_vma=False,
    )
```

```python
import functools

import jax
import jax.numpy as jnp
import numpy as np
from jax import lax
from jax.experimental import pallas as pl
from jax.experimental.pallas import tpu as pltpu
from jax.sharding import PartitionSpec as P

RAYS = 256
K = 4
S = 32
REG = 128
SEG = RAYS * K
NB = 352
FREQ = 64
HID = 256
LANES = 128
NETS = HID + 8
PART = NETS // 3
COPIES = 152
GF = 32
CHUNKS = (2, 3, 2, 1, 1, 1, 1)
GR = 32
GB = 32
AHEAD = 3
PARTS = 8
BOUNDS = 376

F32 = jnp.float32
BF16 = jnp.bfloat16
FREQ_TYPE = BF16

SIN_C = (4.44288292, -7.3082457, 3.60635441, -0.84611289, 0.10982699)
COS_C = (1.4142135, -6.97885099, 5.73946117, -1.88356298, 0.31069819)

HBM = pl.BlockSpec(memory_space=pltpu.HBM)
VM = pl.BlockSpec(memory_space=pltpu.VMEM)
SM = pl.BlockSpec(memory_space=pltpu.SMEM)
ANY = pl.BlockSpec(memory_space=pl.ANY)


def iota(shape, dim):
    return lax.broadcasted_iota(jnp.int32, shape, dim)


def dot(a, b, dims=((1,), (0,))):
    return lax.dot_general(a, b, (dims, ((), ())), preferred_element_type=F32)


def pieces(x):
    hi = x.astype(BF16)
    rest = x - hi.astype(F32)
    mid = rest.astype(BF16)
    low = (rest - mid.astype(F32)).astype(BF16)
    return hi, mid, low


def exact_dot(x, pattern):
    hi, mid, low = pieces(x)
    return dot(hi, pattern) + dot(mid, pattern) + dot(low, pattern)


def poly(z, coef):
    out = coef[-1] * z + coef[-2]
    for value in coef[-3::-1]:
        out = out * z + value
    return out


def sort_places(crossed):
    owner = jnp.concatenate([crossed[k:k + 1] for k in range(K)], axis=1)
    onehot = (iota((REG, SEG), 0) == owner).astype(F32)
    onehot16 = onehot.astype(BF16)
    earlier = (iota((SEG, SEG), 0) < iota((SEG, SEG), 1)).astype(F32).astype(BF16)
    rank = dot(onehot16, earlier)
    counts = jnp.sum(onehot, axis=1, keepdims=True)
    blocks = jnp.floor((counts + 3.0) * 0.25)
    lower = (iota((REG, REG), 1) <= iota((REG, REG), 0)).astype(F32).astype(BF16)
    ends = dot(lower, jnp.broadcast_to(blocks, (REG, LANES)).astype(BF16))[:, :1]
    starts = ends - blocks
    rank_row = jnp.sum(onehot * rank, axis=0, keepdims=True)
    start_row = jnp.sum(onehot * starts, axis=0, keepdims=True)
    step = jnp.floor(rank_row * 0.25)
    place = (rank_row - 4.0 * step) * NB + start_row + step
    block_at = iota((REG, 384), 1).astype(F32)
    owner_of = jnp.sum((block_at >= ends).astype(F32), axis=0, keepdims=True)
    owner_of = jnp.minimum(owner_of, REG - 1.0)
    total = jnp.sum(blocks, axis=0, keepdims=True)
    table = jnp.where(iota((1, 384), 1) == 383, total, owner_of)
    for part in range(PARTS - 1):
        last = (part + 1) * (REG // PARTS)
        table = jnp.where(iota((1, 384), 1) == BOUNDS + part, ends[last - 1:last], table)
    return place.astype(jnp.int32), table.astype(jnp.int32)


def sort_sources(sources):
    lane_group = iota((RAYS, LANES), 1) // S
    rows = []
    for k in range(K):
        row = jnp.zeros((RAYS, LANES), F32)
        for c in range(4):
            moved = sources[c]
            if c != k:
                moved = pltpu.roll(moved, ((c - k) % 4) * S, 1)
            row = jnp.where(lane_group == c, moved, row)
        rows.append(row)
    packed = jnp.concatenate(rows, axis=0)
    return jnp.concatenate(pieces(packed), axis=1)


def sort_coords(picks_ref, source, coords_ref):
    block_group = iota((NB, LANES), 1) // S
    coords = [jnp.zeros((NB, LANES), F32) for _ in range(4)]
    for q in range(4):
        three = dot(picks_ref[q], source)
        got = three[:, :128] + three[:, 128:256] + three[:, 256:]
        for c in range(4):
            moved = got
            if c != q:
                moved = pltpu.roll(got, ((q - c) % 4) * S, 1)
            coords[c] = jnp.where(block_group == q, moved, coords[c])
    for c in range(4):
        value = coords[c] * np.float32(0.5 / np.pi) if c < 3 else coords[c]
        coords_ref[pl.ds(c, NB, stride=4), :] = value
    return coords[3]


def bounded(region):
    return jnp.maximum(jnp.minimum(region, REG - 1), 0)


def features_of(freq, coords):
    freq = freq.astype(F32)
    f12 = jnp.concatenate([freq, freq, freq], axis=0).astype(BF16)
    hi = coords.astype(BF16).astype(F32)
    mid = (coords - hi).astype(BF16).astype(F32)
    low = coords - hi - mid
    x12 = jnp.concatenate([hi, mid, low], axis=0).astype(BF16)
    return dot(f12, x12, ((0,), (0,)))[:FREQ]


def encode(turns):
    r = turns - jnp.round(turns)
    z = r * r
    s = r * poly(z, SIN_C)
    c = poly(z, COS_C)
    return jnp.concatenate([s * c, 1.0 - s * s], axis=0).astype(BF16)


ORDERS = ((0, 1, 2), (1, 2, 0), (2, 0, 1))
STRIDES = (32, 8, 2)
MESH_ID = pl.DeviceIdType.MESH


def greet(barrier, me):
    base, inner, outer = me - lax.rem(me, 8), lax.rem(me, 8), lax.div(me, 8)

    def within(step, carry):
        peer = base + lax.rem(inner + step, 8)
        pl.semaphore_signal(barrier, inc=1, device_id=(peer,), device_id_type=MESH_ID)
        return carry

    def across(step, carry):
        peer = lax.rem(outer + step, 16) * 8 + inner
        pl.semaphore_signal(barrier, inc=1, device_id=(peer,), device_id_type=MESH_ID)
        return carry

    lax.fori_loop(1, 8, within, 0)
    lax.fori_loop(1, 16, across, 0)


def gather_kernel(
    crossed_hbm, points_hbm, spacing_hbm, freq_hbm, hidden_hbm, head_hbm,
    nets_ref, feature_out_ref, picks_out_ref, spacing_out_ref, table_out_ref,
    payload_ref, freq_ref, feature_ref, picks_ref, coords_ref, table_ref,
    crossed_ref, points_ref, spacing_ref, freq_in_ref, hidden_in_ref, head_in_ref,
    send_sem, recv_sem, freq_send, freq_recv, local_sem, feature_sem, input_sem,
):
    me = lax.axis_index("region")
    core = lax.rem(me, 2)
    sibling = me + 1 - 2 * core
    pos = [lax.rem(lax.div(me, stride), 4) for stride in STRIDES]
    base, inner, outer = me - lax.rem(me, 8), lax.rem(me, 8), lax.div(me, 8)
    barrier = pltpu.get_barrier_semaphore()
    inputs = [
        pltpu.make_async_copy(src, dst, input_sem.at[number])
        for number, (src, dst) in enumerate((
            (hidden_hbm, hidden_in_ref), (freq_hbm, freq_in_ref), (head_hbm, head_in_ref),
            (crossed_hbm, crossed_ref), (points_hbm, points_ref), (spacing_hbm, spacing_ref),
        ))
    ]
    for copy in inputs:
        copy.start()
    greet(barrier, me)
    for copy in inputs[:3]:
        copy.wait()
    payload_ref[0:HID, :] = hidden_in_ref[...].astype(F32).T.astype(BF16)
    head = head_in_ref[...].astype(F32)
    head = jnp.concatenate([head[:, :LANES], head[:, LANES:]], axis=0)
    payload_ref[HID:NETS, :] = head.astype(BF16)
    freq_in = jnp.concatenate([freq_in_ref[...].astype(F32), jnp.zeros((3, FREQ), F32)], axis=1)
    freq_in = jnp.concatenate([freq_in, jnp.zeros((1, LANES), F32)], axis=0)
    freq_ref[me] = freq_in.astype(FREQ_TYPE)
    pl.semaphore_wait(barrier, 22)

    def freq_within(step, carry):
        peer = base + lax.rem(inner + step, 8)
        pltpu.make_async_remote_copy(
            freq_ref.at[me], freq_ref.at[me], freq_send.at[0], freq_recv.at[0],
            device_id=(peer,), device_id_type=MESH_ID,
        ).start()
        return carry

    def freq_across(step, carry):
        peer = lax.rem(outer + step, 16) * 8 + inner
        rows = pl.ds(base, 8)
        pltpu.make_async_remote_copy(
            freq_ref.at[rows], freq_ref.at[rows], freq_send.at[1], freq_recv.at[1],
            device_id=(peer,), device_id_type=MESH_ID,
        ).start()
        return carry

    lax.fori_loop(1, 8, freq_within, 0)

    counter = [0]
    sends = []

    def new_id():
        counter[0] += 1
        return counter[0] - 1

    def device(axis, delta):
        return me + (lax.rem(pos[axis] + delta, 4) - pos[axis]) * STRIDES[axis]

    def view(where, parity, rows):
        return nets_ref.at[where[0], where[1], where[2], parity, rows, :]

    def start(src, dst, peer, number):
        copy = pltpu.make_async_remote_copy(
            src, dst, send_sem.at[number], recv_sem.at[number],
            device_id=(peer,), device_id_type=MESH_ID,
        )
        copy.start()
        sends.append(copy)

    def arrive(dst, number):
        pltpu.make_async_remote_copy(
            dst, dst, send_sem.at[number], recv_sem.at[number],
            device_id=(sibling,), device_id_type=MESH_ID,
        ).wait_recv()

    home = {0: pos[0], 1: pos[1], 2: pos[2]}
    sibling_waits = []

    def to_sibling(where, rows):
        number = new_id()
        start(view(where, core, rows), view(where, core, rows), sibling, number)
        sibling_waits.append((view(where, 1 - core, rows), number))

    whole = pl.ds(0, 4)

    def make_stream(t):
        a, b, c = ORDERS[t]
        rows = pl.ds(PART * t, PART)
        base = dict(home)
        left = {axis: lax.rem(pos[axis] + 3, 4) for axis in range(3)}
        right = {axis: lax.rem(pos[axis] + 1, 4) for axis in range(3)}
        opposite = {axis: lax.rem(pos[axis] + 2, 4) for axis in range(3)}

        def spec(**kw):
            out = dict(base)
            for key, value in kw.items():
                out[{"a": a, "b": b, "c": c}[key]] = value
            return out

        ids = {}

        def send(name, axis, delta, where, src=None):
            number = new_id()
            source = view(where, core, rows) if src is None else src
            start(source, view(where, core, rows), device(axis, delta), number)
            ids[name] = number

        def wait(name, where):
            arrive(view(where, core, rows), ids[name])

        def stage0():
            mine = payload_ref.at[rows, :]
            send("A+", a, 1, spec(), src=mine)
            send("A-", a, 3, spec(), src=mine)
            send("A=", a, 2, spec(), src=mine)
            send("B+o", b, 1, spec(), src=mine)
            send("B-o", b, 3, spec(), src=mine)
            send("C+o", c, 1, spec(), src=mine)
            send("C-o", c, 3, spec(), src=mine)

        def spread(where, tag):
            send("B+" + tag, b, 1, where)
            send("B-" + tag, b, 3, where)
            send("C+" + tag, c, 1, where)
            send("C-" + tag, c, 3, where)

        def stage1():
            low, high, across = spec(a=left[a]), spec(a=right[a]), spec(a=opposite[a])
            wait("A+", low)
            spread(low, "l")
            wait("A-", high)
            spread(high, "r")
            wait("A=", across)
            spread(across, "d")

        def stage2():
            for chip in (left[a], right[a], opposite[a]):
                to_sibling(spec(a=chip), rows)

        def line_arrivals(prefix, **kw):
            wait(prefix + "o", spec(**kw))
            wait(prefix + "l", spec(a=left[a], **kw))
            wait(prefix + "r", spec(a=right[a], **kw))
            wait(prefix + "d", spec(a=opposite[a], **kw))

        def stage3():
            line_arrivals("B+", b=left[b])
            low = spec(a=whole, b=left[b])
            send("BH+", b, 1, spec(a=pl.ds(0, 2), b=left[b]))
            send("C+L", c, 1, low)
            send("C-L", c, 3, low)
            line_arrivals("B-", b=right[b])
            high = spec(a=whole, b=right[b])
            send("BH-", b, 3, spec(a=pl.ds(2, 2), b=right[b]))
            send("C+R", c, 1, high)
            send("C-R", c, 3, high)
            to_sibling(low, rows)
            to_sibling(high, rows)

        def stage4():
            line_arrivals("C+", c=left[c])
            send("CH+o", c, 1, spec(a=whole, c=left[c]))
            wait("BH+", spec(a=pl.ds(0, 2), b=opposite[b]))
            wait("BH-", spec(a=pl.ds(2, 2), b=opposite[b]))
            across = spec(a=whole, b=opposite[b])
            send("C+D", c, 1, across)
            send("C-D", c, 3, across)
            to_sibling(across, rows)

        def stage5():
            line_arrivals("C-", c=right[c])
            wait("C-R", spec(a=whole, b=right[b], c=right[c]))
            send("CH-R", c, 3, spec(a=whole, b=right[b], c=right[c]))
            wait("C+L", spec(a=whole, b=left[b], c=left[c]))
            send("CH+L", c, 1, spec(a=whole, b=left[b], c=left[c]))
            to_sibling(spec(a=whole, c=left[c]), rows)
            to_sibling(spec(a=whole, c=right[c]), rows)
            to_sibling(spec(a=whole, b=left[b], c=left[c]), rows)
            to_sibling(spec(a=whole, b=right[b], c=right[c]), rows)

        def stage6():
            wait("C-D", spec(a=whole, b=opposite[b], c=right[c]))
            send("CH-D", c, 3, spec(a=whole, b=opposite[b], c=right[c]))
            wait("C+R", spec(a=whole, b=right[b], c=left[c]))
            wait("C+D", spec(a=whole, b=opposite[b], c=left[c]))
            wait("C-L", spec(a=whole, b=left[b], c=right[c]))
            to_sibling(spec(a=whole, b=right[b], c=left[c]), rows)
            to_sibling(spec(a=whole, b=opposite[b], c=left[c]), rows)
            to_sibling(spec(a=whole, b=left[b], c=right[c]), rows)
            to_sibling(spec(a=whole, b=opposite[b], c=right[c]), rows)

        def stage7(name, line):
            where = spec(a=whole, b=line, c=opposite[c])
            wait(name, where)
            to_sibling(where, rows)

        lines = (("CH+o", pos[b]), ("CH+L", left[b]), ("CH-R", right[b]), ("CH-D", opposite[b]))
        last = [functools.partial(stage7, name, line) for name, line in lines]
        return [stage0, stage1, stage2, stage3, stage4, stage5, stage6] + last

    streams = [make_stream(t) for t in range(3)]

    def stage(number):
        for stream in streams:
            stream[number]()

    stage(0)
    own = new_id()
    start(payload_ref, view(home, core, pl.ds(0, NETS)), sibling, own)
    sibling_waits.append((view(home, 1 - core, pl.ds(0, NETS)), own))
    keep = pltpu.make_async_copy(payload_ref, view(home, core, pl.ds(0, NETS)), local_sem)
    keep.start()

    def features(first, count):
        def body(step, carry):
            turns = []
            for j in range(GF):
                b = step * GF + j
                turns.append(features_of(freq_ref[bounded(table_ref[0, b])], coords_ref[pl.ds(b * 4, 4), :]))
            for j in range(GF):
                feature_ref[step * GF + j] = encode(turns[j])
            return carry

        lax.fori_loop(first, first + count, body, 0)
        part = pl.ds(first * GF, count * GF)
        copy = pltpu.make_async_copy(
            feature_ref.at[part], feature_out_ref.at[part], feature_sem.at[first]
        )
        copy.start()
        feature_copies.append(copy)

    feature_copies = []
    inputs[3].wait()
    place, table = sort_places(crossed_ref[...])
    table_out_ref[...] = table
    table_copy = pltpu.make_async_copy(table_out_ref, table_ref, input_sem.at[6])
    table_copy.start()
    seven, many = freq_ref.at[pl.ds(0, 7)], freq_ref.at[pl.ds(0, 120)]
    pltpu.make_async_copy(seven, seven, freq_recv.at[0]).wait()
    lax.fori_loop(1, 16, freq_across, 0)
    stage(1)
    for q in range(4):
        picks_ref[q] = (iota((NB, SEG), 0) + q * NB == place).astype(F32).astype(BF16)
    picks_copy = pltpu.make_async_copy(picks_ref, picks_out_ref, input_sem.at[7])
    picks_copy.start()
    stage(2)
    inputs[4].wait()
    inputs[5].wait()
    source = sort_sources([points_ref[0], points_ref[1], points_ref[2], spacing_ref[...]])
    stage(3)
    spacing_out_ref[...] = sort_coords(picks_ref, source, coords_ref)
    table_copy.wait()
    pltpu.make_async_copy(many, many, freq_recv.at[1]).wait()
    done = 0
    for number in range(4, 11):
        count = CHUNKS[number - 4]
        if count:
            features(done, count)
        done += count
        stage(number)
    for ref, number in sibling_waits:
        arrive(ref, number)
    for copy in sends:
        copy.wait_send()
    pltpu.make_async_copy(seven, seven, freq_send.at[0]).wait()
    pltpu.make_async_copy(many, many, freq_send.at[1]).wait()
    keep.wait()
    picks_copy.wait()
    for copy in feature_copies:
        copy.wait()


def tri(kind):
    row, col = iota((LANES, LANES), 0), iota((LANES, LANES), 1)
    same = row // S == col // S
    if kind == "upto":
        keep = row <= col
    elif kind == "after":
        keep = row > col
    else:
        keep = row >= 0
    return (same & keep).astype(F32).astype(BF16)


def render_kernel(
    table_ref, spacing_ref, colour_grad_ref, picks_hbm_ref, feature_hbm_ref, nets_hbm_ref,
    rendered_ref, grad_out_ref, hidden_ref, raw_ref, feature_ref, nets_ref, picks_ref, grad_ref,
    feature_sem, nets_sem, picks_sem,
):
    total = table_ref[0, 383]

    groups = lax.div(total + (GR - 1), GR)

    def net_copy(part):
        rows = pl.ds(part * (REG // PARTS), REG // PARTS)
        return pltpu.make_async_copy(nets_hbm_ref.at[rows], nets_ref.at[rows], nets_sem.at[part])

    def feature_copy(step):
        rows = pl.ds(step * GR, GR)
        return pltpu.make_async_copy(feature_hbm_ref.at[rows], feature_ref.at[rows], feature_sem.at[step])

    net_copy(0).start()
    feature_copy(0).start()
    net_copy(1).start()
    for step in range(1, AHEAD):
        feature_copy(step).start()
    picks_copy = pltpu.make_async_copy(picks_hbm_ref, picks_ref, picks_sem)

    def raw_of(step):
        outs = []
        for j in range(GR):
            b = step * GR + j
            head = nets_ref[table_ref[0, b], HID:NETS, :].astype(F32)
            head = jnp.concatenate([head[0:4], head[4:8]], axis=1)
            head = jnp.concatenate([head, jnp.zeros((4, HID), F32)], axis=0).astype(BF16)
            outs.append(dot(head, hidden_ref[b]))
        for j in range(GR):
            raw_ref[pl.ds((step * GR + j) * 8, 8), :] = outs[j]

    def forward(step, carry):
        @pl.when(step + AHEAD < groups)
        def _():
            feature_copy(step + AHEAD).start()

        feature_copy(step).wait()
        raw_of(jnp.maximum(step - 1, 0))
        for j in range(GR):
            b = step * GR + j
            hid = dot(nets_ref[table_ref[0, b], 0:HID, :], feature_ref[b])
            hidden_ref[b] = jnp.maximum(hid, 0.0).astype(BF16)
        return carry

    def blank(step, carry):
        for j in range(GR):
            raw_ref[pl.ds((step * GR + j) * 8, 8), :] = jnp.zeros((8, LANES), F32)
        return carry

    first = 0
    for part in range(PARTS):
        if part + 2 < PARTS:
            net_copy(part + 2).start()
        elif part + 2 == PARTS:
            picks_copy.start()
        net_copy(part).wait()
        last = groups if part == PARTS - 1 else lax.div(table_ref[0, BOUNDS + part], GR)
        lax.fori_loop(first, last, forward, 0)
        first = last
    raw_of(groups - 1)
    lax.fori_loop(groups, NB // GR, blank, 0)
    for step in range(AHEAD):
        @pl.when(step >= groups)
        def _(step=step):
            feature_copy(step).wait()

    raw = [raw_ref[pl.ds(o, NB, stride=8), :] for o in range(4)]
    spacing = spacing_ref[...]
    picks_copy.wait()
    soft = jnp.maximum(raw[0], 0.0) + jnp.log1p(jnp.exp(-jnp.abs(raw[0])))
    colour = [1.0 / (1.0 + jnp.exp(-raw[c])) for c in (1, 2, 3)]
    gate = 1.0 / (1.0 + jnp.exp(-raw[0]))
    optical = soft * spacing
    running = exact_dot(optical, tri("upto"))
    after = jnp.exp(-running)
    weight = jnp.exp(optical - running) * (1.0 - jnp.exp(-optical))
    chooser = (iota((8, LANES), 1) // S == iota((8, LANES), 0)).astype(F32).astype(BF16)
    last = (iota((8, LANES), 1) == iota((8, LANES), 0) * S + (S - 1)).astype(F32).astype(BF16)

    def seg_rows(value, pattern):
        return [dot(pattern, part, ((1,), (1,))) for part in pieces(value)]

    sums = []
    for c in range(3):
        three = seg_rows(weight * colour[c], chooser)
        sums.append(three[0] + three[1] + three[2])
    three = seg_rows(after, last)
    sums.append(three[0] + three[1] + three[2])
    by_seg = jnp.zeros((16, SEG), F32)
    for q in range(4):
        four = jnp.concatenate([value[q:q + 1] for value in sums], axis=0)
        hi, mid, low = pieces(four)
        rows = jnp.concatenate(
            [hi.astype(F32), mid.astype(F32), low.astype(F32), jnp.zeros((4, NB), F32)], axis=0
        )
        by_seg = by_seg + dot(rows.astype(BF16), picks_ref[q])
    partial = by_seg[0:4] + by_seg[4:8] + by_seg[8:12]
    seg_colour = [partial[0:3, k * RAYS:(k + 1) * RAYS] for k in range(K)]
    seg_trans = [partial[3:4, k * RAYS:(k + 1) * RAYS] for k in range(K)]
    upstream = colour_grad_ref[...]
    before = jnp.ones((1, RAYS), F32)
    befores = []
    rendered = jnp.zeros((3, RAYS), F32)
    for k in range(K):
        befores.append(before)
        rendered = rendered + before * seg_colour[k]
        before = before * seg_trans[k]
    rendered_ref[...] = rendered
    behind = jnp.zeros((3, RAYS), F32)
    grads = [None] * K
    for k in range(K - 1, -1, -1):
        trans = befores[k] * jnp.sum(upstream * behind, axis=0, keepdims=True)
        grads[k] = jnp.concatenate([befores[k] * upstream, trans], axis=0)
        behind = seg_colour[k] + seg_trans[k] * behind
    grad_rows = jnp.concatenate(grads, axis=1)
    hi, mid, low = pieces(grad_rows)
    grad_rows = jnp.concatenate(
        [hi.astype(F32), mid.astype(F32), low.astype(F32), jnp.zeros((4, SEG), F32)], axis=0
    ).astype(BF16)
    spread = [jnp.zeros((NB, LANES), F32) for _ in range(4)]
    for q in range(4):
        got = dot(picks_ref[q], grad_rows, ((1,), (1,))).astype(BF16)
        lane = iota((16, LANES), 1) // S == q
        for o in range(4):
            row = iota((16, LANES), 0)
            expand = (lane & (row % 4 == o) & (row < 12)).astype(F32).astype(BF16)
            spread[o] = spread[o] + dot(got, expand)
    shade = spread[0] * colour[0] + spread[1] * colour[1] + spread[2] * colour[2]
    later = exact_dot(shade * weight, tri("after")) + spread[3] * exact_dot_last(after)
    d_optical = shade * after - later
    raw_grads = [d_optical * spacing * gate]
    for c in range(3):
        raw_grads.append(spread[c] * weight * colour[c] * (1.0 - colour[c]))
    for o in range(4):
        raw_ref[pl.ds(o, NB, stride=8), :] = raw_grads[o]
    for o in range(4, 8):
        raw_ref[pl.ds(o, NB, stride=8), :] = jnp.zeros((NB, LANES), F32)
    grad_ref[...] = jnp.zeros_like(grad_ref)

    def backward(step, carry):
        total_grad, before_region = carry
        parts = []
        for j in range(GB):
            b = step * GB + j
            rg = raw_ref[pl.ds(b * 8, 8), :].astype(BF16)
            parts.append(dot(rg, hidden_ref[b], ((1,), (1,))))
        for j in range(GB):
            region = table_ref[0, step * GB + j]
            total_grad = parts[j] + jnp.where(region == before_region, total_grad, 0.0)
            grad_ref[0, region] = total_grad[0:4, :LANES]
            grad_ref[1, region] = total_grad[0:4, LANES:]
            before_region = region
        return total_grad, before_region

    start = (jnp.zeros((8, HID), F32), jnp.int32(-1))
    lax.fori_loop(0, lax.div(total + (GB - 1), GB), backward, start)
    grad_copy = pltpu.make_async_copy(grad_ref, grad_out_ref, picks_sem)
    grad_copy.start()
    grad_copy.wait()


def exact_dot_last(after):
    row, col = iota((LANES, LANES), 0), iota((LANES, LANES), 1)
    pattern = ((row // S == col // S) & (row % S == S - 1)).astype(F32).astype(BF16)
    return exact_dot(after, pattern)


def params(mib, **kw):
    return pltpu.CompilerParams(vmem_limit_bytes=mib * 1024 * 1024, **kw)


def gather_nets(crossed, points, spacing, freq, hidden, head):
    return pl.pallas_call(
        gather_kernel,
        out_shape=(
            jax.ShapeDtypeStruct((4, 4, 4, 2, NETS, LANES), BF16),
            jax.ShapeDtypeStruct((NB, LANES, LANES), BF16),
            jax.ShapeDtypeStruct((4, NB, SEG), BF16),
            jax.ShapeDtypeStruct((NB, LANES), F32),
            jax.ShapeDtypeStruct((1, 384), jnp.int32),
        ),
        in_specs=[HBM] * 6,
        out_specs=(HBM, HBM, HBM, VM, VM),
        scratch_shapes=[
            pltpu.VMEM((NETS, LANES), BF16),
            pltpu.VMEM((REG, 4, LANES), FREQ_TYPE),
            pltpu.VMEM((NB, LANES, LANES), BF16),
            pltpu.VMEM((4, NB, SEG), BF16),
            pltpu.VMEM((NB * 4, LANES), F32),
            pltpu.SMEM((1, 384), jnp.int32),
            pltpu.VMEM((K, RAYS), jnp.int32),
            pltpu.VMEM((3, RAYS, LANES), F32),
            pltpu.VMEM((RAYS, LANES), F32),
            pltpu.VMEM((3, FREQ), BF16),
            pltpu.VMEM((LANES, HID), BF16),
            pltpu.VMEM((4, HID), BF16),
            pltpu.SemaphoreType.DMA((COPIES,)),
            pltpu.SemaphoreType.DMA((COPIES,)),
            pltpu.SemaphoreType.DMA((2,)),
            pltpu.SemaphoreType.DMA((2,)),
            pltpu.SemaphoreType.DMA,
            pltpu.SemaphoreType.DMA((NB // GF,)),
            pltpu.SemaphoreType.DMA((8,)),
        ],
        compiler_params=params(62, collective_id=0, has_side_effects=True),
    )(crossed, points, spacing, freq, hidden, head)


def render_all(table, spacing, colour_grad, picks, feature, nets):
    return pl.pallas_call(
        render_kernel,
        out_shape=(
            jax.ShapeDtypeStruct((3, RAYS), F32),
            jax.ShapeDtypeStruct((2, REG, 4, LANES), F32),
        ),
        in_specs=[SM, VM, VM, HBM, HBM, HBM],
        out_specs=(VM, HBM),
        scratch_shapes=[
            pltpu.VMEM((NB, HID, LANES), BF16),
            pltpu.VMEM((NB * 8, LANES), F32),
            pltpu.VMEM((NB, LANES, LANES), BF16),
            pltpu.VMEM((REG, NETS, LANES), BF16),
            pltpu.VMEM((4, NB, SEG), BF16),
            pltpu.VMEM((2, REG, 4, LANES), F32),
            pltpu.SemaphoreType.DMA((NB // GR,)),
            pltpu.SemaphoreType.DMA((PARTS,)),
            pltpu.SemaphoreType.DMA,
        ],
        compiler_params=params(62),
    )(table, spacing, colour_grad, picks, feature, nets)


def reduce_kernel(
    grad_hbm_ref, out_ref, grad_ref, got_a, sum_a, last_a, got_b, sum_b, last_b, send_sem, recv_sem, load_sem
):
    load = pltpu.make_async_copy(grad_hbm_ref, grad_ref, load_sem)
    load.start()
    me = lax.axis_index("region")
    base, inner, outer = me - lax.rem(me, 8), lax.rem(me, 8), lax.div(me, 8)
    barrier = pltpu.get_barrier_semaphore()
    greet(barrier, me)
    load.wait()
    pl.semaphore_wait(barrier, 22)
    within = lambda step: base + lax.rem(inner + step, 8)
    across = lambda step: lax.rem(outer + step, 16) * 8 + inner

    def copy(src, dst, number, peer):
        return pltpu.make_async_remote_copy(
            src, dst, send_sem.at[number], recv_sem.at[number],
            device_id=(peer,), device_id_type=MESH_ID,
        )

    def each(count, first, make):
        def body(step, carry):
            make(step, first + step)
            return carry

        lax.fori_loop(1, count, body, 0)

    sent_a = lambda step: grad_ref.at[0, :, lax.rem(inner + step, 8)]
    sent_b = lambda step: grad_ref.at[1, lax.rem(outer + step, 16)]
    each(8, 0, lambda step, n: copy(sent_a(step), got_a.at[step], n, within(step)).start())
    each(16, 8, lambda step, n: copy(sent_b(step), got_b.at[step], n, across(step)).start())

    def add_a(step, total):
        copy(sent_a(step), got_a.at[step], step, within(step)).wait_recv()
        return total + got_a[step]

    sum_a[...] = lax.fori_loop(1, 8, add_a, grad_ref[0, :, inner])
    part_a = lambda step: sum_a.at[lax.rem(outer + step, 16)]
    each(16, 24, lambda step, n: copy(part_a(step), last_a.at[step], n, across(step)).start())

    def add_b(step, total):
        copy(sent_b(step), got_b.at[step], 8 + step, across(step)).wait_recv()
        return total + got_b[step]

    sum_b[...] = lax.fori_loop(1, 16, add_b, grad_ref[1, outer])
    part_b = lambda step: sum_b.at[lax.rem(inner + step, 8)]
    each(8, 40, lambda step, n: copy(part_b(step), last_b.at[step], n, within(step)).start())

    def end_a(step, total):
        copy(part_a(step), last_a.at[step], 24 + step, across(step)).wait_recv()
        return total + last_a[step]

    def end_b(step, total):
        copy(part_b(step), last_b.at[step], 40 + step, within(step)).wait_recv()
        return total + last_b[step]

    out_ref[:, :LANES] = lax.fori_loop(1, 16, end_a, sum_a[outer])
    out_ref[:, LANES:] = lax.fori_loop(1, 8, end_b, sum_b[inner])
    each(8, 0, lambda step, n: copy(sent_a(step), got_a.at[step], n, within(step)).wait_send())
    each(16, 8, lambda step, n: copy(sent_b(step), got_b.at[step], n, across(step)).wait_send())
    each(16, 24, lambda step, n: copy(part_a(step), last_a.at[step], n, across(step)).wait_send())
    each(8, 40, lambda step, n: copy(part_b(step), last_b.at[step], n, within(step)).wait_send())


def reduce_heads(grad):
    return pl.pallas_call(
        reduce_kernel,
        out_shape=jax.ShapeDtypeStruct((4, HID), F32),
        in_specs=[HBM],
        out_specs=VM,
        scratch_shapes=[
            pltpu.VMEM((2, 16, 8, 4, LANES), F32),
            pltpu.VMEM((8, 16, 4, LANES), F32),
            pltpu.VMEM((16, 4, LANES), F32),
            pltpu.VMEM((16, 4, LANES), F32),
            pltpu.VMEM((16, 8, 4, LANES), F32),
            pltpu.VMEM((8, 4, LANES), F32),
            pltpu.VMEM((8, 4, LANES), F32),
            pltpu.SemaphoreType.DMA((48,)),
            pltpu.SemaphoreType.DMA((48,)),
            pltpu.SemaphoreType.DMA,
        ],
        compiler_params=params(62, collective_id=1, has_side_effects=True),
    )(grad.reshape(2, 16, 8, 4, LANES))


def on_device(sample_points, sample_spacing, crossed, colour_grad, freq, w_hidden, w_head):
    nets, feature, picks, spacing, table = gather_nets(
        crossed.T, sample_points.transpose(1, 0, 2), sample_spacing, freq[0], w_hidden[0], w_head[0]
    )
    nets = nets.reshape(REG, NETS, LANES)
    rendered, grad = render_all(table, spacing, colour_grad, picks, feature, nets)
    return rendered, reduce_heads(grad)[None]


def solution(mesh):
    return jax.shard_map(
        on_device,
        mesh=mesh,
        in_specs=(
            P("region", None, None),
            P("region", None),
            P("region", None),
            P(None, "region"),
            P("region", None, None),
            P("region", None, None),
            P("region", None, None),
        ),
        out_specs=(P(None, "region"), P("region", None, None)),
        check_vma=False,
    )
```

```python
import functools

import jax
import jax.numpy as jnp
import numpy as np
from jax import lax
from jax.experimental import pallas as pl
from jax.experimental.pallas import tpu as pltpu
from jax.sharding import PartitionSpec as P

RAYS = 256
K = 4
S = 32
REG = 128
SEG = RAYS * K
NB = 352
FREQ = 64
HID = 256
LANES = 128
NETS = HID + 8
PART = NETS // 3
COPIES = 96
GF = 32
CHUNKS = (2, 3, 2, 1, 1, 1, 1)
GR = 32
GB = 32
AHEAD = 3
PARTS = 8
BOUNDS = 376

F32 = jnp.float32
BF16 = jnp.bfloat16
FREQ_TYPE = BF16

SIN_C = (4.44288292, -7.3082457, 3.60635441, -0.84611289, 0.10982699)
COS_C = (1.4142135, -6.97885099, 5.73946117, -1.88356298, 0.31069819)

HBM = pl.BlockSpec(memory_space=pltpu.HBM)
VM = pl.BlockSpec(memory_space=pltpu.VMEM)
SM = pl.BlockSpec(memory_space=pltpu.SMEM)
ANY = pl.BlockSpec(memory_space=pl.ANY)


def iota(shape, dim):
    return lax.broadcasted_iota(jnp.int32, shape, dim)


def dot(a, b, dims=((1,), (0,))):
    return lax.dot_general(a, b, (dims, ((), ())), preferred_element_type=F32)


def pieces(x):
    hi = x.astype(BF16)
    rest = x - hi.astype(F32)
    mid = rest.astype(BF16)
    low = (rest - mid.astype(F32)).astype(BF16)
    return hi, mid, low


def exact_dot(x, pattern):
    hi, mid, low = pieces(x)
    return dot(hi, pattern) + dot(mid, pattern) + dot(low, pattern)


def poly(z, coef):
    out = coef[-1] * z + coef[-2]
    for value in coef[-3::-1]:
        out = out * z + value
    return out


def sort_places(crossed):
    owner = jnp.concatenate([crossed[k:k + 1] for k in range(K)], axis=1)
    onehot = (iota((REG, SEG), 0) == owner).astype(F32)
    onehot16 = onehot.astype(BF16)
    earlier = (iota((SEG, SEG), 0) < iota((SEG, SEG), 1)).astype(F32).astype(BF16)
    rank = dot(onehot16, earlier)
    counts = jnp.sum(onehot, axis=1, keepdims=True)
    blocks = jnp.floor((counts + 3.0) * 0.25)
    lower = (iota((REG, REG), 1) <= iota((REG, REG), 0)).astype(F32).astype(BF16)
    ends = dot(lower, jnp.broadcast_to(blocks, (REG, LANES)).astype(BF16))[:, :1]
    starts = ends - blocks
    rank_row = jnp.sum(onehot * rank, axis=0, keepdims=True)
    start_row = jnp.sum(onehot * starts, axis=0, keepdims=True)
    step = jnp.floor(rank_row * 0.25)
    place = (rank_row - 4.0 * step) * NB + start_row + step
    block_at = iota((REG, 384), 1).astype(F32)
    owner_of = jnp.sum((block_at >= ends).astype(F32), axis=0, keepdims=True)
    owner_of = jnp.minimum(owner_of, REG - 1.0)
    total = jnp.sum(blocks, axis=0, keepdims=True)
    table = jnp.where(iota((1, 384), 1) == 383, total, owner_of)
    for part in range(PARTS - 1):
        last = (part + 1) * (REG // PARTS)
        table = jnp.where(iota((1, 384), 1) == BOUNDS + part, ends[last - 1:last], table)
    return place.astype(jnp.int32), table.astype(jnp.int32)


def sort_sources(sources):
    lane_group = iota((RAYS, LANES), 1) // S
    rows = []
    for k in range(K):
        row = jnp.zeros((RAYS, LANES), F32)
        for c in range(4):
            moved = sources[c]
            if c != k:
                moved = pltpu.roll(moved, ((c - k) % 4) * S, 1)
            row = jnp.where(lane_group == c, moved, row)
        rows.append(row)
    packed = jnp.concatenate(rows, axis=0)
    return jnp.concatenate(pieces(packed), axis=1)


def sort_coords(picks_ref, source, coords_ref):
    block_group = iota((NB, LANES), 1) // S
    coords = [jnp.zeros((NB, LANES), F32) for _ in range(4)]
    for q in range(4):
        three = dot(picks_ref[q], source)
        got = three[:, :128] + three[:, 128:256] + three[:, 256:]
        for c in range(4):
            moved = got
            if c != q:
                moved = pltpu.roll(got, ((q - c) % 4) * S, 1)
            coords[c] = jnp.where(block_group == q, moved, coords[c])
    for c in range(4):
        value = coords[c] * np.float32(0.5 / np.pi) if c < 3 else coords[c]
        coords_ref[pl.ds(c, NB, stride=4), :] = value
    return coords[3]


def bounded(region):
    return jnp.maximum(jnp.minimum(region, REG - 1), 0)


def features_of(freq, coords):
    freq = freq.astype(F32)
    f12 = jnp.concatenate([freq, freq, freq], axis=0).astype(BF16)
    hi = coords.astype(BF16).astype(F32)
    mid = (coords - hi).astype(BF16).astype(F32)
    low = coords - hi - mid
    x12 = jnp.concatenate([hi, mid, low], axis=0).astype(BF16)
    return dot(f12, x12, ((0,), (0,)))[:FREQ]


def encode(turns):
    r = turns - jnp.round(turns)
    z = r * r
    s = r * poly(z, SIN_C)
    c = poly(z, COS_C)
    return jnp.concatenate([s * c, 1.0 - s * s], axis=0).astype(BF16)


ORDERS = ((0, 1, 2), (1, 2, 0), (2, 0, 1))
STRIDES = (32, 8, 2)
MESH_ID = pl.DeviceIdType.MESH


def greet(barrier, me):
    base, inner, outer = me - lax.rem(me, 8), lax.rem(me, 8), lax.div(me, 8)

    def within(step, carry):
        peer = base + lax.rem(inner + step, 8)
        pl.semaphore_signal(barrier, inc=1, device_id=(peer,), device_id_type=MESH_ID)
        return carry

    def across(step, carry):
        peer = lax.rem(outer + step, 16) * 8 + inner
        pl.semaphore_signal(barrier, inc=1, device_id=(peer,), device_id_type=MESH_ID)
        return carry

    lax.fori_loop(1, 8, within, 0)
    lax.fori_loop(1, 16, across, 0)


def gather_kernel(
    crossed_hbm, points_hbm, spacing_hbm, freq_hbm, hidden_hbm, head_hbm,
    nets_ref, feature_out_ref, picks_out_ref, spacing_out_ref, table_out_ref,
    payload_ref, freq_ref, feature_ref, picks_ref, coords_ref, table_ref,
    crossed_ref, points_ref, spacing_ref, freq_in_ref, hidden_in_ref, head_in_ref,
    send_sem, recv_sem, freq_send, freq_recv, local_sem, feature_sem, input_sem,
):
    me = lax.axis_index("region")
    core = lax.rem(me, 2)
    sibling = me + 1 - 2 * core
    pos = [lax.rem(lax.div(me, stride), 4) for stride in STRIDES]
    base, inner, outer = me - lax.rem(me, 8), lax.rem(me, 8), lax.div(me, 8)
    barrier = pltpu.get_barrier_semaphore()
    inputs = [
        pltpu.make_async_copy(src, dst, input_sem.at[number])
        for number, (src, dst) in enumerate((
            (hidden_hbm, hidden_in_ref), (freq_hbm, freq_in_ref), (head_hbm, head_in_ref),
            (crossed_hbm, crossed_ref), (points_hbm, points_ref), (spacing_hbm, spacing_ref),
        ))
    ]
    for copy in inputs:
        copy.start()
    greet(barrier, me)
    for copy in inputs[:3]:
        copy.wait()
    payload_ref[0:HID, :] = hidden_in_ref[...].astype(F32).T.astype(BF16)
    head = head_in_ref[...].astype(F32)
    head = jnp.concatenate([head[:, :LANES], head[:, LANES:]], axis=0)
    payload_ref[HID:NETS, :] = head.astype(BF16)
    freq_in = jnp.concatenate([freq_in_ref[...].astype(F32), jnp.zeros((3, FREQ), F32)], axis=1)
    freq_in = jnp.concatenate([freq_in, jnp.zeros((1, LANES), F32)], axis=0)
    freq_ref[me] = freq_in.astype(FREQ_TYPE)
    pl.semaphore_wait(barrier, 22)

    def freq_within(step, carry):
        peer = base + lax.rem(inner + step, 8)
        pltpu.make_async_remote_copy(
            freq_ref.at[me], freq_ref.at[me], freq_send.at[0], freq_recv.at[0],
            device_id=(peer,), device_id_type=MESH_ID,
        ).start()
        return carry

    def freq_across(step, carry):
        peer = lax.rem(outer + step, 16) * 8 + inner
        rows = pl.ds(base, 8)
        pltpu.make_async_remote_copy(
            freq_ref.at[rows], freq_ref.at[rows], freq_send.at[1], freq_recv.at[1],
            device_id=(peer,), device_id_type=MESH_ID,
        ).start()
        return carry

    lax.fori_loop(1, 8, freq_within, 0)

    counter = [0]

    def new_id():
        counter[0] += 1
        return counter[0] - 1

    def device(axis, delta):
        return me + (lax.rem(pos[axis] + delta, 4) - pos[axis]) * STRIDES[axis]

    def view(where, parity, rows):
        return nets_ref.at[where[0], where[1], where[2], parity, rows, :]

    def start(src, dst, peer, number):
        pltpu.make_async_remote_copy(
            src, dst, send_sem, recv_sem.at[number],
            device_id=(peer,), device_id_type=MESH_ID,
        ).start()

    def arrive(dst, number):
        pltpu.make_async_remote_copy(
            dst, dst, send_sem, recv_sem.at[number],
            device_id=(sibling,), device_id_type=MESH_ID,
        ).wait_recv()

    home = {0: pos[0], 1: pos[1], 2: pos[2]}

    def to_sibling(where, rows):
        start(view(where, core, rows), view(where, core, rows), sibling, COPIES)

    whole = pl.ds(0, 4)

    def make_stream(t):
        a, b, c = ORDERS[t]
        rows = pl.ds(PART * t, PART)
        base = dict(home)
        left = {axis: lax.rem(pos[axis] + 3, 4) for axis in range(3)}
        right = {axis: lax.rem(pos[axis] + 1, 4) for axis in range(3)}
        opposite = {axis: lax.rem(pos[axis] + 2, 4) for axis in range(3)}

        def spec(**kw):
            out = dict(base)
            for key, value in kw.items():
                out[{"a": a, "b": b, "c": c}[key]] = value
            return out

        ids = {}

        def send(name, axis, delta, where, src=None):
            number = new_id()
            source = view(where, core, rows) if src is None else src
            start(source, view(where, core, rows), device(axis, delta), number)
            ids[name] = number

        def wait(name, where):
            arrive(view(where, core, rows), ids[name])

        def stage0():
            mine = payload_ref.at[rows, :]
            send("A+", a, 1, spec(), src=mine)
            send("A-", a, 3, spec(), src=mine)
            send("A=", a, 2, spec(), src=mine)
            send("B+o", b, 1, spec(), src=mine)
            send("B-o", b, 3, spec(), src=mine)
            send("C+o", c, 1, spec(), src=mine)
            send("C-o", c, 3, spec(), src=mine)

        def spread(where, tag):
            send("B+" + tag, b, 1, where)
            send("B-" + tag, b, 3, where)
            send("C+" + tag, c, 1, where)
            send("C-" + tag, c, 3, where)

        def stage1():
            low, high, across = spec(a=left[a]), spec(a=right[a]), spec(a=opposite[a])
            wait("A+", low)
            spread(low, "l")
            wait("A-", high)
            spread(high, "r")
            wait("A=", across)
            spread(across, "d")

        def stage2():
            for chip in (left[a], right[a], opposite[a]):
                to_sibling(spec(a=chip), rows)

        def line_arrivals(prefix, **kw):
            wait(prefix + "o", spec(**kw))
            wait(prefix + "l", spec(a=left[a], **kw))
            wait(prefix + "r", spec(a=right[a], **kw))
            wait(prefix + "d", spec(a=opposite[a], **kw))

        def stage3():
            line_arrivals("B+", b=left[b])
            low = spec(a=whole, b=left[b])
            send("BH+", b, 1, spec(a=pl.ds(0, 2), b=left[b]))
            send("C+L", c, 1, low)
            send("C-L", c, 3, low)
            line_arrivals("B-", b=right[b])
            high = spec(a=whole, b=right[b])
            send("BH-", b, 3, spec(a=pl.ds(2, 2), b=right[b]))
            send("C+R", c, 1, high)
            send("C-R", c, 3, high)
            to_sibling(low, rows)
            to_sibling(high, rows)

        def stage4():
            line_arrivals("C+", c=left[c])
            send("CH+o", c, 1, spec(a=whole, c=left[c]))
            wait("BH+", spec(a=pl.ds(0, 2), b=opposite[b]))
            wait("BH-", spec(a=pl.ds(2, 2), b=opposite[b]))
            across = spec(a=whole, b=opposite[b])
            send("C+D", c, 1, across)
            send("C-D", c, 3, across)
            to_sibling(across, rows)

        def stage5():
            line_arrivals("C-", c=right[c])
            wait("C-R", spec(a=whole, b=right[b], c=right[c]))
            send("CH-R", c, 3, spec(a=whole, b=right[b], c=right[c]))
            wait("C+L", spec(a=whole, b=left[b], c=left[c]))
            send("CH+L", c, 1, spec(a=whole, b=left[b], c=left[c]))
            to_sibling(spec(a=whole, c=left[c]), rows)
            to_sibling(spec(a=whole, c=right[c]), rows)
            to_sibling(spec(a=whole, b=left[b], c=left[c]), rows)
            to_sibling(spec(a=whole, b=right[b], c=right[c]), rows)

        def stage6():
            wait("C-D", spec(a=whole, b=opposite[b], c=right[c]))
            send("CH-D", c, 3, spec(a=whole, b=opposite[b], c=right[c]))
            wait("C+R", spec(a=whole, b=right[b], c=left[c]))
            wait("C+D", spec(a=whole, b=opposite[b], c=left[c]))
            wait("C-L", spec(a=whole, b=left[b], c=right[c]))
            to_sibling(spec(a=whole, b=right[b], c=left[c]), rows)
            to_sibling(spec(a=whole, b=opposite[b], c=left[c]), rows)
            to_sibling(spec(a=whole, b=left[b], c=right[c]), rows)
            to_sibling(spec(a=whole, b=opposite[b], c=right[c]), rows)

        def stage7(name, line):
            where = spec(a=whole, b=line, c=opposite[c])
            wait(name, where)
            to_sibling(where, rows)

        lines = (("CH+o", pos[b]), ("CH+L", left[b]), ("CH-R", right[b]), ("CH-D", opposite[b]))
        last = [functools.partial(stage7, name, line) for name, line in lines]
        return [stage0, stage1, stage2, stage3, stage4, stage5, stage6] + last

    streams = [make_stream(t) for t in range(3)]

    def stage(number):
        for stream in streams:
            stream[number]()

    stage(0)
    start(payload_ref, view(home, core, pl.ds(0, NETS)), sibling, COPIES)
    keep = pltpu.make_async_copy(payload_ref, view(home, core, pl.ds(0, NETS)), local_sem)
    keep.start()

    def features(first, count):
        def body(step, carry):
            turns = []
            for j in range(GF):
                b = step * GF + j
                turns.append(features_of(freq_ref[bounded(table_ref[0, b])], coords_ref[pl.ds(b * 4, 4), :]))
            for j in range(GF):
                feature_ref[step * GF + j] = encode(turns[j])
            return carry

        lax.fori_loop(first, first + count, body, 0)
        part = pl.ds(first * GF, count * GF)
        copy = pltpu.make_async_copy(
            feature_ref.at[part], feature_out_ref.at[part], feature_sem.at[first]
        )
        copy.start()
        feature_copies.append(copy)

    feature_copies = []
    inputs[3].wait()
    place, table = sort_places(crossed_ref[...])
    table_out_ref[...] = table
    table_copy = pltpu.make_async_copy(table_out_ref, table_ref, input_sem.at[6])
    table_copy.start()
    seven, many = freq_ref.at[pl.ds(0, 7)], freq_ref.at[pl.ds(0, 120)]
    pltpu.make_async_copy(seven, seven, freq_recv.at[0]).wait()
    lax.fori_loop(1, 16, freq_across, 0)
    stage(1)
    for q in range(4):
        picks_ref[q] = (iota((NB, SEG), 0) + q * NB == place).astype(F32).astype(BF16)
    picks_copy = pltpu.make_async_copy(picks_ref, picks_out_ref, input_sem.at[7])
    picks_copy.start()
    stage(2)
    inputs[4].wait()
    inputs[5].wait()
    source = sort_sources([points_ref[0], points_ref[1], points_ref[2], spacing_ref[...]])
    stage(3)
    spacing_out_ref[...] = sort_coords(picks_ref, source, coords_ref)
    table_copy.wait()
    pltpu.make_async_copy(many, many, freq_recv.at[1]).wait()
    done = 0
    for number in range(4, 11):
        count = CHUNKS[number - 4]
        if count:
            features(done, count)
        done += count
        stage(number)
    half = nets_ref.at[pl.ds(0, 2)]
    pltpu.make_async_copy(half, half, recv_sem.at[COPIES]).wait()
    for sent in (half, nets_ref.at[0], nets_ref.at[0, pl.ds(0, 3)], nets_ref.at[0, 0, pl.ds(0, 3)], nets_ref.at[0, 0, 0, 0]):
        pltpu.make_async_copy(sent, sent, send_sem).wait()
    pltpu.make_async_copy(seven, seven, freq_send.at[0]).wait()
    pltpu.make_async_copy(many, many, freq_send.at[1]).wait()
    keep.wait()
    picks_copy.wait()
    for copy in feature_copies:
        copy.wait()


def tri(kind):
    row, col = iota((LANES, LANES), 0), iota((LANES, LANES), 1)
    same = row // S == col // S
    if kind == "upto":
        keep = row <= col
    elif kind == "after":
        keep = row > col
    else:
        keep = row >= 0
    return (same & keep).astype(F32).astype(BF16)


def render_kernel(
    table_ref, spacing_ref, colour_grad_ref, picks_hbm_ref, feature_hbm_ref, nets_hbm_ref,
    rendered_ref, grad_out_ref, hidden_ref, raw_ref, feature_ref, nets_ref, picks_ref, grad_ref,
    feature_sem, nets_sem, picks_sem,
):
    total = table_ref[0, 383]

    groups = lax.div(total + (GR - 1), GR)

    def net_copy(part):
        rows = pl.ds(part * (REG // PARTS), REG // PARTS)
        return pltpu.make_async_copy(nets_hbm_ref.at[rows], nets_ref.at[rows], nets_sem.at[part])

    def feature_copy(step):
        rows = pl.ds(step * GR, GR)
        return pltpu.make_async_copy(feature_hbm_ref.at[rows], feature_ref.at[rows], feature_sem.at[step])

    net_copy(0).start()
    feature_copy(0).start()
    net_copy(1).start()
    for step in range(1, AHEAD):
        feature_copy(step).start()
    picks_copy = pltpu.make_async_copy(picks_hbm_ref, picks_ref, picks_sem)

    def raw_of(step):
        outs = []
        for j in range(GR):
            b = step * GR + j
            head = nets_ref[table_ref[0, b], HID:NETS, :].astype(F32)
            head = jnp.concatenate([head[0:4], head[4:8]], axis=1)
            head = jnp.concatenate([head, jnp.zeros((4, HID), F32)], axis=0).astype(BF16)
            outs.append(dot(head, hidden_ref[b]))
        for j in range(GR):
            raw_ref[pl.ds((step * GR + j) * 8, 8), :] = outs[j]

    def forward(step, carry):
        @pl.when(step + AHEAD < groups)
        def _():
            feature_copy(step + AHEAD).start()

        feature_copy(step).wait()
        raw_of(jnp.maximum(step - 1, 0))
        for j in range(GR):
            b = step * GR + j
            hid = dot(nets_ref[table_ref[0, b], 0:HID, :], feature_ref[b])
            hidden_ref[b] = jnp.maximum(hid, 0.0).astype(BF16)
        return carry

    def blank(step, carry):
        for j in range(GR):
            raw_ref[pl.ds((step * GR + j) * 8, 8), :] = jnp.zeros((8, LANES), F32)
        return carry

    first = 0
    for part in range(PARTS):
        if part + 2 < PARTS:
            net_copy(part + 2).start()
        elif part + 2 == PARTS:
            picks_copy.start()
        net_copy(part).wait()
        last = groups if part == PARTS - 1 else lax.div(table_ref[0, BOUNDS + part], GR)
        lax.fori_loop(first, last, forward, 0)
        first = last
    raw_of(groups - 1)
    lax.fori_loop(groups, NB // GR, blank, 0)
    for step in range(AHEAD):
        @pl.when(step >= groups)
        def _(step=step):
            feature_copy(step).wait()

    raw = [raw_ref[pl.ds(o, NB, stride=8), :] for o in range(4)]
    spacing = spacing_ref[...]
    picks_copy.wait()
    soft = jnp.maximum(raw[0], 0.0) + jnp.log1p(jnp.exp(-jnp.abs(raw[0])))
    colour = [1.0 / (1.0 + jnp.exp(-raw[c])) for c in (1, 2, 3)]
    gate = 1.0 / (1.0 + jnp.exp(-raw[0]))
    optical = soft * spacing
    running = exact_dot(optical, tri("upto"))
    after = jnp.exp(-running)
    weight = jnp.exp(optical - running) * (1.0 - jnp.exp(-optical))
    chooser = (iota((8, LANES), 1) // S == iota((8, LANES), 0)).astype(F32).astype(BF16)
    last = (iota((8, LANES), 1) == iota((8, LANES), 0) * S + (S - 1)).astype(F32).astype(BF16)

    def seg_rows(value, pattern):
        return [dot(pattern, part, ((1,), (1,))) for part in pieces(value)]

    sums = []
    for c in range(3):
        three = seg_rows(weight * colour[c], chooser)
        sums.append(three[0] + three[1] + three[2])
    three = seg_rows(after, last)
    sums.append(three[0] + three[1] + three[2])
    by_seg = jnp.zeros((16, SEG), F32)
    for q in range(4):
        four = jnp.concatenate([value[q:q + 1] for value in sums], axis=0)
        hi, mid, low = pieces(four)
        rows = jnp.concatenate(
            [hi.astype(F32), mid.astype(F32), low.astype(F32), jnp.zeros((4, NB), F32)], axis=0
        )
        by_seg = by_seg + dot(rows.astype(BF16), picks_ref[q])
    partial = by_seg[0:4] + by_seg[4:8] + by_seg[8:12]
    seg_colour = [partial[0:3, k * RAYS:(k + 1) * RAYS] for k in range(K)]
    seg_trans = [partial[3:4, k * RAYS:(k + 1) * RAYS] for k in range(K)]
    upstream = colour_grad_ref[...]
    before = jnp.ones((1, RAYS), F32)
    befores = []
    rendered = jnp.zeros((3, RAYS), F32)
    for k in range(K):
        befores.append(before)
        rendered = rendered + before * seg_colour[k]
        before = before * seg_trans[k]
    rendered_ref[...] = rendered
    behind = jnp.zeros((3, RAYS), F32)
    grads = [None] * K
    for k in range(K - 1, -1, -1):
        trans = befores[k] * jnp.sum(upstream * behind, axis=0, keepdims=True)
        grads[k] = jnp.concatenate([befores[k] * upstream, trans], axis=0)
        behind = seg_colour[k] + seg_trans[k] * behind
    grad_rows = jnp.concatenate(grads, axis=1)
    hi, mid, low = pieces(grad_rows)
    grad_rows = jnp.concatenate(
        [hi.astype(F32), mid.astype(F32), low.astype(F32), jnp.zeros((4, SEG), F32)], axis=0
    ).astype(BF16)
    spread = [jnp.zeros((NB, LANES), F32) for _ in range(4)]
    for q in range(4):
        got = dot(picks_ref[q], grad_rows, ((1,), (1,))).astype(BF16)
        lane = iota((16, LANES), 1) // S == q
        for o in range(4):
            row = iota((16, LANES), 0)
            expand = (lane & (row % 4 == o) & (row < 12)).astype(F32).astype(BF16)
            spread[o] = spread[o] + dot(got, expand)
    shade = spread[0] * colour[0] + spread[1] * colour[1] + spread[2] * colour[2]
    later = exact_dot(shade * weight, tri("after")) + spread[3] * exact_dot_last(after)
    d_optical = shade * after - later
    raw_grads = [d_optical * spacing * gate]
    for c in range(3):
        raw_grads.append(spread[c] * weight * colour[c] * (1.0 - colour[c]))
    for o in range(4):
        raw_ref[pl.ds(o, NB, stride=8), :] = raw_grads[o]
    for o in range(4, 8):
        raw_ref[pl.ds(o, NB, stride=8), :] = jnp.zeros((NB, LANES), F32)
    grad_ref[...] = jnp.zeros_like(grad_ref)

    def backward(step, carry):
        total_grad, before_region = carry
        parts = []
        for j in range(GB):
            b = step * GB + j
            rg = raw_ref[pl.ds(b * 8, 8), :].astype(BF16)
            parts.append(dot(rg, hidden_ref[b], ((1,), (1,))))
        for j in range(GB):
            region = table_ref[0, step * GB + j]
            total_grad = parts[j] + jnp.where(region == before_region, total_grad, 0.0)
            grad_ref[0, region] = total_grad[0:4, :LANES]
            grad_ref[1, region] = total_grad[0:4, LANES:]
            before_region = region
        return total_grad, before_region

    start = (jnp.zeros((8, HID), F32), jnp.int32(-1))
    lax.fori_loop(0, lax.div(total + (GB - 1), GB), backward, start)
    grad_copy = pltpu.make_async_copy(grad_ref, grad_out_ref, picks_sem)
    grad_copy.start()
    grad_copy.wait()


def exact_dot_last(after):
    row, col = iota((LANES, LANES), 0), iota((LANES, LANES), 1)
    pattern = ((row // S == col // S) & (row % S == S - 1)).astype(F32).astype(BF16)
    return exact_dot(after, pattern)


def params(mib, **kw):
    return pltpu.CompilerParams(vmem_limit_bytes=mib * 1024 * 1024, **kw)


def gather_nets(crossed, points, spacing, freq, hidden, head):
    return pl.pallas_call(
        gather_kernel,
        out_shape=(
            jax.ShapeDtypeStruct((4, 4, 4, 2, NETS, LANES), BF16),
            jax.ShapeDtypeStruct((NB, LANES, LANES), BF16),
            jax.ShapeDtypeStruct((4, NB, SEG), BF16),
            jax.ShapeDtypeStruct((NB, LANES), F32),
            jax.ShapeDtypeStruct((1, 384), jnp.int32),
        ),
        in_specs=[HBM] * 6,
        out_specs=(HBM, HBM, HBM, VM, VM),
        scratch_shapes=[
            pltpu.VMEM((NETS, LANES), BF16),
            pltpu.VMEM((REG, 4, LANES), FREQ_TYPE),
            pltpu.VMEM((NB, LANES, LANES), BF16),
            pltpu.VMEM((4, NB, SEG), BF16),
            pltpu.VMEM((NB * 4, LANES), F32),
            pltpu.SMEM((1, 384), jnp.int32),
            pltpu.VMEM((K, RAYS), jnp.int32),
            pltpu.VMEM((3, RAYS, LANES), F32),
            pltpu.VMEM((RAYS, LANES), F32),
            pltpu.VMEM((3, FREQ), BF16),
            pltpu.VMEM((LANES, HID), BF16),
            pltpu.VMEM((4, HID), BF16),
            pltpu.SemaphoreType.DMA,
            pltpu.SemaphoreType.DMA((COPIES + 1,)),
            pltpu.SemaphoreType.DMA((2,)),
            pltpu.SemaphoreType.DMA((2,)),
            pltpu.SemaphoreType.DMA,
            pltpu.SemaphoreType.DMA((NB // GF,)),
            pltpu.SemaphoreType.DMA((8,)),
        ],
        compiler_params=params(62, collective_id=0, has_side_effects=True),
    )(crossed, points, spacing, freq, hidden, head)


def render_all(table, spacing, colour_grad, picks, feature, nets):
    return pl.pallas_call(
        render_kernel,
        out_shape=(
            jax.ShapeDtypeStruct((3, RAYS), F32),
            jax.ShapeDtypeStruct((2, REG, 4, LANES), F32),
        ),
        in_specs=[SM, VM, VM, HBM, HBM, HBM],
        out_specs=(VM, HBM),
        scratch_shapes=[
            pltpu.VMEM((NB, HID, LANES), BF16),
            pltpu.VMEM((NB * 8, LANES), F32),
            pltpu.VMEM((NB, LANES, LANES), BF16),
            pltpu.VMEM((REG, NETS, LANES), BF16),
            pltpu.VMEM((4, NB, SEG), BF16),
            pltpu.VMEM((2, REG, 4, LANES), F32),
            pltpu.SemaphoreType.DMA((NB // GR,)),
            pltpu.SemaphoreType.DMA((PARTS,)),
            pltpu.SemaphoreType.DMA,
        ],
        compiler_params=params(62),
    )(table, spacing, colour_grad, picks, feature, nets)


def reduce_kernel(
    grad_hbm_ref, out_ref, grad_ref, got_a, sum_a, last_a, got_b, sum_b, last_b, send_sem, recv_sem, load_sem
):
    load = pltpu.make_async_copy(grad_hbm_ref, grad_ref, load_sem)
    load.start()
    me = lax.axis_index("region")
    base, inner, outer = me - lax.rem(me, 8), lax.rem(me, 8), lax.div(me, 8)
    barrier = pltpu.get_barrier_semaphore()
    greet(barrier, me)
    load.wait()
    pl.semaphore_wait(barrier, 22)
    within = lambda step: base + lax.rem(inner + step, 8)
    across = lambda step: lax.rem(outer + step, 16) * 8 + inner

    def send(src, dst, number, peer):
        pltpu.make_async_remote_copy(
            src, dst, send_sem.at[number], recv_sem.at[number],
            device_id=(peer,), device_id_type=MESH_ID,
        ).start()

    def finish(ref, sem):
        pltpu.make_async_copy(ref, ref, sem).wait()

    rest_a, rest_b = got_a.at[pl.ds(1, 7)], got_b.at[pl.ds(1, 15)]
    end_a, end_b = last_a.at[pl.ds(1, 15)], last_b.at[pl.ds(1, 7)]
    for step in range(1, 16):
        send(grad_ref.at[1, lax.rem(outer + step, 16)], got_b.at[step], 0, across(step))
    for step in range(1, 8):
        send(grad_ref.at[0, :, lax.rem(inner + step, 8)], got_a.at[step], 1, within(step))
    finish(rest_b, recv_sem.at[0])
    total = grad_ref[1, outer]
    for step in range(1, 16):
        total = total + got_b[step]
    sum_b[...] = total
    for step in range(1, 8):
        send(sum_b.at[lax.rem(inner + step, 8)], last_b.at[step], 2, within(step))
    finish(rest_a, recv_sem.at[1])
    total = grad_ref[0, :, inner]
    for step in range(1, 8):
        total = total + got_a[step]
    sum_a[...] = total
    for step in range(1, 16):
        send(sum_a.at[lax.rem(outer + step, 16)], last_a.at[step], 3, across(step))
    finish(end_b, recv_sem.at[2])
    total = sum_b[inner]
    for step in range(1, 8):
        total = total + last_b[step]
    out_ref[:, LANES:] = total
    finish(end_a, recv_sem.at[3])
    total = sum_a[outer]
    for step in range(1, 16):
        total = total + last_a[step]
    out_ref[:, :LANES] = total
    finish(rest_b, send_sem.at[0])
    finish(rest_a, send_sem.at[1])
    finish(end_b, send_sem.at[2])
    finish(end_a, send_sem.at[3])


def reduce_heads(grad):
    return pl.pallas_call(
        reduce_kernel,
        out_shape=jax.ShapeDtypeStruct((4, HID), F32),
        in_specs=[HBM],
        out_specs=VM,
        scratch_shapes=[
            pltpu.VMEM((2, 16, 8, 4, LANES), F32),
            pltpu.VMEM((8, 16, 4, LANES), F32),
            pltpu.VMEM((16, 4, LANES), F32),
            pltpu.VMEM((16, 4, LANES), F32),
            pltpu.VMEM((16, 8, 4, LANES), F32),
            pltpu.VMEM((8, 4, LANES), F32),
            pltpu.VMEM((8, 4, LANES), F32),
            pltpu.SemaphoreType.DMA((4,)),
            pltpu.SemaphoreType.DMA((4,)),
            pltpu.SemaphoreType.DMA,
        ],
        compiler_params=params(62, collective_id=1, has_side_effects=True),
    )(grad.reshape(2, 16, 8, 4, LANES))


def on_device(sample_points, sample_spacing, crossed, colour_grad, freq, w_hidden, w_head):
    nets, feature, picks, spacing, table = gather_nets(
        crossed.T, sample_points.transpose(1, 0, 2), sample_spacing, freq[0], w_hidden[0], w_head[0]
    )
    nets = nets.reshape(REG, NETS, LANES)
    rendered, grad = render_all(table, spacing, colour_grad, picks, feature, nets)
    return rendered, reduce_heads(grad)[None]


def solution(mesh):
    return jax.shard_map(
        on_device,
        mesh=mesh,
        in_specs=(
            P("region", None, None),
            P("region", None),
            P("region", None),
            P(None, "region"),
            P("region", None, None),
            P("region", None, None),
            P("region", None, None),
        ),
        out_specs=(P(None, "region"), P("region", None, None)),
        check_vma=False,
    )
```

```python
import functools

import jax
import jax.numpy as jnp
import numpy as np
from jax import lax
from jax.experimental import pallas as pl
from jax.experimental.pallas import tpu as pltpu
from jax.sharding import PartitionSpec as P

RAYS = 256
K = 4
S = 32
REG = 128
SEG = RAYS * K
NB = 352
FREQ = 64
HID = 256
LANES = 128
NETS = HID + 8
PART = NETS // 3
COPIES = 96
GF = 32
CHUNKS = (2, 3, 2, 1, 1, 1, 1)
GR = 44
GB = 44
AHEAD = 2
PARTS = 8
BOUNDS = 376

F32 = jnp.float32
BF16 = jnp.bfloat16
FREQ_TYPE = BF16

SIN_C = (4.44288292, -7.3082457, 3.60635441, -0.84611289, 0.10982699)
COS_C = (1.4142135, -6.97885099, 5.73946117, -1.88356298, 0.31069819)

HBM = pl.BlockSpec(memory_space=pltpu.HBM)
VM = pl.BlockSpec(memory_space=pltpu.VMEM)
SM = pl.BlockSpec(memory_space=pltpu.SMEM)
ANY = pl.BlockSpec(memory_space=pl.ANY)


def iota(shape, dim):
    return lax.broadcasted_iota(jnp.int32, shape, dim)


def dot(a, b, dims=((1,), (0,))):
    return lax.dot_general(a, b, (dims, ((), ())), preferred_element_type=F32)


def pieces(x):
    hi = x.astype(BF16)
    rest = x - hi.astype(F32)
    mid = rest.astype(BF16)
    low = (rest - mid.astype(F32)).astype(BF16)
    return hi, mid, low


def exact_dot(x, pattern):
    hi, mid, low = pieces(x)
    return dot(hi, pattern) + dot(mid, pattern) + dot(low, pattern)


def poly(z, coef):
    out = coef[-1] * z + coef[-2]
    for value in coef[-3::-1]:
        out = out * z + value
    return out


def sort_places(crossed):
    owner = jnp.concatenate([crossed[k:k + 1] for k in range(K)], axis=1)
    onehot = (iota((REG, SEG), 0) == owner).astype(F32)
    onehot16 = onehot.astype(BF16)
    earlier = (iota((SEG, SEG), 0) < iota((SEG, SEG), 1)).astype(F32).astype(BF16)
    rank = dot(onehot16, earlier)
    counts = jnp.sum(onehot, axis=1, keepdims=True)
    blocks = jnp.floor((counts + 3.0) * 0.25)
    lower = (iota((REG, REG), 1) <= iota((REG, REG), 0)).astype(F32).astype(BF16)
    ends = dot(lower, jnp.broadcast_to(blocks, (REG, LANES)).astype(BF16))[:, :1]
    starts = ends - blocks
    rank_row = jnp.sum(onehot * rank, axis=0, keepdims=True)
    start_row = jnp.sum(onehot * starts, axis=0, keepdims=True)
    step = jnp.floor(rank_row * 0.25)
    place = (rank_row - 4.0 * step) * NB + start_row + step
    block_at = iota((REG, 384), 1).astype(F32)
    owner_of = jnp.sum((block_at >= ends).astype(F32), axis=0, keepdims=True)
    owner_of = jnp.minimum(owner_of, REG - 1.0)
    total = jnp.sum(blocks, axis=0, keepdims=True)
    table = jnp.where(iota((1, 384), 1) == 383, total, owner_of)
    for part in range(PARTS - 1):
        last = (part + 1) * (REG // PARTS)
        table = jnp.where(iota((1, 384), 1) == BOUNDS + part, ends[last - 1:last], table)
    return place.astype(jnp.int32), table.astype(jnp.int32)


def sort_sources(sources):
    lane_group = iota((RAYS, LANES), 1) // S
    rows = []
    for k in range(K):
        row = jnp.zeros((RAYS, LANES), F32)
        for c in range(4):
            moved = sources[c]
            if c != k:
                moved = pltpu.roll(moved, ((c - k) % 4) * S, 1)
            row = jnp.where(lane_group == c, moved, row)
        rows.append(row)
    packed = jnp.concatenate(rows, axis=0)
    return jnp.concatenate(pieces(packed), axis=1)


def sort_coords(picks_ref, source, coords_ref):
    block_group = iota((NB, LANES), 1) // S
    coords = [jnp.zeros((NB, LANES), F32) for _ in range(4)]
    for q in range(4):
        three = dot(picks_ref[q], source)
        got = three[:, :128] + three[:, 128:256] + three[:, 256:]
        for c in range(4):
            moved = got
            if c != q:
                moved = pltpu.roll(got, ((q - c) % 4) * S, 1)
            coords[c] = jnp.where(block_group == q, moved, coords[c])
    for c in range(4):
        value = coords[c] * np.float32(0.5 / np.pi) if c < 3 else coords[c]
        coords_ref[pl.ds(c, NB, stride=4), :] = value
    return coords[3]


def bounded(region):
    return jnp.maximum(jnp.minimum(region, REG - 1), 0)


def features_of(freq, coords):
    freq = freq.astype(F32)
    f12 = jnp.concatenate([freq, freq, freq], axis=0).astype(BF16)
    hi = coords.astype(BF16).astype(F32)
    mid = (coords - hi).astype(BF16).astype(F32)
    low = coords - hi - mid
    x12 = jnp.concatenate([hi, mid, low], axis=0).astype(BF16)
    return dot(f12, x12, ((0,), (0,)))[:FREQ]


def encode(turns):
    r = turns - jnp.round(turns)
    z = r * r
    s = r * poly(z, SIN_C)
    c = poly(z, COS_C)
    return jnp.concatenate([s * c, 1.0 - s * s], axis=0).astype(BF16)


ORDERS = ((0, 1, 2), (1, 2, 0), (2, 0, 1))
STRIDES = (32, 8, 2)
MESH_ID = pl.DeviceIdType.MESH


def greet(barrier, me):
    base, inner, outer = me - lax.rem(me, 8), lax.rem(me, 8), lax.div(me, 8)

    def within(step, carry):
        peer = base + lax.rem(inner + step, 8)
        pl.semaphore_signal(barrier, inc=1, device_id=(peer,), device_id_type=MESH_ID)
        return carry

    def across(step, carry):
        peer = lax.rem(outer + step, 16) * 8 + inner
        pl.semaphore_signal(barrier, inc=1, device_id=(peer,), device_id_type=MESH_ID)
        return carry

    lax.fori_loop(1, 8, within, 0)
    lax.fori_loop(1, 16, across, 0)


def gather_kernel(
    crossed_hbm, points_hbm, spacing_hbm, freq_hbm, hidden_hbm, head_hbm,
    nets_ref, feature_out_ref, picks_out_ref, spacing_out_ref, table_out_ref,
    payload_ref, freq_ref, feature_ref, picks_ref, coords_ref, table_ref,
    crossed_ref, points_ref, spacing_ref, freq_in_ref, hidden_in_ref, head_in_ref,
    send_sem, recv_sem, freq_send, freq_recv, local_sem, feature_sem, input_sem,
):
    me = lax.axis_index("region")
    core = lax.rem(me, 2)
    sibling = me + 1 - 2 * core
    pos = [lax.rem(lax.div(me, stride), 4) for stride in STRIDES]
    base, inner, outer = me - lax.rem(me, 8), lax.rem(me, 8), lax.div(me, 8)
    barrier = pltpu.get_barrier_semaphore()
    inputs = [
        pltpu.make_async_copy(src, dst, input_sem.at[number])
        for number, (src, dst) in enumerate((
            (hidden_hbm, hidden_in_ref), (freq_hbm, freq_in_ref), (head_hbm, head_in_ref),
            (crossed_hbm, crossed_ref), (points_hbm, points_ref), (spacing_hbm, spacing_ref),
        ))
    ]
    for copy in inputs:
        copy.start()
    greet(barrier, me)
    for copy in inputs[:3]:
        copy.wait()
    payload_ref[0:HID, :] = hidden_in_ref[...].astype(F32).T.astype(BF16)
    head = head_in_ref[...].astype(F32)
    head = jnp.concatenate([head[:, :LANES], head[:, LANES:]], axis=0)
    payload_ref[HID:NETS, :] = head.astype(BF16)
    freq_in = jnp.concatenate([freq_in_ref[...].astype(F32), jnp.zeros((3, FREQ), F32)], axis=1)
    freq_in = jnp.concatenate([freq_in, jnp.zeros((1, LANES), F32)], axis=0)
    freq_ref[me] = freq_in.astype(FREQ_TYPE)
    pl.semaphore_wait(barrier, 22)

    def freq_within(step, carry):
        peer = base + lax.rem(inner + step, 8)
        pltpu.make_async_remote_copy(
            freq_ref.at[me], freq_ref.at[me], freq_send.at[0], freq_recv.at[0],
            device_id=(peer,), device_id_type=MESH_ID,
        ).start()
        return carry

    def freq_across(step, carry):
        peer = lax.rem(outer + step, 16) * 8 + inner
        rows = pl.ds(base, 8)
        pltpu.make_async_remote_copy(
            freq_ref.at[rows], freq_ref.at[rows], freq_send.at[1], freq_recv.at[1],
            device_id=(peer,), device_id_type=MESH_ID,
        ).start()
        return carry

    lax.fori_loop(1, 8, freq_within, 0)

    counter = [0]

    def new_id():
        counter[0] += 1
        return counter[0] - 1

    def device(axis, delta):
        return me + (lax.rem(pos[axis] + delta, 4) - pos[axis]) * STRIDES[axis]

    def view(where, parity, rows):
        return nets_ref.at[where[0], where[1], where[2], parity, rows, :]

    def start(src, dst, peer, number):
        pltpu.make_async_remote_copy(
            src, dst, send_sem, recv_sem.at[number],
            device_id=(peer,), device_id_type=MESH_ID,
        ).start()

    def arrive(dst, number):
        pltpu.make_async_remote_copy(
            dst, dst, send_sem, recv_sem.at[number],
            device_id=(sibling,), device_id_type=MESH_ID,
        ).wait_recv()

    home = {0: pos[0], 1: pos[1], 2: pos[2]}

    def to_sibling(where, rows):
        start(view(where, core, rows), view(where, core, rows), sibling, COPIES)

    whole = pl.ds(0, 4)

    def make_stream(t):
        a, b, c = ORDERS[t]
        rows = pl.ds(PART * t, PART)
        base = dict(home)
        left = {axis: lax.rem(pos[axis] + 3, 4) for axis in range(3)}
        right = {axis: lax.rem(pos[axis] + 1, 4) for axis in range(3)}
        opposite = {axis: lax.rem(pos[axis] + 2, 4) for axis in range(3)}

        def spec(**kw):
            out = dict(base)
            for key, value in kw.items():
                out[{"a": a, "b": b, "c": c}[key]] = value
            return out

        ids = {}

        def send(name, axis, delta, where, src=None):
            number = new_id()
            source = view(where, core, rows) if src is None else src
            start(source, view(where, core, rows), device(axis, delta), number)
            ids[name] = number

        def wait(name, where):
            arrive(view(where, core, rows), ids[name])

        def stage0():
            mine = payload_ref.at[rows, :]
            send("A+", a, 1, spec(), src=mine)
            send("A-", a, 3, spec(), src=mine)
            send("A=", a, 2, spec(), src=mine)
            send("B+o", b, 1, spec(), src=mine)
            send("B-o", b, 3, spec(), src=mine)
            send("C+o", c, 1, spec(), src=mine)
            send("C-o", c, 3, spec(), src=mine)

        def spread(where, tag):
            send("B+" + tag, b, 1, where)
            send("B-" + tag, b, 3, where)
            send("C+" + tag, c, 1, where)
            send("C-" + tag, c, 3, where)

        def stage1():
            low, high, across = spec(a=left[a]), spec(a=right[a]), spec(a=opposite[a])
            wait("A+", low)
            spread(low, "l")
            wait("A-", high)
            spread(high, "r")
            wait("A=", across)
            spread(across, "d")

        def stage2():
            for chip in (left[a], right[a], opposite[a]):
                to_sibling(spec(a=chip), rows)

        def line_arrivals(prefix, **kw):
            wait(prefix + "o", spec(**kw))
            wait(prefix + "l", spec(a=left[a], **kw))
            wait(prefix + "r", spec(a=right[a], **kw))
            wait(prefix + "d", spec(a=opposite[a], **kw))

        def stage3():
            line_arrivals("B+", b=left[b])
            low = spec(a=whole, b=left[b])
            send("BH+", b, 1, spec(a=pl.ds(0, 2), b=left[b]))
            send("C+L", c, 1, low)
            send("C-L", c, 3, low)
            line_arrivals("B-", b=right[b])
            high = spec(a=whole, b=right[b])
            send("BH-", b, 3, spec(a=pl.ds(2, 2), b=right[b]))
            send("C+R", c, 1, high)
            send("C-R", c, 3, high)
            to_sibling(low, rows)
            to_sibling(high, rows)

        def stage4():
            line_arrivals("C+", c=left[c])
            send("CH+o", c, 1, spec(a=whole, c=left[c]))
            wait("BH+", spec(a=pl.ds(0, 2), b=opposite[b]))
            wait("BH-", spec(a=pl.ds(2, 2), b=opposite[b]))
            across = spec(a=whole, b=opposite[b])
            send("C+D", c, 1, across)
            send("C-D", c, 3, across)
            to_sibling(across, rows)

        def stage5():
            line_arrivals("C-", c=right[c])
            wait("C-R", spec(a=whole, b=right[b], c=right[c]))
            send("CH-R", c, 3, spec(a=whole, b=right[b], c=right[c]))
            wait("C+L", spec(a=whole, b=left[b], c=left[c]))
            send("CH+L", c, 1, spec(a=whole, b=left[b], c=left[c]))
            to_sibling(spec(a=whole, c=left[c]), rows)
            to_sibling(spec(a=whole, c=right[c]), rows)
            to_sibling(spec(a=whole, b=left[b], c=left[c]), rows)
            to_sibling(spec(a=whole, b=right[b], c=right[c]), rows)

        def stage6():
            wait("C-D", spec(a=whole, b=opposite[b], c=right[c]))
            send("CH-D", c, 3, spec(a=whole, b=opposite[b], c=right[c]))
            wait("C+R", spec(a=whole, b=right[b], c=left[c]))
            wait("C+D", spec(a=whole, b=opposite[b], c=left[c]))
            wait("C-L", spec(a=whole, b=left[b], c=right[c]))
            to_sibling(spec(a=whole, b=right[b], c=left[c]), rows)
            to_sibling(spec(a=whole, b=opposite[b], c=left[c]), rows)
            to_sibling(spec(a=whole, b=left[b], c=right[c]), rows)
            to_sibling(spec(a=whole, b=opposite[b], c=right[c]), rows)

        def stage7(name, line):
            where = spec(a=whole, b=line, c=opposite[c])
            wait(name, where)
            to_sibling(where, rows)

        lines = (("CH+o", pos[b]), ("CH+L", left[b]), ("CH-R", right[b]), ("CH-D", opposite[b]))
        last = [functools.partial(stage7, name, line) for name, line in lines]
        return [stage0, stage1, stage2, stage3, stage4, stage5, stage6] + last

    streams = [make_stream(t) for t in range(3)]

    def stage(number):
        for stream in streams:
            stream[number]()

    stage(0)
    start(payload_ref, view(home, core, pl.ds(0, NETS)), sibling, COPIES)
    keep = pltpu.make_async_copy(payload_ref, view(home, core, pl.ds(0, NETS)), local_sem)
    keep.start()

    def features(first, count):
        def body(step, carry):
            turns = []
            for j in range(GF):
                b = step * GF + j
                turns.append(features_of(freq_ref[bounded(table_ref[0, b])], coords_ref[pl.ds(b * 4, 4), :]))
            for j in range(GF):
                feature_ref[step * GF + j] = encode(turns[j])
            return carry

        lax.fori_loop(first, first + count, body, 0)
        part = pl.ds(first * GF, count * GF)
        copy = pltpu.make_async_copy(
            feature_ref.at[part], feature_out_ref.at[part], feature_sem.at[first]
        )
        copy.start()
        feature_copies.append(copy)

    feature_copies = []
    inputs[3].wait()
    place, table = sort_places(crossed_ref[...])
    table_out_ref[...] = table
    table_copy = pltpu.make_async_copy(table_out_ref, table_ref, input_sem.at[6])
    table_copy.start()
    seven, many = freq_ref.at[pl.ds(0, 7)], freq_ref.at[pl.ds(0, 120)]
    pltpu.make_async_copy(seven, seven, freq_recv.at[0]).wait()
    lax.fori_loop(1, 16, freq_across, 0)
    stage(1)
    for q in range(4):
        picks_ref[q] = (iota((NB, SEG), 0) + q * NB == place).astype(F32).astype(BF16)
    picks_copy = pltpu.make_async_copy(picks_ref, picks_out_ref, input_sem.at[7])
    picks_copy.start()
    stage(2)
    inputs[4].wait()
    inputs[5].wait()
    source = sort_sources([points_ref[0], points_ref[1], points_ref[2], spacing_ref[...]])
    stage(3)
    spacing_out_ref[...] = sort_coords(picks_ref, source, coords_ref)
    table_copy.wait()
    pltpu.make_async_copy(many, many, freq_recv.at[1]).wait()
    done = 0
    for number in range(4, 11):
        count = CHUNKS[number - 4]
        if count:
            features(done, count)
        done += count
        stage(number)
    half = nets_ref.at[pl.ds(0, 2)]
    pltpu.make_async_copy(half, half, recv_sem.at[COPIES]).wait()
    for sent in (half, nets_ref.at[0], nets_ref.at[0, pl.ds(0, 3)], nets_ref.at[0, 0, pl.ds(0, 3)], nets_ref.at[0, 0, 0, 0]):
        pltpu.make_async_copy(sent, sent, send_sem).wait()
    pltpu.make_async_copy(seven, seven, freq_send.at[0]).wait()
    pltpu.make_async_copy(many, many, freq_send.at[1]).wait()
    keep.wait()
    picks_copy.wait()
    for copy in feature_copies:
        copy.wait()


def tri(kind):
    row, col = iota((LANES, LANES), 0), iota((LANES, LANES), 1)
    same = row // S == col // S
    if kind == "upto":
        keep = row <= col
    elif kind == "after":
        keep = row > col
    else:
        keep = row >= 0
    return (same & keep).astype(F32).astype(BF16)


def render_kernel(
    table_ref, spacing_ref, colour_grad_ref, picks_hbm_ref, feature_hbm_ref, nets_hbm_ref,
    rendered_ref, grad_out_ref, hidden_ref, raw_ref, feature_ref, nets_ref, picks_ref, grad_ref,
    feature_sem, nets_sem, picks_sem,
):
    total = table_ref[0, 383]

    groups = lax.div(total + (GR - 1), GR)

    def net_copy(part):
        rows = pl.ds(part * (REG // PARTS), REG // PARTS)
        return pltpu.make_async_copy(nets_hbm_ref.at[rows], nets_ref.at[rows], nets_sem.at[part])

    def feature_copy(step):
        rows = pl.ds(step * GR, GR)
        return pltpu.make_async_copy(feature_hbm_ref.at[rows], feature_ref.at[rows], feature_sem.at[step])

    net_copy(0).start()
    feature_copy(0).start()
    net_copy(1).start()
    for step in range(1, AHEAD):
        feature_copy(step).start()
    picks_copy = pltpu.make_async_copy(picks_hbm_ref, picks_ref, picks_sem)

    def raw_of(step):
        outs = []
        for j in range(GR):
            b = step * GR + j
            head = nets_ref[table_ref[0, b], HID:NETS, :].astype(F32)
            head = jnp.concatenate([head[0:4], head[4:8]], axis=1)
            head = jnp.concatenate([head, jnp.zeros((4, HID), F32)], axis=0).astype(BF16)
            outs.append(dot(head, hidden_ref[b]))
        for j in range(GR):
            raw_ref[pl.ds((step * GR + j) * 8, 8), :] = outs[j]

    def forward(step, carry):
        @pl.when(step + AHEAD < groups)
        def _():
            feature_copy(step + AHEAD).start()

        feature_copy(step).wait()
        raw_of(jnp.maximum(step - 1, 0))
        for j in range(GR):
            b = step * GR + j
            hid = dot(nets_ref[table_ref[0, b], 0:HID, :], feature_ref[b])
            hidden_ref[b] = jnp.maximum(hid, 0.0).astype(BF16)
        return carry

    def blank(step, carry):
        for j in range(GR):
            raw_ref[pl.ds((step * GR + j) * 8, 8), :] = jnp.zeros((8, LANES), F32)
        return carry

    first = 0
    for part in range(PARTS):
        if part + 2 < PARTS:
            net_copy(part + 2).start()
        elif part + 2 == PARTS:
            picks_copy.start()
        net_copy(part).wait()
        last = groups if part == PARTS - 1 else lax.div(table_ref[0, BOUNDS + part], GR)
        lax.fori_loop(first, last, forward, 0)
        first = last
    raw_of(groups - 1)
    lax.fori_loop(groups, NB // GR, blank, 0)
    for step in range(AHEAD):
        @pl.when(step >= groups)
        def _(step=step):
            feature_copy(step).wait()

    raw = [raw_ref[pl.ds(o, NB, stride=8), :] for o in range(4)]
    spacing = spacing_ref[...]
    picks_copy.wait()
    soft = jnp.maximum(raw[0], 0.0) + jnp.log1p(jnp.exp(-jnp.abs(raw[0])))
    colour = [1.0 / (1.0 + jnp.exp(-raw[c])) for c in (1, 2, 3)]
    gate = 1.0 / (1.0 + jnp.exp(-raw[0]))
    optical = soft * spacing
    sums = exact_dot(optical, jnp.concatenate([tri("upto"), tri("all")], axis=1))
    running, passed = sums[:, :LANES], jnp.exp(-sums[:, LANES:])
    after = jnp.exp(-running)
    weight = jnp.exp(optical - running) * (1.0 - jnp.exp(-optical))
    chooser = (iota((8, LANES), 1) // S == iota((8, LANES), 0)).astype(F32).astype(BF16)
    last = (iota((8, LANES), 1) == iota((8, LANES), 0) * S + (S - 1)).astype(F32).astype(BF16)

    def seg_rows(value, pattern):
        return [dot(pattern, part, ((1,), (1,))) for part in pieces(value)]

    sums = []
    for c in range(3):
        three = seg_rows(weight * colour[c], chooser)
        sums.append(three[0] + three[1] + three[2])
    three = seg_rows(after, last)
    sums.append(three[0] + three[1] + three[2])
    by_seg = jnp.zeros((16, SEG), F32)
    for q in range(4):
        four = jnp.concatenate([value[q:q + 1] for value in sums], axis=0)
        hi, mid, low = pieces(four)
        rows = jnp.concatenate(
            [hi.astype(F32), mid.astype(F32), low.astype(F32), jnp.zeros((4, NB), F32)], axis=0
        )
        by_seg = by_seg + dot(rows.astype(BF16), picks_ref[q])
    partial = by_seg[0:4] + by_seg[4:8] + by_seg[8:12]
    seg_colour = [partial[0:3, k * RAYS:(k + 1) * RAYS] for k in range(K)]
    seg_trans = [partial[3:4, k * RAYS:(k + 1) * RAYS] for k in range(K)]
    upstream = colour_grad_ref[...]
    before = jnp.ones((1, RAYS), F32)
    befores = []
    rendered = jnp.zeros((3, RAYS), F32)
    for k in range(K):
        befores.append(before)
        rendered = rendered + before * seg_colour[k]
        before = before * seg_trans[k]
    rendered_ref[...] = rendered
    behind = jnp.zeros((3, RAYS), F32)
    grads = [None] * K
    for k in range(K - 1, -1, -1):
        trans = befores[k] * jnp.sum(upstream * behind, axis=0, keepdims=True)
        grads[k] = jnp.concatenate([befores[k] * upstream, trans], axis=0)
        behind = seg_colour[k] + seg_trans[k] * behind
    grad_rows = jnp.concatenate(grads, axis=1)
    hi, mid, low = pieces(grad_rows)
    grad_rows = jnp.concatenate(
        [hi.astype(F32), mid.astype(F32), low.astype(F32), jnp.zeros((4, SEG), F32)], axis=0
    )
    got = jnp.zeros((NB, 64), F32)
    for q in range(4):
        parts = [grad_rows if q == other else jnp.zeros((16, SEG), F32) for other in range(4)]
        rows = jnp.concatenate(parts, axis=0).astype(BF16)
        got = got + dot(picks_ref[q], rows, ((1,), (1,)))
    row, col = iota((64, 4 * LANES), 0), iota((64, 4 * LANES), 1)
    expand = (row // 16 == col % LANES // S) & (row % 4 == col // LANES) & (row % 16 < 12)
    wide = dot(got.astype(BF16), expand.astype(F32).astype(BF16))
    spread = [wide[:, o * LANES:(o + 1) * LANES] for o in range(4)]
    shade = spread[0] * colour[0] + spread[1] * colour[1] + spread[2] * colour[2]
    later = exact_dot(shade * weight, tri("after")) + spread[3] * passed
    d_optical = shade * after - later
    raw_grads = [d_optical * spacing * gate]
    for c in range(3):
        raw_grads.append(spread[c] * weight * colour[c] * (1.0 - colour[c]))
    for o in range(4):
        raw_ref[pl.ds(o, NB, stride=8), :] = raw_grads[o]
    for o in range(4, 8):
        raw_ref[pl.ds(o, NB, stride=8), :] = jnp.zeros((NB, LANES), F32)
    grad_ref[...] = jnp.zeros_like(grad_ref)

    def backward(step, carry):
        total_grad, before_region = carry
        parts = []
        for j in range(GB):
            b = step * GB + j
            rg = raw_ref[pl.ds(b * 8, 8), :].astype(BF16)
            parts.append(dot(rg, hidden_ref[b], ((1,), (1,))))
        for j in range(GB):
            region = table_ref[0, step * GB + j]
            total_grad = parts[j] + jnp.where(region == before_region, total_grad, 0.0)
            grad_ref[0, region] = total_grad[0:4, :LANES]
            grad_ref[1, region] = total_grad[0:4, LANES:]
            before_region = region
        return total_grad, before_region

    start = (jnp.zeros((8, HID), F32), jnp.int32(-1))
    lax.fori_loop(0, lax.div(total + (GB - 1), GB), backward, start)
    grad_copy = pltpu.make_async_copy(grad_ref, grad_out_ref, picks_sem)
    grad_copy.start()
    grad_copy.wait()


def params(mib, **kw):
    return pltpu.CompilerParams(vmem_limit_bytes=mib * 1024 * 1024, **kw)


def gather_nets(crossed, points, spacing, freq, hidden, head):
    return pl.pallas_call(
        gather_kernel,
        out_shape=(
            jax.ShapeDtypeStruct((4, 4, 4, 2, NETS, LANES), BF16),
            jax.ShapeDtypeStruct((NB, LANES, LANES), BF16),
            jax.ShapeDtypeStruct((4, NB, SEG), BF16),
            jax.ShapeDtypeStruct((NB, LANES), F32),
            jax.ShapeDtypeStruct((1, 384), jnp.int32),
        ),
        in_specs=[HBM] * 6,
        out_specs=(HBM, HBM, HBM, VM, VM),
        scratch_shapes=[
            pltpu.VMEM((NETS, LANES), BF16),
            pltpu.VMEM((REG, 4, LANES), FREQ_TYPE),
            pltpu.VMEM((NB, LANES, LANES), BF16),
            pltpu.VMEM((4, NB, SEG), BF16),
            pltpu.VMEM((NB * 4, LANES), F32),
            pltpu.SMEM((1, 384), jnp.int32),
            pltpu.VMEM((K, RAYS), jnp.int32),
            pltpu.VMEM((3, RAYS, LANES), F32),
            pltpu.VMEM((RAYS, LANES), F32),
            pltpu.VMEM((3, FREQ), BF16),
            pltpu.VMEM((LANES, HID), BF16),
            pltpu.VMEM((4, HID), BF16),
            pltpu.SemaphoreType.DMA,
            pltpu.SemaphoreType.DMA((COPIES + 1,)),
            pltpu.SemaphoreType.DMA((2,)),
            pltpu.SemaphoreType.DMA((2,)),
            pltpu.SemaphoreType.DMA,
            pltpu.SemaphoreType.DMA((NB // GF,)),
            pltpu.SemaphoreType.DMA((8,)),
        ],
        compiler_params=params(62, collective_id=0, has_side_effects=True),
    )(crossed, points, spacing, freq, hidden, head)


def render_all(table, spacing, colour_grad, picks, feature, nets):
    return pl.pallas_call(
        render_kernel,
        out_shape=(
            jax.ShapeDtypeStruct((3, RAYS), F32),
            jax.ShapeDtypeStruct((2, REG, 4, LANES), F32),
        ),
        in_specs=[SM, VM, VM, HBM, HBM, HBM],
        out_specs=(VM, HBM),
        scratch_shapes=[
            pltpu.VMEM((NB, HID, LANES), BF16),
            pltpu.VMEM((NB * 8, LANES), F32),
            pltpu.VMEM((NB, LANES, LANES), BF16),
            pltpu.VMEM((REG, NETS, LANES), BF16),
            pltpu.VMEM((4, NB, SEG), BF16),
            pltpu.VMEM((2, REG, 4, LANES), F32),
            pltpu.SemaphoreType.DMA((NB // GR,)),
            pltpu.SemaphoreType.DMA((PARTS,)),
            pltpu.SemaphoreType.DMA,
        ],
        compiler_params=params(62),
    )(table, spacing, colour_grad, picks, feature, nets)


def reduce_kernel(
    grad_hbm_ref, low_ref, high_ref, grad_ref, got_a, sum_a, last_a, got_b, sum_b, last_b, send_sem, recv_sem, load_sem
):
    load = pltpu.make_async_copy(grad_hbm_ref, grad_ref, load_sem)
    load.start()
    me = lax.axis_index("region")
    base, inner, outer = me - lax.rem(me, 8), lax.rem(me, 8), lax.div(me, 8)
    barrier = pltpu.get_barrier_semaphore()
    greet(barrier, me)
    load.wait()
    pl.semaphore_wait(barrier, 22)
    within = lambda step: base + lax.rem(inner + step, 8)
    across = lambda step: lax.rem(outer + step, 16) * 8 + inner

    def send(src, dst, number, peer):
        pltpu.make_async_remote_copy(
            src, dst, send_sem.at[number], recv_sem.at[number],
            device_id=(peer,), device_id_type=MESH_ID,
        ).start()

    def finish(ref, sem):
        pltpu.make_async_copy(ref, ref, sem).wait()

    rest_a, rest_b = got_a.at[pl.ds(1, 7)], got_b.at[pl.ds(1, 15)]
    end_a, end_b = last_a.at[pl.ds(1, 15)], last_b.at[pl.ds(1, 7)]
    for step in range(1, 16):
        send(grad_ref.at[1, lax.rem(outer + step, 16)], got_b.at[step], 0, across(step))
    for step in range(1, 8):
        send(grad_ref.at[0, :, lax.rem(inner + step, 8)], got_a.at[step], 1, within(step))
    finish(rest_b, recv_sem.at[0])
    total = grad_ref[1, outer]
    for step in range(1, 16):
        total = total + got_b[step]
    sum_b[...] = total
    for step in range(1, 8):
        send(sum_b.at[lax.rem(inner + step, 8)], last_b.at[step], 2, within(step))
    finish(rest_a, recv_sem.at[1])
    total = grad_ref[0, :, inner]
    for step in range(1, 8):
        total = total + got_a[step]
    sum_a[...] = total
    for step in range(1, 16):
        send(sum_a.at[lax.rem(outer + step, 16)], last_a.at[step], 3, across(step))
    finish(end_b, recv_sem.at[2])
    total = sum_b[inner]
    for step in range(1, 8):
        total = total + last_b[step]
    high_ref[...] = total
    finish(end_a, recv_sem.at[3])
    total = sum_a[outer]
    for step in range(1, 16):
        total = total + last_a[step]
    low_ref[...] = total
    finish(rest_b, send_sem.at[0])
    finish(rest_a, send_sem.at[1])
    finish(end_b, send_sem.at[2])
    finish(end_a, send_sem.at[3])


def reduce_heads(grad):
    return pl.pallas_call(
        reduce_kernel,
        out_shape=(jax.ShapeDtypeStruct((4, LANES), F32), jax.ShapeDtypeStruct((4, LANES), F32)),
        in_specs=[HBM],
        out_specs=(VM, VM),
        scratch_shapes=[
            pltpu.VMEM((2, 16, 8, 4, LANES), F32),
            pltpu.VMEM((8, 16, 4, LANES), F32),
            pltpu.VMEM((16, 4, LANES), F32),
            pltpu.VMEM((16, 4, LANES), F32),
            pltpu.VMEM((16, 8, 4, LANES), F32),
            pltpu.VMEM((8, 4, LANES), F32),
            pltpu.VMEM((8, 4, LANES), F32),
            pltpu.SemaphoreType.DMA((4,)),
            pltpu.SemaphoreType.DMA((4,)),
            pltpu.SemaphoreType.DMA,
        ],
        compiler_params=params(62, collective_id=1, has_side_effects=True),
    )(grad.reshape(2, 16, 8, 4, LANES))


def on_device(sample_points, sample_spacing, crossed, colour_grad, freq, w_hidden, w_head):
    nets, feature, picks, spacing, table = gather_nets(
        crossed.T, sample_points.transpose(1, 0, 2), sample_spacing, freq[0], w_hidden[0], w_head[0]
    )
    nets = nets.reshape(REG, NETS, LANES)
    rendered, grad = render_all(table, spacing, colour_grad, picks, feature, nets)
    low, high = reduce_heads(grad)
    return rendered, jnp.concatenate([low, high], axis=1)[None]


def solution(mesh):
    return jax.shard_map(
        on_device,
        mesh=mesh,
        in_specs=(
            P("region", None, None),
            P("region", None),
            P("region", None),
            P(None, "region"),
            P("region", None, None),
            P("region", None, None),
            P("region", None, None),
        ),
        out_specs=(P(None, "region"), P("region", None, None)),
        check_vma=False,
    )
```

```python
import functools

import jax
import jax.numpy as jnp
import numpy as np
from jax import lax
from jax.experimental import pallas as pl
from jax.experimental.pallas import tpu as pltpu
from jax.sharding import PartitionSpec as P

RAYS = 256
K = 4
S = 32
REG = 128
SEG = RAYS * K
NB = 352
FREQ = 64
HID = 256
LANES = 128
NETS = HID + 8
PART = NETS // 3
COPIES = 96
GF = 32
CHUNKS = (3, 4, 2, 1, 1, 0, 0)
GR = 44
GB = 44
AHEAD = 2
PARTS = 8
BOUNDS = 376

F32 = jnp.float32
BF16 = jnp.bfloat16
FREQ_TYPE = BF16

SIN_C = (4.44288292, -7.3082457, 3.60635441, -0.84611289, 0.10982699)
COS_C = (1.4142135, -6.97885099, 5.73946117, -1.88356298, 0.31069819)

HBM = pl.BlockSpec(memory_space=pltpu.HBM)
VM = pl.BlockSpec(memory_space=pltpu.VMEM)
SM = pl.BlockSpec(memory_space=pltpu.SMEM)
ANY = pl.BlockSpec(memory_space=pl.ANY)


def iota(shape, dim):
    return lax.broadcasted_iota(jnp.int32, shape, dim)


def dot(a, b, dims=((1,), (0,))):
    return lax.dot_general(a, b, (dims, ((), ())), preferred_element_type=F32)


def pieces(x):
    hi = x.astype(BF16)
    rest = x - hi.astype(F32)
    mid = rest.astype(BF16)
    low = (rest - mid.astype(F32)).astype(BF16)
    return hi, mid, low


def exact_dot(x, pattern):
    hi, mid, low = pieces(x)
    return dot(hi, pattern) + dot(mid, pattern) + dot(low, pattern)


def poly(z, coef):
    out = coef[-1] * z + coef[-2]
    for value in coef[-3::-1]:
        out = out * z + value
    return out


def sort_places(crossed):
    owner = jnp.concatenate([crossed[k:k + 1] for k in range(K)], axis=1)
    onehot = (iota((REG, SEG), 0) == owner).astype(F32)
    onehot16 = onehot.astype(BF16)
    earlier = (iota((SEG, SEG), 0) < iota((SEG, SEG), 1)).astype(F32).astype(BF16)
    rank = dot(onehot16, earlier)
    counts = jnp.sum(onehot, axis=1, keepdims=True)
    blocks = jnp.floor((counts + 3.0) * 0.25)
    lower = (iota((REG, REG), 1) <= iota((REG, REG), 0)).astype(F32).astype(BF16)
    ends = dot(lower, jnp.broadcast_to(blocks, (REG, LANES)).astype(BF16))[:, :1]
    starts = ends - blocks
    rank_row = jnp.sum(onehot * rank, axis=0, keepdims=True)
    start_row = jnp.sum(onehot * starts, axis=0, keepdims=True)
    step = jnp.floor(rank_row * 0.25)
    place = (rank_row - 4.0 * step) * NB + start_row + step
    block_at = iota((REG, 384), 1).astype(F32)
    owner_of = jnp.sum((block_at >= ends).astype(F32), axis=0, keepdims=True)
    owner_of = jnp.minimum(owner_of, REG - 1.0)
    total = jnp.sum(blocks, axis=0, keepdims=True)
    table = jnp.where(iota((1, 384), 1) == 383, total, owner_of)
    for part in range(PARTS - 1):
        last = (part + 1) * (REG // PARTS)
        table = jnp.where(iota((1, 384), 1) == BOUNDS + part, ends[last - 1:last], table)
    return place.astype(jnp.int32), table.astype(jnp.int32)


def sort_sources(sources):
    lane_group = iota((RAYS, LANES), 1) // S
    rows = []
    for k in range(K):
        row = jnp.zeros((RAYS, LANES), F32)
        for c in range(4):
            moved = sources[c]
            if c != k:
                moved = pltpu.roll(moved, ((c - k) % 4) * S, 1)
            row = jnp.where(lane_group == c, moved, row)
        rows.append(row)
    packed = jnp.concatenate(rows, axis=0)
    return jnp.concatenate(pieces(packed), axis=1)


def sort_coords(picks_ref, source, coords_ref):
    block_group = iota((NB, LANES), 1) // S
    coords = [jnp.zeros((NB, LANES), F32) for _ in range(4)]
    for q in range(4):
        three = dot(picks_ref[q], source)
        got = three[:, :128] + three[:, 128:256] + three[:, 256:]
        for c in range(4):
            moved = got
            if c != q:
                moved = pltpu.roll(got, ((q - c) % 4) * S, 1)
            coords[c] = jnp.where(block_group == q, moved, coords[c])
    for c in range(4):
        value = coords[c] * np.float32(0.5 / np.pi) if c < 3 else coords[c]
        coords_ref[pl.ds(c, NB, stride=4), :] = value
    return coords[3]


def bounded(region):
    return jnp.maximum(jnp.minimum(region, REG - 1), 0)


def features_of(freq, coords):
    freq = freq.astype(F32)
    f12 = jnp.concatenate([freq, freq, freq], axis=0).astype(BF16)
    hi = coords.astype(BF16).astype(F32)
    mid = (coords - hi).astype(BF16).astype(F32)
    low = coords - hi - mid
    x12 = jnp.concatenate([hi, mid, low], axis=0).astype(BF16)
    return dot(f12, x12, ((0,), (0,)))[:FREQ]


def encode(turns):
    r = turns - jnp.round(turns)
    z = r * r
    s = r * poly(z, SIN_C)
    c = poly(z, COS_C)
    return jnp.concatenate([s * c, 1.0 - s * s], axis=0).astype(BF16)


ORDERS = ((0, 1, 2), (1, 2, 0), (2, 0, 1))
STRIDES = (32, 8, 2)
MESH_ID = pl.DeviceIdType.MESH


def greet(barrier, me):
    base, inner, outer = me - lax.rem(me, 8), lax.rem(me, 8), lax.div(me, 8)

    def within(step, carry):
        peer = base + lax.rem(inner + step, 8)
        pl.semaphore_signal(barrier, inc=1, device_id=(peer,), device_id_type=MESH_ID)
        return carry

    def across(step, carry):
        peer = lax.rem(outer + step, 16) * 8 + inner
        pl.semaphore_signal(barrier, inc=1, device_id=(peer,), device_id_type=MESH_ID)
        return carry

    lax.fori_loop(1, 8, within, 0)
    lax.fori_loop(1, 16, across, 0)


def gather_kernel(
    crossed_hbm, points_hbm, spacing_hbm, freq_hbm, hidden_hbm, head_hbm,
    nets_ref, feature_out_ref, picks_out_ref, spacing_out_ref, table_out_ref,
    payload_ref, freq_ref, feature_ref, picks_ref, coords_ref, table_ref,
    crossed_ref, points_ref, spacing_ref, freq_in_ref, hidden_in_ref, head_in_ref,
    send_sem, recv_sem, freq_send, freq_recv, local_sem, feature_sem, input_sem,
):
    me = lax.axis_index("region")
    core = lax.rem(me, 2)
    sibling = me + 1 - 2 * core
    pos = [lax.rem(lax.div(me, stride), 4) for stride in STRIDES]
    base, inner, outer = me - lax.rem(me, 8), lax.rem(me, 8), lax.div(me, 8)
    barrier = pltpu.get_barrier_semaphore()
    inputs = [
        pltpu.make_async_copy(src, dst, input_sem.at[number])
        for number, (src, dst) in enumerate((
            (hidden_hbm, hidden_in_ref), (freq_hbm, freq_in_ref), (head_hbm, head_in_ref),
            (crossed_hbm, crossed_ref), (points_hbm, points_ref), (spacing_hbm, spacing_ref),
        ))
    ]
    for copy in inputs:
        copy.start()
    greet(barrier, me)
    for copy in inputs[:3]:
        copy.wait()
    payload_ref[0:HID, :] = hidden_in_ref[...].astype(F32).T.astype(BF16)
    head = head_in_ref[...].astype(F32)
    head = jnp.concatenate([head[:, :LANES], head[:, LANES:]], axis=0)
    payload_ref[HID:NETS, :] = head.astype(BF16)
    freq_in = jnp.concatenate([freq_in_ref[...].astype(F32), jnp.zeros((3, FREQ), F32)], axis=1)
    freq_in = jnp.concatenate([freq_in, jnp.zeros((1, LANES), F32)], axis=0)
    freq_ref[me] = freq_in.astype(FREQ_TYPE)
    pl.semaphore_wait(barrier, 22)

    def freq_within(step, carry):
        peer = base + lax.rem(inner + step, 8)
        pltpu.make_async_remote_copy(
            freq_ref.at[me], freq_ref.at[me], freq_send.at[0], freq_recv.at[0],
            device_id=(peer,), device_id_type=MESH_ID,
        ).start()
        return carry

    def freq_across(step, carry):
        peer = lax.rem(outer + step, 16) * 8 + inner
        rows = pl.ds(base, 8)
        pltpu.make_async_remote_copy(
            freq_ref.at[rows], freq_ref.at[rows], freq_send.at[1], freq_recv.at[1],
            device_id=(peer,), device_id_type=MESH_ID,
        ).start()
        return carry

    counter = [0]

    def new_id():
        counter[0] += 1
        return counter[0] - 1

    def device(axis, delta):
        return me + (lax.rem(pos[axis] + delta, 4) - pos[axis]) * STRIDES[axis]

    def view(where, parity, rows):
        return nets_ref.at[where[0], where[1], where[2], parity, rows, :]

    def start(src, dst, peer, number):
        pltpu.make_async_remote_copy(
            src, dst, send_sem, recv_sem.at[number],
            device_id=(peer,), device_id_type=MESH_ID,
        ).start()

    def arrive(dst, number):
        pltpu.make_async_remote_copy(
            dst, dst, send_sem, recv_sem.at[number],
            device_id=(sibling,), device_id_type=MESH_ID,
        ).wait_recv()

    home = {0: pos[0], 1: pos[1], 2: pos[2]}

    def to_sibling(where, rows):
        start(view(where, core, rows), view(where, core, rows), sibling, COPIES)

    whole = pl.ds(0, 4)

    def make_stream(t):
        a, b, c = ORDERS[t]
        rows = pl.ds(PART * t, PART)
        base = dict(home)
        left = {axis: lax.rem(pos[axis] + 3, 4) for axis in range(3)}
        right = {axis: lax.rem(pos[axis] + 1, 4) for axis in range(3)}
        opposite = {axis: lax.rem(pos[axis] + 2, 4) for axis in range(3)}

        def spec(**kw):
            out = dict(base)
            for key, value in kw.items():
                out[{"a": a, "b": b, "c": c}[key]] = value
            return out

        ids = {}

        def send(name, axis, delta, where, src=None):
            number = new_id()
            source = view(where, core, rows) if src is None else src
            start(source, view(where, core, rows), device(axis, delta), number)
            ids[name] = number

        def wait(name, where):
            arrive(view(where, core, rows), ids[name])

        def stage0():
            mine = payload_ref.at[rows, :]
            send("A+", a, 1, spec(), src=mine)
            send("A-", a, 3, spec(), src=mine)
            send("A=", a, 2, spec(), src=mine)
            send("B+o", b, 1, spec(), src=mine)
            send("B-o", b, 3, spec(), src=mine)
            send("C+o", c, 1, spec(), src=mine)
            send("C-o", c, 3, spec(), src=mine)

        def spread(where, tag):
            send("B+" + tag, b, 1, where)
            send("B-" + tag, b, 3, where)
            send("C+" + tag, c, 1, where)
            send("C-" + tag, c, 3, where)

        def stage1():
            low, high, across = spec(a=left[a]), spec(a=right[a]), spec(a=opposite[a])
            wait("A+", low)
            spread(low, "l")
            wait("A-", high)
            spread(high, "r")
            wait("A=", across)
            spread(across, "d")

        def stage2():
            for chip in (left[a], right[a], opposite[a]):
                to_sibling(spec(a=chip), rows)

        def line_arrivals(prefix, **kw):
            wait(prefix + "o", spec(**kw))
            wait(prefix + "l", spec(a=left[a], **kw))
            wait(prefix + "r", spec(a=right[a], **kw))
            wait(prefix + "d", spec(a=opposite[a], **kw))

        def stage3():
            line_arrivals("B+", b=left[b])
            low = spec(a=whole, b=left[b])
            send("BH+", b, 1, spec(a=pl.ds(0, 2), b=left[b]))
            send("C+L", c, 1, low)
            send("C-L", c, 3, low)
            line_arrivals("B-", b=right[b])
            high = spec(a=whole, b=right[b])
            send("BH-", b, 3, spec(a=pl.ds(2, 2), b=right[b]))
            send("C+R", c, 1, high)
            send("C-R", c, 3, high)
            to_sibling(low, rows)
            to_sibling(high, rows)

        def stage4():
            line_arrivals("C+", c=left[c])
            send("CH+o", c, 1, spec(a=whole, c=left[c]))
            wait("BH+", spec(a=pl.ds(0, 2), b=opposite[b]))
            wait("BH-", spec(a=pl.ds(2, 2), b=opposite[b]))
            across = spec(a=whole, b=opposite[b])
            send("C+D", c, 1, across)
            send("C-D", c, 3, across)
            to_sibling(across, rows)

        def stage5():
            line_arrivals("C-", c=right[c])
            wait("C-R", spec(a=whole, b=right[b], c=right[c]))
            send("CH-R", c, 3, spec(a=whole, b=right[b], c=right[c]))
            wait("C+L", spec(a=whole, b=left[b], c=left[c]))
            send("CH+L", c, 1, spec(a=whole, b=left[b], c=left[c]))
            to_sibling(spec(a=whole, c=left[c]), rows)
            to_sibling(spec(a=whole, c=right[c]), rows)
            to_sibling(spec(a=whole, b=left[b], c=left[c]), rows)
            to_sibling(spec(a=whole, b=right[b], c=right[c]), rows)

        def stage6():
            wait("C-D", spec(a=whole, b=opposite[b], c=right[c]))
            send("CH-D", c, 3, spec(a=whole, b=opposite[b], c=right[c]))
            wait("C+R", spec(a=whole, b=right[b], c=left[c]))
            wait("C+D", spec(a=whole, b=opposite[b], c=left[c]))
            wait("C-L", spec(a=whole, b=left[b], c=right[c]))
            to_sibling(spec(a=whole, b=right[b], c=left[c]), rows)
            to_sibling(spec(a=whole, b=opposite[b], c=left[c]), rows)
            to_sibling(spec(a=whole, b=left[b], c=right[c]), rows)
            to_sibling(spec(a=whole, b=opposite[b], c=right[c]), rows)

        def stage7(name, line):
            where = spec(a=whole, b=line, c=opposite[c])
            wait(name, where)
            to_sibling(where, rows)

        lines = (("CH+o", pos[b]), ("CH+L", left[b]), ("CH-R", right[b]), ("CH-D", opposite[b]))
        last = [functools.partial(stage7, name, line) for name, line in lines]
        return [stage0, stage1, stage2, stage3, stage4, stage5, stage6] + last

    streams = [make_stream(t) for t in range(3)]

    def stage(number):
        for stream in streams:
            stream[number]()

    stage(0)
    lax.fori_loop(1, 8, freq_within, 0)
    start(payload_ref, view(home, core, pl.ds(0, NETS)), sibling, COPIES)
    keep = pltpu.make_async_copy(payload_ref, view(home, core, pl.ds(0, NETS)), local_sem)
    keep.start()

    def features(first, count):
        def body(step, carry):
            turns = []
            for j in range(GF):
                b = step * GF + j
                turns.append(features_of(freq_ref[bounded(table_ref[0, b])], coords_ref[pl.ds(b * 4, 4), :]))
            for j in range(GF):
                feature_ref[step * GF + j] = encode(turns[j])
            return carry

        lax.fori_loop(first, first + count, body, 0)
        part = pl.ds(first * GF, count * GF)
        copy = pltpu.make_async_copy(
            feature_ref.at[part], feature_out_ref.at[part], feature_sem.at[first]
        )
        copy.start()
        feature_copies.append(copy)

    feature_copies = []
    inputs[3].wait()
    place, table = sort_places(crossed_ref[...])
    table_out_ref[...] = table
    table_copy = pltpu.make_async_copy(table_out_ref, table_ref, input_sem.at[6])
    table_copy.start()
    seven, many = freq_ref.at[pl.ds(0, 7)], freq_ref.at[pl.ds(0, 120)]
    stage(1)
    pltpu.make_async_copy(seven, seven, freq_recv.at[0]).wait()
    lax.fori_loop(1, 16, freq_across, 0)
    for q in range(4):
        picks_ref[q] = (iota((NB, SEG), 0) + q * NB == place).astype(F32).astype(BF16)
    picks_copy = pltpu.make_async_copy(picks_ref, picks_out_ref, input_sem.at[7])
    picks_copy.start()
    stage(2)
    inputs[4].wait()
    inputs[5].wait()
    source = sort_sources([points_ref[0], points_ref[1], points_ref[2], spacing_ref[...]])
    stage(3)
    spacing_out_ref[...] = sort_coords(picks_ref, source, coords_ref)
    table_copy.wait()
    pltpu.make_async_copy(many, many, freq_recv.at[1]).wait()
    done = 0
    for number in range(4, 11):
        count = CHUNKS[number - 4]
        if count:
            features(done, count)
        done += count
        stage(number)
    half = nets_ref.at[pl.ds(0, 2)]
    pltpu.make_async_copy(half, half, recv_sem.at[COPIES]).wait()
    for sent in (half, nets_ref.at[0], nets_ref.at[0, pl.ds(0, 3)], nets_ref.at[0, 0, pl.ds(0, 3)], nets_ref.at[0, 0, 0, 0]):
        pltpu.make_async_copy(sent, sent, send_sem).wait()
    pltpu.make_async_copy(seven, seven, freq_send.at[0]).wait()
    pltpu.make_async_copy(many, many, freq_send.at[1]).wait()
    keep.wait()
    picks_copy.wait()
    for copy in feature_copies:
        copy.wait()


def tri(kind):
    row, col = iota((LANES, LANES), 0), iota((LANES, LANES), 1)
    same = row // S == col // S
    if kind == "upto":
        keep = row <= col
    elif kind == "after":
        keep = row > col
    else:
        keep = row >= 0
    return (same & keep).astype(F32).astype(BF16)


def render_kernel(
    table_ref, spacing_ref, colour_grad_ref, picks_hbm_ref, feature_hbm_ref, nets_hbm_ref,
    rendered_ref, grad_out_ref, hidden_ref, raw_ref, feature_ref, nets_ref, picks_ref, grad_ref,
    feature_sem, nets_sem, picks_sem,
):
    total = table_ref[0, 383]

    groups = lax.div(total + (GR - 1), GR)

    def net_copy(part):
        rows = pl.ds(part * (REG // PARTS), REG // PARTS)
        return pltpu.make_async_copy(nets_hbm_ref.at[rows], nets_ref.at[rows], nets_sem.at[part])

    def feature_copy(step):
        rows = pl.ds(step * GR, GR)
        return pltpu.make_async_copy(feature_hbm_ref.at[rows], feature_ref.at[rows], feature_sem.at[step])

    net_copy(0).start()
    feature_copy(0).start()
    net_copy(1).start()
    for step in range(1, AHEAD):
        feature_copy(step).start()
    picks_copy = pltpu.make_async_copy(picks_hbm_ref, picks_ref, picks_sem)

    def raw_of(step):
        outs = []
        for j in range(GR):
            b = step * GR + j
            head = nets_ref[table_ref[0, b], HID:NETS, :].astype(F32)
            head = jnp.concatenate([head[0:4], head[4:8]], axis=1)
            head = jnp.concatenate([head, jnp.zeros((4, HID), F32)], axis=0).astype(BF16)
            outs.append(dot(head, hidden_ref[b]))
        for j in range(GR):
            raw_ref[pl.ds((step * GR + j) * 8, 8), :] = outs[j]

    def forward(step, carry):
        @pl.when(step + AHEAD < groups)
        def _():
            feature_copy(step + AHEAD).start()

        feature_copy(step).wait()
        raw_of(jnp.maximum(step - 1, 0))
        for j in range(GR):
            b = step * GR + j
            hid = dot(nets_ref[table_ref[0, b], 0:HID, :], feature_ref[b])
            hidden_ref[b] = jnp.maximum(hid, 0.0).astype(BF16)
        return carry

    def blank(step, carry):
        for j in range(GR):
            raw_ref[pl.ds((step * GR + j) * 8, 8), :] = jnp.zeros((8, LANES), F32)
        return carry

    first = 0
    for part in range(PARTS):
        if part + 2 < PARTS:
            net_copy(part + 2).start()
        elif part + 2 == PARTS:
            picks_copy.start()
        net_copy(part).wait()
        last = groups if part == PARTS - 1 else lax.div(table_ref[0, BOUNDS + part], GR)
        lax.fori_loop(first, last, forward, 0)
        first = last
    raw_of(groups - 1)
    lax.fori_loop(groups, NB // GR, blank, 0)
    for step in range(AHEAD):
        @pl.when(step >= groups)
        def _(step=step):
            feature_copy(step).wait()

    raw = [raw_ref[pl.ds(o, NB, stride=8), :] for o in range(4)]
    spacing = spacing_ref[...]
    picks_copy.wait()
    soft = jnp.maximum(raw[0], 0.0) + jnp.log1p(jnp.exp(-jnp.abs(raw[0])))
    colour = [1.0 / (1.0 + jnp.exp(-raw[c])) for c in (1, 2, 3)]
    gate = 1.0 / (1.0 + jnp.exp(-raw[0]))
    optical = soft * spacing
    sums = exact_dot(optical, jnp.concatenate([tri("upto"), tri("all")], axis=1))
    running, passed = sums[:, :LANES], jnp.exp(-sums[:, LANES:])
    after = jnp.exp(-running)
    weight = jnp.exp(optical - running) * (1.0 - jnp.exp(-optical))
    chooser = (iota((8, LANES), 1) // S == iota((8, LANES), 0)).astype(F32).astype(BF16)
    last = (iota((8, LANES), 1) == iota((8, LANES), 0) * S + (S - 1)).astype(F32).astype(BF16)

    def seg_rows(value, pattern):
        return [dot(pattern, part, ((1,), (1,))) for part in pieces(value)]

    sums = []
    for c in range(3):
        three = seg_rows(weight * colour[c], chooser)
        sums.append(three[0] + three[1] + three[2])
    three = seg_rows(after, last)
    sums.append(three[0] + three[1] + three[2])
    by_seg = jnp.zeros((16, SEG), F32)
    for q in range(4):
        four = jnp.concatenate([value[q:q + 1] for value in sums], axis=0)
        hi, mid, low = pieces(four)
        rows = jnp.concatenate(
            [hi.astype(F32), mid.astype(F32), low.astype(F32), jnp.zeros((4, NB), F32)], axis=0
        )
        by_seg = by_seg + dot(rows.astype(BF16), picks_ref[q])
    partial = by_seg[0:4] + by_seg[4:8] + by_seg[8:12]
    seg_colour = [partial[0:3, k * RAYS:(k + 1) * RAYS] for k in range(K)]
    seg_trans = [partial[3:4, k * RAYS:(k + 1) * RAYS] for k in range(K)]
    upstream = colour_grad_ref[...]
    before = jnp.ones((1, RAYS), F32)
    befores = []
    rendered = jnp.zeros((3, RAYS), F32)
    for k in range(K):
        befores.append(before)
        rendered = rendered + before * seg_colour[k]
        before = before * seg_trans[k]
    rendered_ref[...] = rendered
    behind = jnp.zeros((3, RAYS), F32)
    grads = [None] * K
    for k in range(K - 1, -1, -1):
        trans = befores[k] * jnp.sum(upstream * behind, axis=0, keepdims=True)
        grads[k] = jnp.concatenate([befores[k] * upstream, trans], axis=0)
        behind = seg_colour[k] + seg_trans[k] * behind
    grad_rows = jnp.concatenate(grads, axis=1)
    hi, mid, low = pieces(grad_rows)
    grad_rows = jnp.concatenate(
        [hi.astype(F32), mid.astype(F32), low.astype(F32), jnp.zeros((4, SEG), F32)], axis=0
    )
    got = jnp.zeros((NB, 64), F32)
    for q in range(4):
        parts = [grad_rows if q == other else jnp.zeros((16, SEG), F32) for other in range(4)]
        rows = jnp.concatenate(parts, axis=0).astype(BF16)
        got = got + dot(picks_ref[q], rows, ((1,), (1,)))
    row, col = iota((64, 4 * LANES), 0), iota((64, 4 * LANES), 1)
    expand = (row // 16 == col % LANES // S) & (row % 4 == col // LANES) & (row % 16 < 12)
    wide = dot(got.astype(BF16), expand.astype(F32).astype(BF16))
    spread = [wide[:, o * LANES:(o + 1) * LANES] for o in range(4)]
    shade = spread[0] * colour[0] + spread[1] * colour[1] + spread[2] * colour[2]
    later = exact_dot(shade * weight, tri("after")) + spread[3] * passed
    d_optical = shade * after - later
    raw_grads = [d_optical * spacing * gate]
    for c in range(3):
        raw_grads.append(spread[c] * weight * colour[c] * (1.0 - colour[c]))
    for o in range(4):
        raw_ref[pl.ds(o, NB, stride=8), :] = raw_grads[o]
    for o in range(4, 8):
        raw_ref[pl.ds(o, NB, stride=8), :] = jnp.zeros((NB, LANES), F32)
    grad_ref[...] = jnp.zeros_like(grad_ref)

    def backward(step, carry):
        total_grad, before_region = carry
        parts = []
        for j in range(GB):
            b = step * GB + j
            rg = raw_ref[pl.ds(b * 8, 8), :].astype(BF16)
            parts.append(dot(rg, hidden_ref[b], ((1,), (1,))))
        for j in range(GB):
            region = table_ref[0, step * GB + j]
            total_grad = parts[j] + jnp.where(region == before_region, total_grad, 0.0)
            grad_ref[0, region] = total_grad[0:4, :LANES]
            grad_ref[1, region] = total_grad[0:4, LANES:]
            before_region = region
        return total_grad, before_region

    start = (jnp.zeros((8, HID), F32), jnp.int32(-1))
    lax.fori_loop(0, lax.div(total + (GB - 1), GB), backward, start)
    grad_copy = pltpu.make_async_copy(grad_ref, grad_out_ref, picks_sem)
    grad_copy.start()
    grad_copy.wait()


def params(mib, **kw):
    return pltpu.CompilerParams(vmem_limit_bytes=mib * 1024 * 1024, **kw)


def gather_nets(crossed, points, spacing, freq, hidden, head):
    return pl.pallas_call(
        gather_kernel,
        out_shape=(
            jax.ShapeDtypeStruct((4, 4, 4, 2, NETS, LANES), BF16),
            jax.ShapeDtypeStruct((NB, LANES, LANES), BF16),
            jax.ShapeDtypeStruct((4, NB, SEG), BF16),
            jax.ShapeDtypeStruct((NB, LANES), F32),
            jax.ShapeDtypeStruct((1, 384), jnp.int32),
        ),
        in_specs=[HBM] * 6,
        out_specs=(HBM, HBM, HBM, VM, VM),
        scratch_shapes=[
            pltpu.VMEM((NETS, LANES), BF16),
            pltpu.VMEM((REG, 4, LANES), FREQ_TYPE),
            pltpu.VMEM((NB, LANES, LANES), BF16),
            pltpu.VMEM((4, NB, SEG), BF16),
            pltpu.VMEM((NB * 4, LANES), F32),
            pltpu.SMEM((1, 384), jnp.int32),
            pltpu.VMEM((K, RAYS), jnp.int32),
            pltpu.VMEM((3, RAYS, LANES), F32),
            pltpu.VMEM((RAYS, LANES), F32),
            pltpu.VMEM((3, FREQ), BF16),
            pltpu.VMEM((LANES, HID), BF16),
            pltpu.VMEM((4, HID), BF16),
            pltpu.SemaphoreType.DMA,
            pltpu.SemaphoreType.DMA((COPIES + 1,)),
            pltpu.SemaphoreType.DMA((2,)),
            pltpu.SemaphoreType.DMA((2,)),
            pltpu.SemaphoreType.DMA,
            pltpu.SemaphoreType.DMA((NB // GF,)),
            pltpu.SemaphoreType.DMA((8,)),
        ],
        compiler_params=params(62, collective_id=0, has_side_effects=True),
    )(crossed, points, spacing, freq, hidden, head)


def render_all(table, spacing, colour_grad, picks, feature, nets):
    return pl.pallas_call(
        render_kernel,
        out_shape=(
            jax.ShapeDtypeStruct((3, RAYS), F32),
            jax.ShapeDtypeStruct((2, REG, 4, LANES), F32),
        ),
        in_specs=[SM, VM, VM, HBM, HBM, HBM],
        out_specs=(VM, HBM),
        scratch_shapes=[
            pltpu.VMEM((NB, HID, LANES), BF16),
            pltpu.VMEM((NB * 8, LANES), F32),
            pltpu.VMEM((NB, LANES, LANES), BF16),
            pltpu.VMEM((REG, NETS, LANES), BF16),
            pltpu.VMEM((4, NB, SEG), BF16),
            pltpu.VMEM((2, REG, 4, LANES), F32),
            pltpu.SemaphoreType.DMA((NB // GR,)),
            pltpu.SemaphoreType.DMA((PARTS,)),
            pltpu.SemaphoreType.DMA,
        ],
        compiler_params=params(62),
    )(table, spacing, colour_grad, picks, feature, nets)


def reduce_kernel(
    grad_hbm_ref, low_ref, high_ref, grad_ref, got_a, sum_a, last_a, got_b, sum_b, last_b, send_sem, recv_sem, load_sem
):
    load = pltpu.make_async_copy(grad_hbm_ref, grad_ref, load_sem)
    load.start()
    me = lax.axis_index("region")
    base, inner, outer = me - lax.rem(me, 8), lax.rem(me, 8), lax.div(me, 8)
    barrier = pltpu.get_barrier_semaphore()
    greet(barrier, me)
    load.wait()
    pl.semaphore_wait(barrier, 22)
    within = lambda step: base + lax.rem(inner + step, 8)
    across = lambda step: lax.rem(outer + step, 16) * 8 + inner

    def send(src, dst, number, peer):
        pltpu.make_async_remote_copy(
            src, dst, send_sem.at[number], recv_sem.at[number],
            device_id=(peer,), device_id_type=MESH_ID,
        ).start()

    def finish(ref, sem):
        pltpu.make_async_copy(ref, ref, sem).wait()

    rest_a, rest_b = got_a.at[pl.ds(1, 7)], got_b.at[pl.ds(1, 15)]
    end_a, end_b = last_a.at[pl.ds(1, 15)], last_b.at[pl.ds(1, 7)]
    for step in range(1, 8):
        send(grad_ref.at[0, :, lax.rem(inner + step, 8)], got_a.at[step], 1, within(step))
    for step in range(1, 16):
        send(grad_ref.at[1, lax.rem(outer + step, 16)], got_b.at[step], 0, across(step))
    finish(rest_a, recv_sem.at[1])
    total = grad_ref[0, :, inner]
    for step in range(1, 8):
        total = total + got_a[step]
    sum_a[...] = total
    for step in range(1, 16):
        send(sum_a.at[lax.rem(outer + step, 16)], last_a.at[step], 3, across(step))
    finish(rest_b, recv_sem.at[0])
    total = grad_ref[1, outer]
    for step in range(1, 16):
        total = total + got_b[step]
    sum_b[...] = total
    for step in range(1, 8):
        send(sum_b.at[lax.rem(inner + step, 8)], last_b.at[step], 2, within(step))
    finish(end_b, recv_sem.at[2])
    total = sum_b[inner]
    for step in range(1, 8):
        total = total + last_b[step]
    high_ref[...] = total
    finish(end_a, recv_sem.at[3])
    total = sum_a[outer]
    for step in range(1, 16):
        total = total + last_a[step]
    low_ref[...] = total
    finish(rest_b, send_sem.at[0])
    finish(rest_a, send_sem.at[1])
    finish(end_b, send_sem.at[2])
    finish(end_a, send_sem.at[3])


def reduce_heads(grad):
    return pl.pallas_call(
        reduce_kernel,
        out_shape=(jax.ShapeDtypeStruct((4, LANES), F32), jax.ShapeDtypeStruct((4, LANES), F32)),
        in_specs=[HBM],
        out_specs=(VM, VM),
        scratch_shapes=[
            pltpu.VMEM((2, 16, 8, 4, LANES), F32),
            pltpu.VMEM((8, 16, 4, LANES), F32),
            pltpu.VMEM((16, 4, LANES), F32),
            pltpu.VMEM((16, 4, LANES), F32),
            pltpu.VMEM((16, 8, 4, LANES), F32),
            pltpu.VMEM((8, 4, LANES), F32),
            pltpu.VMEM((8, 4, LANES), F32),
            pltpu.SemaphoreType.DMA((4,)),
            pltpu.SemaphoreType.DMA((4,)),
            pltpu.SemaphoreType.DMA,
        ],
        compiler_params=params(62, collective_id=1, has_side_effects=True),
    )(grad.reshape(2, 16, 8, 4, LANES))


def on_device(sample_points, sample_spacing, crossed, colour_grad, freq, w_hidden, w_head):
    nets, feature, picks, spacing, table = gather_nets(
        crossed.T, sample_points.transpose(1, 0, 2), sample_spacing, freq[0], w_hidden[0], w_head[0]
    )
    nets = nets.reshape(REG, NETS, LANES)
    rendered, grad = render_all(table, spacing, colour_grad, picks, feature, nets)
    low, high = reduce_heads(grad)
    return rendered, jnp.concatenate([low, high], axis=1)[None]


def solution(mesh):
    return jax.shard_map(
        on_device,
        mesh=mesh,
        in_specs=(
            P("region", None, None),
            P("region", None),
            P("region", None),
            P(None, "region"),
            P("region", None, None),
            P("region", None, None),
            P("region", None, None),
        ),
        out_specs=(P(None, "region"), P("region", None, None)),
        check_vma=False,
    )
```
